32 devices in a mesh: wide: 8 (over y, x, core), narrow: 4 (over z).
Axes of the slice: x: 2, y: 2, z: 4, core: 2. Of those that a mesh axis runs over, the one named last changes fastest.
Arguments:
- layer_input: bfloat16 [2, 8, 256, 2048], P(None, 'wide', 'narrow'), may hold values from -6 to 6
- document_lengths: int32 [2, 8, 4], P(None, 'wide'), may hold values from 1 to 128, 256 in all within a row
- attn_gain: bfloat16 [2048], replicated, may hold values from 0.5 to 1.5
- w_query: bfloat16 [2048, 2048], P(None, 'narrow'), may hold values from -0.125 to 0.125
- w_key: bfloat16 [2048, 1024], P(None, 'narrow'), may hold values from -0.125 to 0.125
- w_value: bfloat16 [2048, 1024], P(None, 'narrow'), may hold values from -0.125 to 0.125
- query_gain: bfloat16 [128], replicated, may hold values from 1 to 2.5
- key_gain: bfloat16 [128], replicated, may hold values from 1 to 2.5
- w_out: bfloat16 [2048, 2048], P('narrow'), may hold values from -0.75 to 0.75
- mlp_gain: bfloat16 [2048], replicated, may hold values from 0.5 to 1.5
- w_gate: bfloat16 [2048, 6144], P(None, 'narrow'), may hold values from -0.125 to 0.125
- w_up: bfloat16 [2048, 6144], P(None, 'narrow'), may hold values from -0.125 to 0.125
- w_down: bfloat16 [6144, 2048], P('narrow'), may hold values from -0.078125 to 0.078125
- output_cotangent: bfloat16 [2, 8, 256, 2048], P(None, 'wide', 'narrow'), may hold values from -6 to 6
Outputs:
- layer_out: float32 [2, 8, 256, 2048], P(None, 'wide', 'narrow')
- in_grad: float32 [2, 8, 256, 2048], P(None, 'wide', 'narrow')
- attn_gain_grad: float32 [2048], replicated
- w_query_grad: float32 [2048, 2048], P('wide', 'narrow')
- w_key_grad: float32 [2048, 1024], P('wide', 'narrow')
- w_value_grad: float32 [2048, 1024], P('wide', 'narrow')
- query_gain_grad: float32 [128], replicated
- key_gain_grad: float32 [128], replicated
- w_out_grad: float32 [2048, 2048], P('narrow', 'wide')
- mlp_gain_grad: float32 [2048], replicated
- w_gate_grad: float32 [2048, 6144], P('wide', 'narrow')
- w_up_grad: float32 [2048, 6144], P('wide', 'narrow')
- w_down_grad: float32 [6144, 2048], P('narrow', 'wide')
The draws below stay inside these ranges and needn't reach their ends.
Inputs may be any that keep to these rules, and one draw needn't show every extreme that they name: `document_lengths`: each row's 4 document lengths sum to 256, and in every row the longest is exactly 128.
All inputs are finite; a program needn't handle non-finite values.
Results may differ from the reference program's by a relative error of at most 0.013.
The reference program's roundings to bfloat16 on the way count: a program that leaves them out, or rounds other values in their place, can miss the bound.
Values may be sent and summed in bfloat16 or wider, within the bound.
A program may use at most 192 MiB of HBM per device.

```python
import math
import jax
import jax.numpy as jnp
import numpy as np
from jax import lax

MODEL_WIDTH = 2048
H = 16
KV = 8
HD = 128
FF = 6144
ROW_LENGTH = 256
DOCS_PER_ROW = 4
MICRO_BATCHES = 2
PACKED_ROWS = 8


def spiked(result, own_key, source, target, parts, factor):
    def block_of(dim):
        return (jnp.arange(result.shape[dim]) // (result.shape[dim] // parts)).reshape((-1,) + (1,) * (result.ndim - 1 - dim))

    near = jax.random.permutation(own_key, parts)[block_of(target)]
    far = (block_of(target) + parts // 2) % parts
    return jnp.where((block_of(source) == near) | (block_of(source) == far), factor * result, result)


def levels(own_key, extent, cuts, low, largest):
    def one(axis_at, shards_of):
        heights = jax.random.uniform(jax.random.fold_in(jax.random.fold_in(own_key, 6), axis_at), (shards_of,), jnp.float32, low / len(cuts), largest / len(cuts))
        return jnp.repeat(jnp.exp(heights), extent[axis_at] // shards_of).reshape((-1,) + (1,) * (len(extent) - axis_at - 1))

    factor_of = one(*cuts[0])
    for cut in cuts[1:]:
        factor_of = factor_of * one(*cut)
    return factor_of


def profile(number_of, total, bound, slope):
    portions = [(1 << 20) // math.isqrt(grade ** slope) + 1 for grade in range(2, number_of + 1)]
    spare, counts = total - bound - (number_of - 1), [1] * (number_of - 1)
    while spare > 0:
        free = [i for i in range(number_of - 1) if counts[i] < bound]
        pool, remaining = sum([portions[i] for i in free]), spare
        for i in free:
            extra = min(bound - counts[i], max(1, remaining * portions[i] // pool), spare)
            counts[i] = counts[i] + extra
            spare = spare - extra
    return np.array([bound] + counts)


def uneven(own_key, number_of, total, limit, skew):
    if number_of == 2:
        one = jax.random.randint(own_key, (), max(1, total - limit), min(limit, total - 1) + 1)
        return jnp.stack([one, total - one])
    tallies = jnp.asarray(profile(number_of, total, limit, skew), jnp.int32)
    pairs = (number_of - 1) // 2
    donor, taker = tallies[1:1 + 2 * pairs:2], tallies[2:2 + 2 * pairs:2]
    room = jnp.minimum(donor - 1, limit - taker)
    moved = jax.random.randint(jax.random.fold_in(own_key, 1), (pairs,), 0, 1 << 20) % (room + 1)
    tallies = tallies.at[1:1 + 2 * pairs:2].set(donor - moved).at[2:2 + 2 * pairs:2].set(taker + moved)
    return tallies[jax.random.permutation(jax.random.fold_in(own_key, 2), number_of)]


def bell_draw(stream_key, extent, spread, reach, split=(), dtype=jnp.bfloat16):
    factor_of = levels(stream_key, extent, split, -0.22, 0.18) if split else 1.0
    values = jax.random.normal(stream_key, extent, jnp.float32) * spread * factor_of
    return jnp.minimum(jnp.maximum(values, -reach), reach).astype(dtype)


def noise_with(own_key, extent, scale, limit, pieces, heavy, held_as=jnp.bfloat16):
    entries = scale * jax.random.normal(own_key, extent, jnp.float32)
    if pieces:
        entries = entries * levels(own_key, extent, pieces, -0.22, 0.18)
    return jnp.clip(spiked(entries, jax.random.fold_in(own_key, 3), *heavy), -limit, limit).astype(held_as)


def setup_inputs(seed: int = 0) -> dict:
    streams_of = jax.random.split(jax.random.key(seed), 15)
    layer_input = bell_draw(streams_of[0], (MICRO_BATCHES, PACKED_ROWS, ROW_LENGTH, MODEL_WIDTH), 1.0, 6.0, ((1, 8), (2, 4)))
    document_lengths = jax.vmap(lambda own: uneven(own, DOCS_PER_ROW, ROW_LENGTH, ROW_LENGTH // 2, 2))(jax.random.split(streams_of[1], MICRO_BATCHES * PACKED_ROWS)).reshape((MICRO_BATCHES, PACKED_ROWS, DOCS_PER_ROW)).astype(jnp.int32)
    attn_gain = jnp.clip(1.0 + 0.1 * jax.random.normal(streams_of[2], (MODEL_WIDTH,), jnp.float32), 0.5, 1.5).astype(jnp.bfloat16)
    w_query = bell_draw(streams_of[3], (MODEL_WIDTH, H * HD), MODEL_WIDTH ** -0.5, 0.125, ((1, 4),))
    w_key = bell_draw(streams_of[4], (MODEL_WIDTH, KV * HD), MODEL_WIDTH ** -0.5, 0.125, ((1, 4),))
    w_value = bell_draw(streams_of[5], (MODEL_WIDTH, KV * HD), MODEL_WIDTH ** -0.5, 0.125, ((1, 4),))
    query_gain = jnp.clip(jnp.exp(jax.random.uniform(streams_of[6], (HD,), jnp.float32, math.log(1.0), math.log(2.5))), 1.0, 2.5).astype(jnp.bfloat16)
    key_gain = jnp.clip(jnp.exp(jax.random.uniform(streams_of[7], (HD,), jnp.float32, math.log(1.0), math.log(2.5))), 1.0, 2.5).astype(jnp.bfloat16)
    w_out = bell_draw(streams_of[8], (H * HD, MODEL_WIDTH), (H * HD // 32) ** -0.5, 0.75, ((0, 4),))
    mlp_gain = jnp.clip(1.0 + 0.1 * jax.random.normal(streams_of[9], (MODEL_WIDTH,), jnp.float32), 0.5, 1.5).astype(jnp.bfloat16)
    w_gate = bell_draw(streams_of[10], (MODEL_WIDTH, FF), MODEL_WIDTH ** -0.5, 0.125, ((1, 4),))
    w_up = bell_draw(streams_of[11], (MODEL_WIDTH, FF), MODEL_WIDTH ** -0.5, 0.125, ((1, 4),))
    w_down = bell_draw(streams_of[12], (FF, MODEL_WIDTH), FF ** -0.5, 0.078125, ((0, 4),))
    output_cotangent = noise_with(streams_of[13], (MICRO_BATCHES, PACKED_ROWS, ROW_LENGTH, MODEL_WIDTH), 1.0, 6.0, ((1, 8), (2, 4)), (1, 3, 8, 2.0))
    return dict(layer_input=layer_input, document_lengths=document_lengths, attn_gain=attn_gain, w_query=w_query, w_key=w_key, w_value=w_value, query_gain=query_gain, key_gain=key_gain, w_out=w_out, mlp_gain=mlp_gain, w_gate=w_gate, w_up=w_up, w_down=w_down, output_cotangent=output_cotangent)


norm_eps = 1e-06
masked_score = -1e+30
highest = lax.Precision.HIGHEST

@jax.custom_vjp
def low(v):
    return lax.optimization_barrier(v.astype(jnp.bfloat16)).astype(jnp.float32)

@jax.custom_vjp
def low_back(v):
    return v

def low_keep(v):
    return (low(v), None)

def low_pass(kept, grad):
    return (grad,)

def back_keep(v):
    return (v, None)

def back_low(kept, grad):
    return (low(grad),)
low.defvjp(low_keep, low_pass)
low_back.defvjp(back_keep, back_low)

def matmul(first_op, second_op):
    return jnp.dot(first_op, second_op, precision=highest)

def rms_scale(values):
    return lax.rsqrt(lax.optimization_barrier(jnp.mean(values * values, axis=-1, keepdims=True)) + norm_eps)

def doc_layout(lengths, seq_len):
    doc_ends = jnp.cumsum(lengths).astype(jnp.int32)
    starts = (doc_ends - lengths).astype(jnp.int32)
    places = lax.iota(jnp.int32, seq_len)
    segment = lax.optimization_barrier(jnp.sum((places[:, None] >= doc_ends[None, :]).astype(jnp.int32), axis=1)).astype(jnp.int32)
    member = segment[:, None] == lax.iota(jnp.int32, lengths.shape[0])[None, :]
    doc_first = lax.optimization_barrier(jnp.sum(jnp.where(member, starts[None, :], 0), axis=1)).astype(jnp.int32)
    allowed = (segment[:, None] == segment[None, :]) & (places[None, :] <= places[:, None])
    return ((places - doc_first).astype(jnp.int32), allowed)

def rope_tables(inside, head_dim):
    half_dim = head_dim // 2
    frequency = jnp.power(1000000.0, -2.0 * lax.iota(jnp.float32, half_dim) / head_dim)
    angles = inside.astype(jnp.float32)[:, None] * frequency[None, :]
    return (jnp.cos(angles), jnp.sin(angles))

def rotate(values, cos_table, sine_table):
    half_dim = values.shape[-1] // 2
    first_half = values[..., :half_dim]
    second = values[..., half_dim:]
    cos_wide = cos_table[:, None, :]
    sine_wide = sine_table[:, None, :]
    return jnp.concatenate([first_half * cos_wide - second * sine_wide, second * cos_wide + first_half * sine_wide], axis=-1)

def layer_row(layer_input, lengths, params):
    attn_gain, w_query, w_key, w_value, query_gain, key_gain, w_out, mlp_gain, w_gate, w_up, w_down = params
    seq_len = layer_input.shape[0]
    inside, allowed = doc_layout(lengths, seq_len)
    cos_table, sine_table = rope_tables(inside, HD)
    normed = low(layer_input * rms_scale(layer_input) * attn_gain)
    query_raw = low_back(matmul(normed, w_query)).reshape(seq_len, H, HD)
    key_raw = low_back(matmul(normed, w_key)).reshape(seq_len, KV, HD)
    value_rows = low(low_back(matmul(normed, w_value))).reshape(seq_len, KV, HD)
    query_rot = low(rotate(query_raw * rms_scale(query_raw) * query_gain, cos_table, sine_table))
    key_rot = low(rotate(key_raw * rms_scale(key_raw) * key_gain, cos_table, sine_table))
    grouped = query_rot.reshape(seq_len, KV, H // KV, HD)
    scores = low_back(jnp.einsum('tkgd,ukd->kgtu', grouped, key_rot, precision=highest) * HD ** (-0.5))
    scores = jnp.where(allowed[None, None], scores, masked_score)
    prob_low = low(jax.nn.softmax(scores, axis=-1))
    attn_mix = jnp.einsum('kgtu,ukd->tkgd', prob_low, value_rows, precision=highest).reshape(seq_len, H * HD)
    attn_mix = low(low_back(attn_mix))
    attn_branch = low_back(matmul(attn_mix, w_out))
    middle = layer_input + attn_branch
    normed_two = low(middle * rms_scale(middle) * mlp_gain)
    gate_pre = low_back(matmul(normed_two, w_gate))
    up_proj = low_back(matmul(normed_two, w_up))
    activated = low(jax.nn.silu(gate_pre) * up_proj)
    return middle + low_back(matmul(activated, w_down))

def reference(layer_input, document_lengths, attn_gain, w_query, w_key, w_value, query_gain, key_gain, w_out, mlp_gain, w_gate, w_up, w_down, output_cotangent):
    params = tuple((weight.astype(jnp.float32) for weight in (attn_gain, w_query, w_key, w_value, query_gain, key_gain, w_out, mlp_gain, w_gate, w_up, w_down)))
    input_arrays = layer_input.astype(jnp.float32).reshape(MICRO_BATCHES * PACKED_ROWS, ROW_LENGTH, MODEL_WIDTH)
    lengths = document_lengths.reshape(MICRO_BATCHES * PACKED_ROWS, DOCS_PER_ROW)

    def forward(rows_in, weights):

        def one_row(state_in, row_item):
            return (state_in, jax.checkpoint(layer_row)(row_item[0], row_item[1], weights))
        unused, outputs = lax.scan(one_row, jnp.zeros((), jnp.float32), (rows_in, lengths))
        return outputs
    outputs, pullback = jax.vjp(forward, input_arrays, params)
    in_grad, grads = pullback(output_cotangent.astype(jnp.float32).reshape(input_arrays.shape))
    full_shape = layer_input.shape
    return (outputs.reshape(full_shape), in_grad.reshape(full_shape), grads[0], grads[1], grads[2], grads[3], grads[4], grads[5], grads[6], grads[7], grads[8], grads[9], grads[10])
```

```python
import functools

import jax
import jax.numpy as jnp
from jax import lax
from jax.experimental import pallas as pl
from jax.experimental.pallas import tpu as pltpu
from jax.sharding import PartitionSpec as P

MESH = pl.DeviceIdType.MESH
F32 = jnp.float32
BF16 = jnp.bfloat16
norm_eps = 1e-06
masked_score = -1e30


def both(*conds):
    out = conds[0]
    for cond in conds[1:]:
        out = jnp.logical_and(out, cond)
    return out


def remote(src, dst, ssem, rsem, z):
    return pltpu.make_async_remote_copy(
        src_ref=src, dst_ref=dst, send_sem=ssem, recv_sem=rsem,
        device_id=(lax.axis_index("wide"), z), device_id_type=MESH,
    )


def line_barrier(n):
    z = lax.axis_index("narrow")
    bar = pltpu.get_barrier_semaphore()
    for step in range(1, n):
        pl.semaphore_signal(
            bar, inc=1, device_id=(lax.axis_index("wide"), lax.rem(z + step, n)), device_id_type=MESH
        )
    pl.semaphore_wait(bar, n - 1)


class Gather:
    def __init__(self, n, parts, rows, full, ssem, rsem):
        self.n, self.parts, self.rows, self.full, self.ssem, self.rsem = n, parts, rows, full, ssem, rsem
        self.z = lax.axis_index("narrow")

    def copy(self, way, hop, part, chunk):
        where = self.full.at[chunk, pl.ds(part * self.rows, self.rows)]
        z_to = self.z + 1 if way == 0 else self.z - 1
        return remote(where, where, self.ssem.at[way, hop, part], self.rsem.at[way, hop, part], z_to)

    def chunk(self, way, hop):
        return self.z - hop if way == 0 else self.z + hop

    def has(self, way, hop):
        return self.z >= hop if way == 0 else self.z + hop <= self.n - 1

    def can_send(self, way, hop):
        edge = self.z < self.n - 1 if way == 0 else self.z > 0
        return both(self.has(way, hop), edge)

    def send(self, hop, part):
        for way in (0, 1):
            if hop > 0:
                @pl.when(self.has(way, hop))
                def _():
                    self.copy(way, hop - 1, part, self.chunk(way, hop)).wait_recv()

            if hop < self.n - 1:
                @pl.when(self.can_send(way, hop))
                def _():
                    self.copy(way, hop, part, self.chunk(way, hop)).start()

    def drain(self):
        for way in (0, 1):
            for hop in range(self.n - 1):
                for part in range(self.parts):
                    @pl.when(self.can_send(way, hop))
                    def _():
                        self.copy(way, hop, part, self.chunk(way, hop)).wait_send()


class Scatter:
    def __init__(self, n, parts, partial, sbuf, rbuf, ssem, rsem):
        self.n, self.parts, self.partial = n, parts, partial
        self.sbuf, self.rbuf, self.ssem, self.rsem = sbuf, rbuf, ssem, rsem
        self.z = lax.axis_index("narrow")

    def copy(self, way, j, part):
        z_to = self.z + 1 if way == 0 else self.z - 1
        return remote(
            self.sbuf.at[way, j, part], self.rbuf.at[way, j, part],
            self.ssem.at[way, j, part], self.rsem.at[way, j, part], z_to,
        )

    def dest(self, way, j):
        return self.n - 1 - j if way == 0 else j

    def sends(self, way, j):
        return self.dest(way, j) > self.z if way == 0 else self.dest(way, j) < self.z

    def relays(self, way, j):
        inner = self.z > 0 if way == 0 else self.z < self.n - 1
        return both(self.sends(way, j), inner)

    def starts(self, way, j):
        outer = self.z == 0 if way == 0 else self.z == self.n - 1
        return both(self.sends(way, j), outer)

    def step(self, j, part):
        for way in (0, 1):
            @pl.when(self.starts(way, j))
            def _():
                self.sbuf[way, j, part] = self.partial(self.dest(way, j), part).astype(BF16)
                self.copy(way, j, part).start()

            @pl.when(self.relays(way, j))
            def _():
                self.copy(way, j, part).wait_recv()
                value = self.partial(self.dest(way, j), part) + self.rbuf[way, j, part].astype(F32)
                self.sbuf[way, j, part] = value.astype(BF16)
                self.copy(way, j, part).start()

    def final(self, part, acc_ref):
        acc_ref[part] = self.partial(self.z, part)

        @pl.when(self.z > 0)
        def _():
            j = self.n - 1 - self.z
            self.copy(0, j, part).wait_recv()
            acc_ref[part] += self.rbuf[0, j, part].astype(F32)

        @pl.when(self.z < self.n - 1)
        def _():
            j = self.z
            self.copy(1, j, part).wait_recv()
            acc_ref[part] += self.rbuf[1, j, part].astype(F32)

    def drain(self):
        for way in (0, 1):
            for j in range(self.n - 1):
                for part in range(self.parts):
                    @pl.when(self.sends(way, j))
                    def _():
                        self.copy(way, j, part).wait_send()


def rms_scale(values):
    return lax.rsqrt(jnp.mean(values * values, axis=-1, keepdims=True) + norm_eps)


def rms_back(grad_in, hat, scale_rows):
    return scale_rows * (grad_in - hat * jnp.mean(grad_in * hat, axis=-1, keepdims=True))


def gather_kernel(n, parts, rows, x_ref, gain_ref, cot_ref, normed_ref, cot_full, ssem, rsem, ssem2, rsem2):
    z = lax.axis_index("narrow")
    for part in range(parts):
        x = x_ref[part].astype(F32)
        hat = x * rms_scale(x)
        normed_ref[z, part * rows:(part + 1) * rows] = (hat * gain_ref[...].astype(F32)).astype(BF16)
        cot_full[z, part * rows:(part + 1) * rows] = cot_ref[part]
    line_barrier(n)
    one = Gather(n, parts, rows, normed_ref, ssem, rsem)
    two = Gather(n, parts, rows, cot_full, ssem2, rsem2)
    for g in (one, two):
        for hop in range(n):
            for part in range(parts):
                g.send(hop, part)
    one.drain()
    two.drain()


def mid_kernel(n, parts, rows, partial_ref, x_ref, gain_ref, middle_ref, full_ref, sbuf, rbuf, acc, ss, rs, gs, gr):
    z = lax.axis_index("narrow")
    line_barrier(n)
    scat = Scatter(n, parts, lambda d, p: partial_ref[d, p * rows:(p + 1) * rows], sbuf, rbuf, ss, rs)
    gath = Gather(n, parts, rows, full_ref, gs, gr)
    for part in range(parts + 1):
        for j in range(n - 1):
            if part < parts:
                scat.step(j, part)
            if part > 0:
                gath.send(j + 1, part - 1)
        if part < parts:
            scat.final(part, acc)
            middle = x_ref[part].astype(F32) + acc[part]
            middle_ref[part] = middle
            hat = middle * rms_scale(middle)
            full_ref[z, part * rows:(part + 1) * rows] = (hat * gain_ref[...].astype(F32)).astype(BF16)
            gath.send(0, part)
    scat.drain()
    gath.drain()


def back_kernel(n, parts, rows, partial_ref, mlp_ref, middle_ref, cot_ref, gain_ref, dmid_ref, full_ref, gaing_ref, out_ref,
                sbuf, rbuf, sbuf2, rbuf2, acc, ss, rs, gs, gr, ss2, rs2):
    z = lax.axis_index("narrow")
    line_barrier(n)
    scat = Scatter(n, parts, lambda d, p: partial_ref[d, p * rows:(p + 1) * rows], sbuf, rbuf, ss, rs)
    scat2 = Scatter(n, parts, lambda d, p: mlp_ref[d, p * rows:(p + 1) * rows], sbuf2, rbuf2, ss2, rs2)
    gath = Gather(n, parts, rows, full_ref, gs, gr)
    for part in range(parts + 1):
        for j in range(n - 1):
            if part < parts:
                scat.step(j, part)
            if part > 0:
                gath.send(j + 1, part - 1)
                scat2.step(j, part - 1)
        if part < parts:
            scat.final(part, acc)
            dn2 = acc[part]
            middle = middle_ref[part]
            scale = rms_scale(middle)
            hat = middle * scale
            part_sum = jnp.sum(dn2 * hat, axis=0, keepdims=True)
            if part == 0:
                gaing_ref[...] = part_sum
            else:
                gaing_ref[...] += part_sum
            dmid = cot_ref[part].astype(F32) + rms_back(dn2 * gain_ref[...].astype(F32), hat, scale)
            dmid_ref[part] = dmid
            full_ref[z, part * rows:(part + 1) * rows] = dmid.astype(BF16)
            gath.send(0, part)
    for part in range(parts):
        scat2.final(part, acc)
        out_ref[part] = middle_ref[part] + acc[part]
    scat.drain()
    scat2.drain()
    gath.drain()


def last_kernel(n, parts, rows, partial_ref, dmid_ref, x_ref, gain_ref, out_ref, gaing_ref, sbuf, rbuf, acc, ss, rs):
    line_barrier(n)
    scat = Scatter(n, parts, lambda d, p: partial_ref[d, p * rows:(p + 1) * rows], sbuf, rbuf, ss, rs)
    for part in range(parts):
        for j in range(n - 1):
            scat.step(j, part)
    for part in range(parts):
        scat.final(part, acc)
        dn = acc[part]
        x = x_ref[part].astype(F32)
        scale = rms_scale(x)
        hat = x * scale
        part_sum = jnp.sum(dn * hat, axis=0, keepdims=True)
        if part == 0:
            gaing_ref[...] = part_sum
        else:
            gaing_ref[...] += part_sum
        out_ref[part] = dmid_ref[part] + rms_back(dn * gain_ref[...].astype(F32), hat, scale)
    scat.drain()


def comm_call(body, name, cid, outs, scratch, args):
    vm = pl.BlockSpec(memory_space=pltpu.VMEM)
    return pl.pallas_call(
        body, name=name, out_shape=outs, in_specs=[vm] * len(args), out_specs=[vm] * len(outs), scratch_shapes=scratch,
        compiler_params=pltpu.CompilerParams(collective_id=cid, has_side_effects=True, vmem_limit_bytes=48 << 20),
    )(*args)


def doc_layout(lengths, seq_len):
    doc_ends = jnp.cumsum(lengths)
    starts = doc_ends - lengths
    places = lax.iota(jnp.int32, seq_len)
    segment = jnp.sum((places[:, None] >= doc_ends[None, :]).astype(jnp.int32), axis=1)
    member = segment[:, None] == lax.iota(jnp.int32, lengths.shape[0])[None, :]
    doc_first = jnp.sum(jnp.where(member, starts[None, :], 0), axis=1)
    allowed = (segment[:, None] == segment[None, :]) & (places[None, :] <= places[:, None])
    return (places - doc_first, allowed)


def rope_tables(inside, head_dim):
    half_dim = head_dim // 2
    frequency = jnp.power(1000000.0, -2.0 * lax.iota(jnp.float32, half_dim) / head_dim)
    angles = inside.astype(jnp.float32)[..., None] * frequency
    return (jnp.cos(angles), jnp.sin(angles))


def rotate(values, cos_table, sine_table):
    half = values.shape[-1] // 2
    first, second = values[..., :half], values[..., half:]
    cos, sin = cos_table[..., None, :], sine_table[..., None, :]
    return jnp.concatenate([first * cos - second * sin, second * cos + first * sin], axis=-1)


def dot(a, b, ca, cb):
    return lax.dot_general(a, b, (((ca,), (cb,)), ((), ())), preferred_element_type=F32)


def local(layer_input, document_lengths, attn_gain, w_query, w_key, w_value, query_gain, key_gain, w_out, mlp_gain,
          w_gate, w_up, w_down, output_cotangent):
    n = lax.axis_size("narrow")
    C, _, S, D = layer_input.shape
    T = n * C * S
    R = n * S
    HD = query_gain.shape[0]
    QC, KC = w_query.shape[1], w_key.shape[1]
    QH, KH = QC // HD, KC // HD
    G = QH // KH
    FC = w_gate.shape[1]
    sscale = HD ** (-0.5)
    w_qkv = jnp.concatenate([w_query, w_key, w_value], axis=1)
    w_both = jnp.concatenate([w_gate, w_up], axis=1)
    qg, kg = query_gain.astype(F32), key_gain.astype(F32)
    x_own = layer_input[:, 0]
    cot_own = output_cotangent[:, 0]
    sds = jax.ShapeDtypeStruct
    dma = pltpu.SemaphoreType.DMA
    gsem = lambda: dma((2, n - 1, C))
    rbufs = lambda: pltpu.VMEM((2, n - 1, C, S, D), BF16)

    normed_full, cot_full = comm_call(
        functools.partial(gather_kernel, n, C, S), "gather", 0,
        [sds((n, C * S, D), BF16)] * 2, [gsem(), gsem(), gsem(), gsem()],
        (x_own, attn_gain[None], cot_own))

    def to_rows(v):
        return v.reshape(n, C, S, -1).transpose(1, 0, 2, 3).reshape(C, R, -1)

    def from_rows(v):
        return v.reshape(C, n, S, -1).transpose(1, 0, 2, 3).reshape(T, -1)

    inside, allowed = jax.vmap(lambda l: doc_layout(l, R))(document_lengths[:, 0])
    cos, sin = rope_tables(inside, HD)
    proj = to_rows(dot(normed_full.reshape(T, D), w_qkv, 1, 0))
    q_raw = proj[..., :QC].reshape(C, R, QH, HD)
    k_raw = proj[..., QC:QC + KC].reshape(C, R, KH, HD)
    v_rows = proj[..., QC + KC:].astype(BF16).reshape(C, R, KH, HD)
    q_scale = rms_scale(q_raw)
    q_hat = q_raw * q_scale
    q_rot = rotate(q_hat * qg, cos, sin).astype(BF16)
    k_scale = rms_scale(k_raw)
    k_hat = k_raw * k_scale
    k_rot = rotate(k_hat * kg, cos, sin).astype(BF16)
    grouped = q_rot.reshape(C, R, KH, G, HD)
    es = functools.partial(jnp.einsum, preferred_element_type=F32)
    scores = jnp.where(allowed[:, None, None], es("btkgd,bukd->bkgtu", grouped, k_rot) * sscale, masked_score)
    top = jnp.max(scores, axis=-1, keepdims=True)
    ex = jnp.exp(scores - top)
    prob = ex / jnp.sum(ex, axis=-1, keepdims=True)
    prob_low = prob.astype(BF16)
    mix = from_rows(es("bkgtu,bukd->btkgd", prob_low, v_rows).reshape(C, R, QC).astype(BF16))
    attn_part = dot(mix, w_out, 1, 0).reshape(n, C * S, D)

    middle, n2_full = comm_call(
        functools.partial(mid_kernel, n, C, S), "middle", 1,
        [sds((C, S, D), F32), sds((n, C * S, D), BF16)],
        [rbufs(), rbufs(), pltpu.VMEM((C, S, D), F32), gsem(), gsem(), gsem(), gsem()],
        (attn_part, x_own, mlp_gain[None]))

    n2 = n2_full.reshape(T, D)
    cot = cot_full.reshape(T, D)
    gate_up = dot(n2, w_both, 1, 0)
    gate_pre, up_proj = gate_up[:, :FC], gate_up[:, FC:]
    sig = jax.nn.sigmoid(gate_pre)
    silu = gate_pre * sig
    activated = (silu * up_proj).astype(BF16)
    mlp_part = dot(activated, w_down, 1, 0).reshape(n, C * S, D)
    d_act = dot(cot, w_down, 1, 1)
    d_gate = d_act * up_proj * sig * (1.0 + gate_pre * (1.0 - sig))
    d_both = jnp.concatenate([d_gate, d_act * silu], axis=1).astype(BF16)
    dn2_part = dot(d_both, w_both, 1, 1).reshape(n, C * S, D)
    d_middle, db_full, mlp_gain_part, out_own = comm_call(
        functools.partial(back_kernel, n, C, S), "back", 2,
        [sds((C, S, D), F32), sds((n, C * S, D), BF16), sds((1, D), F32), sds((C, S, D), F32)],
        [rbufs(), rbufs(), rbufs(), rbufs(), pltpu.VMEM((C, S, D), F32)] + [gsem() for _ in range(6)],
        (dn2_part, mlp_part, middle, cot_own, mlp_gain[None]))
    scatter = lambda g, dim: lax.psum_scatter(g.astype(BF16), "wide", scatter_dimension=dim, tiled=True).astype(F32)
    down_share = scatter(dot(activated, cot, 0, 0), 1)
    both_share = scatter(dot(n2, d_both, 0, 0), 0)
    db = db_full.reshape(T, D)
    out_share = scatter(dot(mix, db, 0, 0), 1)
    d_mix = to_rows(dot(db, w_out, 1, 1).astype(BF16)).reshape(C, R, KH, G, HD)
    d_prob = es("btkgd,bukd->bkgtu", d_mix, v_rows)
    d_value = es("bkgtu,btkgd->bukd", prob_low, d_mix)
    d_score = (prob * (d_prob - jnp.sum(prob * d_prob, axis=-1, keepdims=True))).astype(BF16)
    d_query = es("bkgtu,bukd->btkgd", d_score, k_rot).reshape(C, R, QH, HD) * sscale
    d_key = es("bkgtu,btkgd->bukd", d_score, grouped) * sscale
    d_qn = rotate(d_query, cos, -sin)
    d_kn = rotate(d_key, cos, -sin)
    qg_part = jnp.sum(d_qn * q_hat, axis=(0, 1, 2))
    kg_part = jnp.sum(d_kn * k_hat, axis=(0, 1, 2))
    d_qr = rms_back(d_qn * qg, q_hat, q_scale)
    d_kr = rms_back(d_kn * kg, k_hat, k_scale)
    d_proj = from_rows(jnp.concatenate(
        [d_qr.reshape(C, R, QC), d_kr.reshape(C, R, KC), d_value.reshape(C, R, KC)], axis=-1).astype(BF16))
    dn_part = dot(d_proj, w_qkv, 1, 1).reshape(n, C * S, D)
    qkv_share = scatter(dot(normed_full.reshape(T, D), d_proj, 0, 0), 0)
    in_own, attn_gain_part = comm_call(
        functools.partial(last_kernel, n, C, S), "last", 3,
        [sds((C, S, D), F32), sds((1, D), F32)],
        [rbufs(), rbufs(), pltpu.VMEM((C, S, D), F32), gsem(), gsem()],
        (dn_part, d_middle, x_own, attn_gain[None]))
    small = lax.psum((attn_gain_part[0], qg_part, kg_part, mlp_gain_part[0]), ("wide", "narrow"))
    return (
        out_own[:, None], in_own[:, None], small[0],
        qkv_share[:, :QC], qkv_share[:, QC:QC + KC], qkv_share[:, QC + KC:],
        small[1], small[2], out_share, small[3], both_share[:, :FC], both_share[:, FC:], down_share,
    )


def solution(mesh):
    in_specs = (
        P(None, "wide", "narrow", None), P(None, "wide", None), P(), P(None, "narrow"), P(None, "narrow"), P(None, "narrow"),
        P(), P(), P("narrow", None), P(), P(None, "narrow"), P(None, "narrow"), P("narrow", None),
        P(None, "wide", "narrow", None),
    )
    out_specs = (
        P(None, "wide", "narrow", None), P(None, "wide", "narrow", None), P(), P("wide", "narrow"), P("wide", "narrow"),
        P("wide", "narrow"), P(), P(), P("narrow", "wide"), P(), P("wide", "narrow"), P("wide", "narrow"), P("narrow", "wide"),
    )
    return jax.shard_map(local, mesh=mesh, in_specs=in_specs, out_specs=out_specs, check_vma=False)
```

```python
import functools

import jax
import jax.numpy as jnp
import numpy as np
from jax import lax
from jax.experimental import pallas as pl
from jax.experimental.pallas import tpu as pltpu
from jax.sharding import PartitionSpec as P

MESH = pl.DeviceIdType.MESH
F32 = jnp.float32
BF16 = jnp.bfloat16
norm_eps = 1e-06
masked_score = -1e30
HALVES = 2


def both(*conds):
    out = conds[0]
    for cond in conds[1:]:
        out = jnp.logical_and(out, cond)
    return out


def rows_at(index, rows):
    return pl.ds(pl.multiple_of(index * rows, rows), rows)


def lanes(index, width):
    return pl.ds(pl.multiple_of(index * width, width), width)


def dot(a, b, ca, cb):
    return lax.dot_general(a, b, (((ca,), (cb,)), ((), ())), preferred_element_type=F32)


def remote(src, dst, ssem, rsem, wide, narrow):
    return pltpu.make_async_remote_copy(
        src_ref=src, dst_ref=dst, send_sem=ssem, recv_sem=rsem, device_id=(wide, narrow), device_id_type=MESH
    )


def barrier(n, wide=0):
    w, z = lax.axis_index("wide"), lax.axis_index("narrow")
    bar = pltpu.get_barrier_semaphore()
    for step in range(1, n):
        pl.semaphore_signal(bar, inc=1, device_id=(w, lax.rem(z + step, n)), device_id_type=MESH)
    for step in range(1, wide):
        pl.semaphore_signal(bar, inc=1, device_id=(lax.rem(w + step, wide), z), device_id_type=MESH)
    pl.semaphore_wait(bar, n - 1 + max(wide - 1, 0))


class Line:
    def __init__(self, n, C, S):
        self.n, self.C, self.S = n, C, S
        self.pieces, self.rows = C * HALVES, S // HALVES
        self.w, self.z = lax.axis_index("wide"), lax.axis_index("narrow")

    def at(self, ref, chunk, p):
        start = chunk * self.S + (p % HALVES) * self.rows
        return ref.at[p // HALVES, pl.ds(pl.multiple_of(start, self.rows), self.rows)]


class Gather(Line):
    def __init__(self, n, C, S, full, ssem, rsem):
        super().__init__(n, C, S)
        self.full, self.ssem, self.rsem = full, ssem, rsem

    def copy(self, way, hop, p):
        chunk = self.z - hop if way == 0 else self.z + hop
        where = self.at(self.full, chunk, p)
        z_to = self.z + 1 if way == 0 else self.z - 1
        return remote(where, where, self.ssem.at[way, hop, p], self.rsem.at[way, hop, p], self.w, z_to)

    def arrival(self, way, hop, p):
        chunk = self.z - hop - 1 if way == 0 else self.z + hop + 1
        where = self.at(self.full, chunk, p)
        z_to = self.z + 1 if way == 0 else self.z - 1
        return remote(where, where, self.ssem.at[way, hop, p], self.rsem.at[way, hop, p], self.w, z_to)

    def has(self, way, hop):
        return self.z >= hop if way == 0 else self.z + hop <= self.n - 1

    def can_send(self, way, hop):
        edge = self.z < self.n - 1 if way == 0 else self.z > 0
        return both(self.has(way, hop), edge, hop < self.n - 1)

    def send(self, hop, p, ok=True):
        known = isinstance(hop, int)
        for way in (0, 1):
            if not (known and hop == 0):
                @pl.when(both(ok, hop > 0, self.has(way, hop)))
                def _():
                    self.arrival(way, hop - 1, p).wait_recv()

            if not (known and hop >= self.n - 1):
                @pl.when(both(ok, self.can_send(way, hop)))
                def _():
                    self.copy(way, hop, p).start()

    def drain(self):
        def step(t, carry):
            hop, p = t // self.pieces, t % self.pieces
            for way in (0, 1):
                @pl.when(self.can_send(way, hop))
                def _():
                    self.copy(way, hop, p).wait_send()
            return carry

        lax.fori_loop(0, (self.n - 1) * self.pieces, step, 0)


class Scatter(Line):
    def __init__(self, n, C, S, partial, sbuf, rbuf, ssem, rsem):
        super().__init__(n, C, S)
        self.partial, self.sbuf, self.rbuf, self.ssem, self.rsem = partial, sbuf, rbuf, ssem, rsem

    def copy(self, way, d, p):
        z_to = self.z + 1 - 2 * way
        slot = jnp.where(both(way == 1, d == z_to), self.n, d)
        return remote(
            self.at(self.sbuf, d, p), self.at(self.rbuf, slot, p), self.ssem.at[d, p], self.rsem.at[way, d, p], self.w, z_to
        )

    def slot(self, way, d):
        return jnp.where(both(way == 1, d == self.z), self.n, d)

    def arrived(self, way, d, p):
        where = self.at(self.rbuf, self.slot(way, d), p)
        remote(where, where, self.ssem.at[d, p], self.rsem.at[way, d, p], self.w, self.z).wait_recv()
        return where[...].astype(F32)

    def originate(self, p):
        def step(i, carry):
            way = jnp.where(self.z == 0, 0, 1)
            d = jnp.where(self.z == 0, self.n - 1 - i, i)

            @pl.when(jnp.logical_or(self.z == 0, self.z == self.n - 1))
            def _():
                if self.partial is not self.sbuf:
                    self.at(self.sbuf, d, p)[...] = self.at(self.partial, d, p)[...].astype(BF16)
                self.copy(way, d, p).start()

            return carry

        lax.fori_loop(0, self.n - 1, step, 0)

    def relay(self, i, p, ok=True):
        def step(order, carry):
            way = jnp.where(self.z < self.n // 2, order, 1 - order)
            d = jnp.where(way == 0, self.n - 1 - i, i)
            goes = jnp.where(way == 0, d > self.z, d < self.z)

            @pl.when(both(ok, goes, self.z > 0, self.z < self.n - 1))
            def _():
                value = self.arrived(way, d, p) + self.at(self.partial, d, p)[...].astype(F32)
                self.at(self.sbuf, d, p)[...] = value.astype(BF16)
                self.copy(way, d, p).start()

            return carry

        lax.fori_loop(0, 2, step, 0)

    def final(self, p, acc):
        acc[...] = self.at(self.partial, self.z, p)[...].astype(F32)
        for way, there in ((0, self.z > 0), (1, self.z < self.n - 1)):
            @pl.when(there)
            def _():
                acc[...] += self.arrived(way, self.z, p)

    def drain(self):
        def step(t, carry):
            d, p = t // self.pieces, t % self.pieces

            @pl.when(d != self.z)
            def _():
                self.copy(jnp.where(d > self.z, 0, 1), d, p).wait_send()

            return carry

        lax.fori_loop(0, self.n * self.pieces, step, 0)


def rms_scale(values):
    return lax.rsqrt(jnp.mean(values * values, axis=-1, keepdims=True) + norm_eps)


def rms_back(grad_in, hat, scale_rows):
    return scale_rows * (grad_in - hat * jnp.mean(grad_in * hat, axis=-1, keepdims=True))


def rope(v, cos2, sin2):
    return v * cos2 + pltpu.roll(v, v.shape[-1] // 2, axis=1) * sin2


def for_arrived(gath, hop, body):
    z, n = gath.z, gath.n
    if hop == 0:
        body(z)
        return
    left = (z >= hop).astype(jnp.int32)
    right = (z + hop <= n - 1).astype(jnp.int32)

    def step(i, carry):
        use_left = both(left == 1, i == 0)
        body(jnp.where(use_left, z - hop, z + hop))
        return carry

    lax.fori_loop(0, left + right, step, 0)


def front_kernel(n, C, S, HD, docs,
                 x_ref, gain_ref, lens_ref, freq_ref, qg_ref, kg_ref, wq_hbm, wk_hbm, wv_hbm,
                 normed_ref, q_ref, k_ref, qrot_ref, krot_ref, v_ref, prob_ref, mix_ref, cos_ref, sin_ref,
                 wq, wk, wv, bias, ssem, rsem, wsem):
    R = n * S
    QC, KC = wq.shape[1], wk.shape[1]
    G = QC // KC
    KH = KC // HD
    loads = [pltpu.make_async_copy(a, b, wsem.at[i]) for i, (a, b) in enumerate(((wq_hbm, wq), (wk_hbm, wk), (wv_hbm, wv)))]
    for load in loads:
        load.start()
    gath = Gather(n, C, S, normed_ref, ssem, rsem)
    z = gath.z
    for part in range(C):
        x = x_ref[part].astype(F32)
        normed_ref[part, rows_at(z, S)] = (x * rms_scale(x) * gain_ref[...].astype(F32)).astype(BF16)
    barrier(n)
    for p in range(gath.pieces):
        gath.send(0, p)
    for part in range(C):
        t = lax.broadcasted_iota(jnp.int32, (R, HD), 0)
        row = lax.broadcasted_iota(jnp.int32, (R, R), 0)
        col = lax.broadcasted_iota(jnp.int32, (R, R), 1)
        first = jnp.zeros((R, HD), jnp.int32)
        first_wide = jnp.zeros((R, R), jnp.int32)
        end = jnp.int32(0)
        for d in range(docs):
            end = end + lens_ref[part, d]
            first = jnp.where(t >= end, end, first)
            first_wide = jnp.where(row >= end, end, first_wide)
        angle = (t - first).astype(F32) * freq_ref[...]
        sign = jnp.where(lax.broadcasted_iota(jnp.int32, (R, HD), 1) < HD // 2, -1.0, 1.0)
        cos_ref[part] = jnp.cos(angle)
        sin_ref[part] = jnp.sin(angle) * sign
        bias[part] = jnp.where(both(col <= row, col >= first_wide), 0.0, masked_score)
    for load in loads:
        load.wait()

    def project(chunk, parts):
        rows = rows_at(chunk, S)
        lhs = jnp.concatenate([normed_ref[p, rows] for p in parts], axis=0)
        for w, out in ((wq, q_ref), (wk, k_ref), (wv, v_ref)):
            res = dot(lhs, w[...], 1, 0).astype(out.dtype)
            for i, p in enumerate(parts):
                out[p, rows] = res[i * S:(i + 1) * S]

    def attend(part):
        def heads(k, carry):
            cos2, sin2 = cos_ref[part], sin_ref[part]

            def turned(src, gain, col):
                raw = src[part, :, lanes(col, HD)]
                return rope(raw * rms_scale(raw) * gain[...].astype(F32), cos2, sin2).astype(BF16)

            kr = turned(k_ref, kg_ref, k)
            krot_ref[part, :, lanes(k, HD)] = kr
            for g in range(G):
                qr = turned(q_ref, qg_ref, k * G + g)
                qrot_ref[part, :, lanes(k * G + g, HD)] = qr
                s = dot(qr, kr, 1, 1) * HD ** (-0.5) + bias[part]
                ex = jnp.exp(s - jnp.max(s, axis=-1, keepdims=True))
                prob = ex / jnp.sum(ex, axis=-1, keepdims=True)
                prob_ref[part, k * G + g] = prob
                mix = dot(prob.astype(BF16), v_ref[part, :, lanes(k, HD)], 1, 0)
                mix_ref[part, :, lanes(k * G + g, HD)] = mix.astype(BF16)
            return carry

        lax.fori_loop(0, KH, heads, 0)

    for hop in range(n - 1):
        if hop > 0:
            for p in range(gath.pieces):
                gath.send(hop, p)
        for_arrived(gath, hop, lambda chunk: project(chunk, tuple(range(C))))
    for part in range(C):
        for h in range(HALVES):
            gath.send(n - 1, part * HALVES + h)
        for_arrived(gath, n - 1, lambda chunk: project(chunk, (part,)))
        attend(part)
    gath.drain()


def weight_block(A, B, sib_a, sib_b, q, cols):
    total = None
    for part in range(A.shape[0]):
        for term in (dot(A[part, :, cols], B[part], 0, 0), dot(sib_a[q, part], sib_b[part], 0, 0)):
            total = term if total is None else total + term
    return total


def middle_kernel(n, C, S, W, push, *refs):
    (x_ref, cot_ref, gain_ref, mix_hbm, wout_hbm, wgate_hbm, wup_hbm, wdown_hbm,
     middle_ref, dmid_ref, gaing_ref, dmix_ref, db_hbm, mlp_hbm) = refs[:14]
    rest = list(refs[14:])
    if push:
        sib_n2, sib_cot, sib_act, sib_dg, sib_du, recv_down, blk_gate, blk_up, own_down, own_gate, own_up = rest[:11]
        rest = rest[11:]
    else:
        n2_hbm, cot_hbm, act_hbm, dg_hbm, du_hbm = rest[:5]
        rest = rest[5:]
    (mixv, wout, wgate, wup, wdown, cotf, n2f, dbf, partial, sbuf, rbuf, sbufm, dact, act, dg, du, acc,
     wsem, cs, cr, s1s, s1r, g2s, g2r, s2s, s2r, g3s, g3r, osem) = rest[:29]
    rest = rest[29:]
    if push:
        stage, stage32, cols_sib, b_sib, sib_ss, sib_rs, down_ss, down_rs, lsem, ssem32 = rest
    R = n * S
    D = x_ref.shape[2]
    FC = wgate.shape[1]
    TN = 512
    nt, nd = FC // TN, D // TN
    P_ = C * HALVES
    rows = S // HALVES
    w, z = lax.axis_index("wide"), lax.axis_index("narrow")
    loads = [pltpu.make_async_copy(a, b, wsem.at[i]) for i, (a, b) in enumerate(
        ((mix_hbm, mixv), (wout_hbm, wout), (wdown_hbm, wdown), (wgate_hbm, wgate), (wup_hbm, wup)))]
    for load in loads:
        load.start()
    for part in range(C):
        cotf[part, rows_at(z, S)] = cot_ref[part]
    barrier(n, W if push else 0)
    gc = Gather(n, C, S, cotf, cs, cr)
    g2 = Gather(n, C, S, n2f, g2s, g2r)
    g3 = Gather(n, C, S, dbf, g3s, g3r)
    s1 = Scatter(n, C, S, partial, sbuf, rbuf, s1s, s1r)
    s2 = Scatter(n, C, S, partial, sbuf, rbuf, s2s, s2r)
    gain = gain_ref[...].astype(F32)
    loads[0].wait()
    loads[1].wait()

    def tiles(count, body):
        def step(j, carry):
            body(j)
            return carry

        lax.fori_loop(0, count, step, 0)

    for part in range(C):
        def out_tile(j):
            partial[part, :, lanes(j, TN)] = dot(mixv[part], wout[:, lanes(j, TN)], 1, 0)

        tiles(nd, out_tile)
        if part == 0:
            for p in range(2):
                s1.originate(p)
                gc.send(0, p)

    def mid_row(p):
        return p // HALVES, rows_at(p % HALVES, rows)

    def phase_one(p):
        @pl.when(p + 2 < P_)
        def _():
            s1.originate(p + 2)
            gc.send(0, p + 2)

        def service(i, carry):
            s1.relay(i, p, p < P_)
            gc.send(i + 1, p, p < P_)
            g2.send(i + 1, p - 1, p > 0)
            return carry

        lax.fori_loop(0, n - 1, service, 0)
        s1.final(p, acc)
        part, rr = mid_row(p)
        middle = x_ref[part, rr].astype(F32) + acc[...]
        middle_ref[part, rr] = middle
        g2.at(n2f, z, p)[...] = (middle * rms_scale(middle) * gain).astype(BF16)
        g2.send(0, p)

    tiles(P_, phase_one)
    loads[2].wait()

    def dact_tile(part, j):
        dact[:, lanes(j, TN)] = dot(cotf[part], wdown[rows_at(j, TN), :], 1, 1)

    for i in range(max(n - 1, nt)):
        if i < nt:
            dact_tile(0, i)
        if i < n - 1:
            g2.send(i + 1, P_ - 1)
    s1.drain()
    if push:
        core = w % 2
        mate = w + 1 - 2 * core
        Q = W // 2
        q_me = w // 2

        def swap(index, src, dst, part):
            return remote(src.at[part], dst.at[part], sib_ss.at[index, part], sib_rs.at[index, part], mate, z)

        for part in range(C):
            swap(0, n2f, sib_n2, part).start()
            swap(1, cotf, sib_cot, part).start()
    loads[3].wait()
    loads[4].wait()

    def service(t, ok=True):
        p, i = t // (n - 1), t % (n - 1)
        s2.relay(i, p, both(ok, p < P_))

        @pl.when(both(ok, i == n - 2, p < P_))
        def _():
            s2.final(p, acc)
            part, rr = mid_row(p)
            dn2 = acc[...]
            middle = middle_ref[part, rr]
            scale = rms_scale(middle)
            hat = middle * scale
            gaing_ref[...] += jnp.sum(dn2 * hat, axis=0, keepdims=True)
            dmid = cot_ref[part, rr].astype(F32) + rms_back(dn2 * gain, hat, scale)
            dmid_ref[part, rr] = dmid
            g3.at(dbf, z, p)[...] = dmid.astype(BF16)

        g3.send(i + 1, p - 1, both(ok, p > 0, p <= P_))

        @pl.when(both(ok, i == n - 2, p < P_))
        def _():
            g3.send(0, p)

    gaing_ref[...] = jnp.zeros_like(gaing_ref)
    per_part = HALVES * (n - 1)

    def feed(part):
        def gate_tile(j):
            @pl.when(part > 0)
            def _():
                dact_tile(part, j)

            at = lanes(j, TN)
            gate = dot(n2f[part], wgate[:, at], 1, 0)
            up = dot(n2f[part], wup[:, at], 1, 0)
            sig = jax.nn.sigmoid(gate)
            silu = gate * sig
            d_act = dact[:, at]
            act[part, :, at] = (silu * up).astype(BF16)
            dg[part, :, at] = (d_act * up * sig * (1.0 + gate * (1.0 - sig))).astype(BF16)
            du[part, :, at] = (d_act * silu).astype(BF16)
            service((part - 1) * per_part + j, both(part > 0, j < per_part))

        tiles(nt, gate_tile)
        if push:
            swap(2, act, sib_act, part).start()
            swap(3, dg, sib_dg, part).start()
            swap(4, du, sib_du, part).start()

        def back_tile(j):
            at = rows_at(j, TN)
            partial[part, :, lanes(j, TN)] = dot(dg[part], wgate[at, :], 1, 1) + dot(du[part], wup[at, :], 1, 1)
            service((part - 1) * per_part + nt + j, both(part > 0, nt + j < per_part))

        tiles(nd, back_tile)
        for h in range(HALVES):
            s2.originate(part * HALVES + h)

    tiles(C, feed)

    def mlp_tile(j):
        for part in range(C):
            sbufm[part, :, lanes(j, TN)] = dot(act[part], wdown[:, lanes(j, TN)], 1, 0).astype(BF16)

    first = (C - 1) * per_part
    last = (P_ + 1) * (n - 1)
    if push:
        width = D // W

        def load_cols(src):
            for q in range(Q):
                for part in range(C):
                    yield pltpu.make_async_copy(
                        src.at[part, :, lanes(2 * q + core, width)], cols_sib.at[q, part], lsem.at[0, q, part])

        def load_b(src):
            for part in range(C):
                yield pltpu.make_async_copy(src.at[part], b_sib.at[part], lsem.at[1, 0, part])

        def fetch(copies):
            copies = list(copies)
            for copy in copies:
                copy.start()
            for copy in copies:
                copy.wait()

        def down_push(o):
            q = lax.rem(q_me + o, Q)
            return remote(stage.at[o - 1], recv_down.at[o - 1], down_ss.at[o - 1], down_rs.at[o - 1], 2 * q + core, z)

        def block(A, B, o):
            q = lax.rem(q_me + o, Q)
            return weight_block(A, B, cols_sib, b_sib, q, lanes(2 * q + core, width))

        def own_copy(dst, index):
            return pltpu.make_async_copy(stage32, dst, ssem32.at[index])

        def put_copy(dst, o, index):
            slot = Q - 1 + (o - 1) % 2
            return pltpu.make_async_copy(stage.at[slot], dst.at[o - 1], osem.at[4 + index * (Q - 1) + o - 1])

        work = []

        def start_down():
            for part in range(C):
                swap(1, sib_cot, sib_cot, part).wait_recv()
                swap(2, sib_act, sib_act, part).wait_recv()
            fetch(load_cols(sib_cot))
            fetch(load_b(sib_act))

        def down(o):
            if o == 1:
                start_down()
            if o < Q:
                stage[o - 1] = block(cotf, act, o).astype(BF16)
                down_push(o).start()
            else:
                stage32[...] = block(cotf, act, 0)
                own_copy(own_down, 0).start()

        def other(index, B, sib_b, own, blocks, o):
            if o == 1:
                for part in range(C):
                    if index == 0:
                        swap(0, sib_n2, sib_n2, part).wait_recv()
                    swap(3 + index, sib_b, sib_b, part).wait_recv()
                if index == 0:
                    fetch(load_cols(sib_n2))
                fetch(load_b(sib_b))
            if o < Q:
                if o > 2:
                    put_copy(blocks, o - 2, index).wait()
                elif index > 0:
                    prev = Q - 1 - (Q - 1 - o) % 2
                    put_copy(blk_gate, prev, 0).wait()
                stage[Q - 1 + (o - 1) % 2] = block(n2f, B, o).astype(BF16)
                put_copy(blocks, o, index).start()
            else:
                own_copy(own_gate, index).wait()
                stage32[...] = block(n2f, B, 0)
                own_copy(own, index + 1).start()

        for o in range(1, Q + 1):
            work.append(functools.partial(down, o))
        for j in range(nd):
            work.append(functools.partial(mlp_tile, j))
        for o in range(1, Q + 1):
            work.append(functools.partial(other, 0, dg, sib_dg, own_gate, blk_gate, o))
        for o in range(1, Q + 1):
            work.append(functools.partial(other, 1, du, sib_du, own_up, blk_up, o))
        steps = last - first
        done = 0
        for k in range(steps):
            service(first + k)
            upto = -(-len(work) * (k + 1) // steps)
            for piece in work[done:upto]:
                piece()
            done = upto
    else:
        tiles(last - first, lambda k: service(first + k))
        tiles(nd, mlp_tile)
        outs = [pltpu.make_async_copy(a, b, osem.at[4 + i]) for i, (a, b) in enumerate(
            ((n2f, n2_hbm), (cotf, cot_hbm), (act, act_hbm), (dg, dg_hbm), (du, du_hbm)))]
        for out in outs:
            out.start()
    mlp_out = pltpu.make_async_copy(sbufm, mlp_hbm, osem.at[0])
    mlp_out.start()
    db_out = pltpu.make_async_copy(dbf, db_hbm, osem.at[1])
    db_out.start()
    for part in range(C):
        dmix_ref[part] = dot(dbf[part], wout[...], 1, 1).astype(BF16)
    mlp_out.wait()
    db_out.wait()
    gc.drain()
    g2.drain()
    g3.drain()
    s2.drain()
    if push:
        for part in range(C):
            for index, (a, b) in enumerate(((n2f, sib_n2), (cotf, sib_cot), (act, sib_act), (dg, sib_dg), (du, sib_du))):
                swap(index, a, b, part).wait_send()
        for index, blocks in enumerate((blk_gate, blk_up)):
            for o in range(1, Q):
                if index == 1 and o > Q - 3:
                    put_copy(blocks, o, index).wait()
        own_copy(own_up, 2).wait()
        for o in range(1, Q):
            down_push(o).wait_send()
            down_push(o).wait_recv()
    else:
        for out in outs:
            out.wait()


def last_kernel(n, C, S, W, HD, push, *refs):
    (x_ref, middle_ref, dmid_ref, gain_ref, qg_ref, kg_ref, gmlp_ref, q_ref, k_ref, qrot_ref, krot_ref, v_ref, prob_ref,
     cos_ref, sin_ref, dmix_ref, mlp_hbm, wq_hbm, wk_hbm, wv_hbm) = refs[:20]
    rest = list(refs[20:])
    if push:
        mix_hbm, db_hbm, normed_hbm, blk_gate, blk_up = rest[:5]
        rest = rest[5:]
    out_ref, in_ref, ga_ref, gm_ref, gq_ref, gk_ref = rest[:6]
    rest = rest[6:]
    if push:
        recv_gate, recv_up, recv_out, recv_qkv, own_out, own_qkv = rest[:6]
        rest = rest[6:]
    else:
        dproj_hbm = rest[0]
        rest = rest[1:]
    (wq, wk, wv, dproj, partial, sbuf, rbuf, sbufm, rbufm, acc, gains, small, small_two,
     lsem, s3s, s3r, sms, smr, gs1, gr1, gs2, gr2) = rest[:22]
    rest = rest[22:]
    if push:
        (mixv, dbv, normv, sib_mix, sib_db, sib_norm, sib_dproj, stage_out, stage_qkv,
         sib_ss, sib_rs, push_ss, push_rs) = rest
    R, D = n * S, x_ref.shape[2]
    QC, KC = wq.shape[1], wk.shape[1]
    G, KH = QC // KC, KC // HD
    TN = 512
    nd = D // TN
    P_ = C * HALVES
    rows = S // HALVES
    w, z = lax.axis_index("wide"), lax.axis_index("narrow")
    pairs = [(mlp_hbm, sbufm), (wq_hbm, wq), (wk_hbm, wk), (wv_hbm, wv)]
    if push:
        pairs += [(mix_hbm, mixv), (db_hbm, dbv), (normed_hbm, normv)]
    loads = [pltpu.make_async_copy(a, b, lsem.at[i]) for i, (a, b) in enumerate(pairs)]
    for load in loads:
        load.start()
    barrier(n, W)
    sm = Scatter(n, C, S, sbufm, sbufm, rbufm, sms, smr)
    s3 = Scatter(n, C, S, partial, sbuf, rbuf, s3s, s3r)
    if push:
        core = w % 2
        mate = w + 1 - 2 * core
        Q = W // 2
        q_me = w // 2
        width = D // W

        def direct(index, src, dst, o):
            q = lax.rem(q_me + o, Q)
            return remote(src.at[o - 1], dst.at[o - 1], push_ss.at[index, o - 1], push_rs.at[index, o - 1], 2 * q + core, z)

        def swap(index, src, dst, part):
            return remote(src.at[part], dst.at[part], sib_ss.at[index, part], sib_rs.at[index, part], mate, z)

        for index, (src, dst) in enumerate(((blk_gate, recv_gate), (blk_up, recv_up))):
            for o in range(1, Q):
                direct(index, src, dst, o).start()
    loads[0].wait()
    for p in range(2):
        sm.originate(p)
    if push:
        for load in loads[4:]:
            load.wait()
        for part in range(C):
            for index, (a, b) in enumerate(((mixv, sib_mix), (dbv, sib_db), (normv, sib_norm))):
                swap(index, a, b, part).start()

    def piece_row(p):
        return p // HALVES, rows_at(p % HALVES, rows)

    def mlp_service(p):
        for i in range(n - 1):
            sm.relay(i, p)
        sm.final(p, acc)
        part, rr = piece_row(p)
        out_ref[part, rr] = middle_ref[part, rr] + acc[...]

        @pl.when(p + 2 < P_)
        def _():
            sm.originate(p + 2)

    gain = gain_ref[...].astype(F32)

    def service(t):
        p, i = t // (n - 1), t % (n - 1)
        s3.relay(i, p)

        @pl.when(i == n - 2)
        def _():
            s3.final(p, acc)
            part, rr = piece_row(p)
            dn = acc[...]
            x = x_ref[part, rr].astype(F32)
            scale = rms_scale(x)
            hat = x * scale
            gains[0:1, :] += jnp.sum(dn * hat, axis=0, keepdims=True)
            in_ref[part, rr] = dmid_ref[part, rr] + rms_back(dn * gain, hat, scale)

    gains[...] = jnp.zeros_like(gains)
    scale = HD ** (-0.5)
    qgain, kgain = qg_ref[...].astype(F32), kg_ref[...].astype(F32)

    def unit(part, k):
        cos2, sin2 = cos_ref[part], sin_ref[part]
        kr, vr = krot_ref[part, :, lanes(k, HD)], v_ref[part, :, lanes(k, HD)]

        def unturned(grad, raw, head_gain, at):
            d_n = grad * cos2 - pltpu.roll(grad, HD // 2, axis=1) * sin2
            r = rms_scale(raw)
            hat = raw * r
            gains[at:at + 1, :HD] += jnp.sum(d_n * hat, axis=0, keepdims=True)
            return rms_back(d_n * head_gain, hat, r).astype(BF16)

        dk, dv = None, None
        for g in range(G):
            h = k * G + g
            pr = prob_ref[part, h]
            dm = dmix_ref[part, :, lanes(h, HD)]
            dp = dot(dm, vr, 1, 1)
            one = dot(pr.astype(BF16), dm, 0, 0)
            dv = one if dv is None else dv + one
            ds = (pr * (dp - jnp.sum(pr * dp, axis=-1, keepdims=True))).astype(BF16)
            one = dot(ds, qrot_ref[part, :, lanes(h, HD)], 0, 0)
            dk = one if dk is None else dk + one
            dq = dot(ds, kr, 1, 0) * scale
            dproj[part, :, lanes(h, HD)] = unturned(dq, q_ref[part, :, lanes(h, HD)], qgain, 1)
        dproj[part, :, lanes(QC // HD + k, HD)] = unturned(dk * scale, k_ref[part, :, lanes(k, HD)], kgain, 2)
        dproj[part, :, lanes(QC // HD + KH + k, HD)] = dv.astype(BF16)

    pieces_per_unit = -(-P_ // (C * KH))

    def backward(part):
        def heads(k, carry):
            unit(part, k)
            for e in range(pieces_per_unit):
                p = (part * KH + k) * pieces_per_unit + e

                @pl.when(p < P_)
                def _():
                    mlp_service(p)

            return carry

        lax.fori_loop(0, KH, heads, 0)

        @pl.when(part == 0)
        def _():
            for load in loads[1:4]:
                load.wait()

        if push:
            swap(3, dproj, sib_dproj, part).start()

        def back_tile(j, carry):
            at = rows_at(j, TN)
            partial[part, :, lanes(j, TN)] = (
                dot(dproj[part, :, 0:QC], wq[at, :], 1, 1) + dot(dproj[part, :, QC:QC + KC], wk[at, :], 1, 1)
                + dot(dproj[part, :, QC + KC:QC + 2 * KC], wv[at, :], 1, 1))
            return carry

        lax.fori_loop(0, nd, back_tile, 0)
        for h in range(HALVES):
            s3.originate(part * HALVES + h)

    def both_parts(part, carry):
        backward(part)
        return carry

    lax.fori_loop(0, C, both_parts, 0)
    steps = P_ * (n - 1)
    if push:
        def block(A, B, sib_a, sib_b, q):
            cols = lanes(2 * q + core, width)
            total = None
            for part in range(C):
                for term in (dot(A[part, :, cols], B[part], 0, 0), dot(sib_a[part, :, cols], sib_b[part], 0, 0)):
                    total = term if total is None else total + term
            return total

        def out_block(o):
            if o == 1:
                for part in range(C):
                    for index, (a, b) in enumerate(((mixv, sib_mix), (dbv, sib_db), (normv, sib_norm), (dproj, sib_dproj))):
                        swap(index, a, b, part).wait_recv()
            if o < Q:
                stage_out[o - 1] = block(dbv, mixv, sib_db, sib_mix, lax.rem(q_me + o, Q)).astype(BF16)
                direct(2, stage_out, recv_out, o).start()
            else:
                own_out[...] = block(dbv, mixv, sib_db, sib_mix, q_me)

        def qkv_block(o):
            if o < Q:
                stage_qkv[o - 1] = block(normv, dproj, sib_norm, sib_dproj, lax.rem(q_me + o, Q)).astype(BF16)
                direct(3, stage_qkv, recv_qkv, o).start()
            else:
                own_qkv[...] = block(normv, dproj, sib_norm, sib_dproj, q_me)

        work = [functools.partial(f, o) for f in (qkv_block, out_block) for o in range(1, Q + 1)]
        work = [functools.partial(f, o) for f in (out_block, qkv_block) for o in range(1, Q)] + [
            functools.partial(f, Q) for f in (out_block, qkv_block)]
        done = 0
        for k in range(steps):
            service(k)
            upto = min(len(work), k + 1)
            for piece in work[done:upto]:
                piece()
            done = upto
        for piece in work[done:]:
            piece()
    else:
        def only_service(k, carry):
            service(k)
            return carry

        lax.fori_loop(0, steps, only_service, 0)
        out = pltpu.make_async_copy(dproj, dproj_hbm, lsem.at[4])
        out.start()
    L = 2 * D + 2 * HD
    small[w, :, 0:D] = gains[0:1, :]
    small[w, :, D:2 * D] = gmlp_ref[...]
    small[w, :, 2 * D:2 * D + HD] = gains[1:2, :HD]
    small[w, :, 2 * D + HD:L] = gains[2:3, :HD]

    def to_wide(s):
        return remote(small.at[w], small.at[w], gs1.at[s], gr1.at[s], lax.rem(w + s, W), z)

    def to_narrow(s):
        return remote(small_two.at[z], small_two.at[z], gs2.at[s], gr2.at[s], w, lax.rem(z + s, n))

    for s in range(1, W):
        to_wide(s).start()
    for s in range(1, W):
        to_wide(s).wait_recv()
    total = small[0]
    for s in range(1, W):
        total = total + small[s]
    small_two[z] = total
    for s in range(1, n):
        to_narrow(s).start()
    for s in range(1, n):
        to_narrow(s).wait_recv()
    total = small_two[0]
    for s in range(1, n):
        total = total + small_two[s]
    ga_ref[...] = total[:, 0:D]
    gm_ref[...] = total[:, D:2 * D]
    gq_ref[...] = total[:, 2 * D:2 * D + HD]
    gk_ref[...] = total[:, 2 * D + HD:L]
    for s in range(1, W):
        to_wide(s).wait_send()
    for s in range(1, n):
        to_narrow(s).wait_send()
    sm.drain()
    s3.drain()
    if push:
        for part in range(C):
            for index, (a, b) in enumerate(((mixv, sib_mix), (dbv, sib_db), (normv, sib_norm), (dproj, sib_dproj))):
                swap(index, a, b, part).wait_send()
        for index, (src, dst) in enumerate(((blk_gate, recv_gate), (blk_up, recv_up), (stage_out, recv_out), (stage_qkv, recv_qkv))):
            for o in range(1, Q):
                direct(index, src, dst, o).wait_send()
                direct(index, src, dst, o).wait_recv()
    else:
        out.wait()


def local(W, layer_input, document_lengths, attn_gain, w_query, w_key, w_value, query_gain, key_gain, w_out, mlp_gain,
          w_gate, w_up, w_down, output_cotangent):
    n = lax.axis_size("narrow")
    C, _, S, D = layer_input.shape
    R = n * S
    T = C * R
    HD = query_gain.shape[0]
    QC, KC = w_query.shape[1], w_key.shape[1]
    QH = QC // HD
    FC = w_gate.shape[1]
    docs = document_lengths.shape[2]
    P_ = C * HALVES
    push = W % 2 == 0 and W >= 4 and W <= 8 and (D // W) % 128 == 0
    Q = W // 2
    width = D // W
    x_own, cot_own = layer_input[:, 0], output_cotangent[:, 0]
    sds = jax.ShapeDtypeStruct
    dma = pltpu.SemaphoreType.DMA
    gsem = lambda: dma((2, n - 1, P_))
    half = np.arange(HD) % (HD // 2)
    freq = jnp.asarray(np.power(np.float32(1000000.0), np.float32(-2.0) * half.astype(np.float32) / np.float32(HD))[None], F32)
    vm = pl.BlockSpec(memory_space=pltpu.VMEM)
    hbm = pl.BlockSpec(memory_space=pl.ANY)
    smem = pl.BlockSpec(memory_space=pltpu.SMEM)
    VM = pltpu.VMEM

    normed_full, q_raw, k_raw, q_rot, k_rot, v_rows, prob, mix, cos2, sin2 = pl.pallas_call(
        functools.partial(front_kernel, n, C, S, HD, docs), name="front",
        out_shape=[sds((C, R, D), BF16), sds((C, R, QC), F32), sds((C, R, KC), F32), sds((C, R, QC), BF16), sds((C, R, KC), BF16),
                   sds((C, R, KC), BF16), sds((C, QH, R, R), F32), sds((C, R, QC), BF16), sds((C, R, HD), F32), sds((C, R, HD), F32)],
        in_specs=[vm, vm, smem, vm, vm, vm, hbm, hbm, hbm], out_specs=[vm] * 10,
        scratch_shapes=[VM(w_query.shape, BF16), VM(w_key.shape, BF16), VM(w_value.shape, BF16),
                        VM((C, R, R), F32), gsem(), gsem(), dma((3,))],
        compiler_params=pltpu.CompilerParams(collective_id=0, has_side_effects=True, vmem_limit_bytes=48 << 20),
    )(x_own, attn_gain[None], document_lengths[:, 0], freq, query_gain[None], key_gain[None], w_query, w_key, w_value)

    full, wide_rows = sds((C, R, D), BF16), sds((C, R, FC), BF16)
    outs = [sds((C, S, D), F32), sds((C, S, D), F32), sds((1, D), F32), sds((C, R, QC), BF16), full, full]
    specs = [vm, vm, vm, vm, hbm, hbm]
    line = lambda: [VM((C, R, D), BF16), VM((C, R + S, D), BF16)]
    scratch = (
        [VM((C, R, QC), BF16), VM(w_out.shape, BF16), VM(w_gate.shape, BF16), VM(w_up.shape, BF16), VM(w_down.shape, BF16)]
        + [VM((C, R, D), BF16)] * 3 + [VM((C, R, D), F32)] + line()
        + [VM((C, R, D), BF16), VM((R, FC), F32)] + [VM((C, R, FC), BF16)] * 3 + [VM((S // HALVES, D), F32)]
        + [dma((5,)), gsem(), gsem(), dma((n, P_)), dma((2, n, P_)), gsem(), gsem(), dma((n, P_)), dma((2, n, P_)),
           gsem(), gsem(), dma((4 + max(2 * (Q - 1), 5),))]
    )
    if push:
        some, own = sds((Q - 1, width, FC), BF16), sds((width, FC), F32)
        outs += [full, full, wide_rows, wide_rows, wide_rows, some, some, some, own, own, own]
        scratch += [VM((Q + 1, width, FC), BF16), VM((width, FC), F32), VM((Q, C, R, width), BF16), VM((C, R, FC), BF16),
                    dma((5, C)), dma((5, C)), dma((Q - 1,)), dma((Q - 1,)), dma((2, Q, C)), dma((3,))]
    else:
        outs += [full, full, wide_rows, wide_rows, wide_rows]
    res = pl.pallas_call(
        functools.partial(middle_kernel, n, C, S, W, push), name="middle", out_shape=outs,
        in_specs=[vm] * 3 + [hbm] * 5, out_specs=specs + [hbm] * (len(outs) - len(specs)), scratch_shapes=scratch,
        compiler_params=pltpu.CompilerParams(collective_id=1, has_side_effects=True, vmem_limit_bytes=63 << 20),
    )(x_own, cot_own, mlp_gain[None], mix, w_out, w_gate, w_up, w_down)
    middle, d_middle, gmlp, d_mix, db_full, mlp_sums = res[:6]

    args = [x_own, middle, d_middle, attn_gain[None], query_gain[None], key_gain[None], gmlp, q_raw, k_raw, q_rot, k_rot, v_rows,
            prob, cos2, sin2, d_mix, mlp_sums, w_query, w_key, w_value]
    in_specs = [vm] * 16 + [hbm] * 4
    own_rows = sds((C, S, D), F32)
    outs = [own_rows, own_rows, sds((1, D), F32), sds((1, D), F32), sds((1, HD), F32), sds((1, HD), F32)]
    specs = [vm] * 6
    PC = QC + 2 * KC
    L = 2 * D + 2 * HD
    scratch = (
        [VM(w_query.shape, BF16), VM(w_key.shape, BF16), VM(w_value.shape, BF16), VM((C, R, PC), BF16), VM((C, R, D), F32)]
        + line() + line() + [VM((S // HALVES, D), F32), VM((8, D), F32), VM((W, 1, L), F32), VM((n, 1, L), F32)]
        + [dma((7,)), dma((n, P_)), dma((2, n, P_)), dma((n, P_)), dma((2, n, P_)), dma((W,)), dma((W,)), dma((n,)), dma((n,))]
    )
    if push:
        sib_n2, sib_cot, sib_act, sib_dg, sib_du, recv_down, blk_gate, blk_up, own_down, own_gate, own_up = res[6:]
        args += [mix, db_full, normed_full, blk_gate, blk_up]
        in_specs += [hbm] * 5
        outs += [sds((Q - 1, width, FC), BF16)] * 2 + [sds((Q - 1, width, QC), BF16), sds((Q - 1, width, PC), BF16),
                                                       sds((width, QC), F32), sds((width, PC), F32)]
        specs += [hbm] * 4 + [vm] * 2
        scratch += [VM((C, R, QC), BF16), VM((C, R, D), BF16), VM((C, R, D), BF16)]
        scratch += [VM((C, R, QC), BF16), VM((C, R, D), BF16), VM((C, R, D), BF16), VM((C, R, PC), BF16)]
        scratch += [VM((Q - 1, width, QC), BF16), VM((Q - 1, width, PC), BF16)]
        scratch += [dma((4, C)), dma((4, C)), dma((4, Q - 1)), dma((4, Q - 1))]
    else:
        outs += [sds((C, R, PC), BF16)]
        specs += [hbm]
    last = pl.pallas_call(
        functools.partial(last_kernel, n, C, S, W, HD, push), name="last", out_shape=outs, in_specs=in_specs, out_specs=specs,
        scratch_shapes=scratch,
        compiler_params=pltpu.CompilerParams(collective_id=2, has_side_effects=True, vmem_limit_bytes=60 << 20),
    )(*args)
    out_own, in_own, g_attn, g_mlp, g_query, g_key = last[:6]
    if push:
        recv_gate, recv_up, recv_out, recv_qkv, own_out, own_qkv = last[6:]

        def gathered(own, parts):
            return own + jnp.sum(parts.astype(F32), axis=0)

        down = gathered(own_down, recv_down).T
        gate, up = gathered(own_gate, recv_gate), gathered(own_up, recv_up)
        out_g = gathered(own_out, recv_out).T
        qkv = gathered(own_qkv, recv_qkv)
    else:
        n2, cot, act, dg, du = [v.reshape(T, -1) for v in res[6:]]
        d_proj = last[6].reshape(T, PC)
        db, mixed, normed = db_full.reshape(T, D), mix.reshape(T, QC), normed_full.reshape(T, D)

        def scatter(a, b, dim):
            return lax.psum_scatter(dot(a, b, 0, 0).astype(BF16), "wide", scatter_dimension=dim, tiled=True).astype(F32)

        down, gate, up = scatter(act, cot, 1), scatter(n2, dg, 0), scatter(n2, du, 0)
        out_g, qkv = scatter(mixed, db, 1), scatter(normed, d_proj, 0)
    return (
        out_own[:, None], in_own[:, None], g_attn[0], qkv[:, :QC], qkv[:, QC:QC + KC], qkv[:, QC + KC:],
        g_query[0], g_key[0], out_g, g_mlp[0], gate, up, down,
    )


def solution(mesh):
    rows = P(None, "wide", "narrow", None)
    cols, tall = P(None, "narrow"), P("narrow", None)
    in_specs = (rows, P(None, "wide", None), P(), cols, cols, cols, P(), P(), tall, P(), cols, cols, tall, rows)
    both_ways, turned = P("wide", "narrow"), P("narrow", "wide")
    out_specs = (rows, rows, P(), both_ways, both_ways, both_ways, P(), P(), turned, P(), both_ways, both_ways, turned)
    body = functools.partial(local, mesh.shape["wide"])
    return jax.shard_map(body, mesh=mesh, in_specs=in_specs, out_specs=out_specs, check_vma=False)
```

```python
import functools

import jax
import jax.numpy as jnp
import numpy as np
from jax import lax
from jax.experimental import pallas as pl
from jax.experimental.pallas import tpu as pltpu
from jax.sharding import PartitionSpec as P

MESH = pl.DeviceIdType.MESH
F32 = jnp.float32
BF16 = jnp.bfloat16
norm_eps = 1e-06
masked_score = -1e30
HALVES = 2


def both(*conds):
    out = True
    for cond in conds:
        if isinstance(cond, bool):
            if not cond:
                return False
        else:
            out = cond if out is True else jnp.logical_and(out, cond)
    return out


def when(cond):
    if isinstance(cond, bool):
        return (lambda body: body()) if cond else (lambda body: None)
    return pl.when(cond)


def rows_at(index, rows):
    return pl.ds(pl.multiple_of(index * rows, rows), rows)


def lanes(index, width):
    return pl.ds(pl.multiple_of(index * width, width), width)


def dot(a, b, ca, cb):
    return lax.dot_general(a, b, (((ca,), (cb,)), ((), ())), preferred_element_type=F32)


def remote(src, dst, ssem, rsem, wide, narrow):
    return pltpu.make_async_remote_copy(
        src_ref=src, dst_ref=dst, send_sem=ssem, recv_sem=rsem, device_id=(wide, narrow), device_id_type=MESH
    )


def barrier(n, wide=0):
    w, z = lax.axis_index("wide"), lax.axis_index("narrow")
    bar = pltpu.get_barrier_semaphore()
    for step in range(1, n):
        pl.semaphore_signal(bar, inc=1, device_id=(w, lax.rem(z + step, n)), device_id_type=MESH)
    for step in range(1, wide):
        pl.semaphore_signal(bar, inc=1, device_id=(lax.rem(w + step, wide), z), device_id_type=MESH)
    pl.semaphore_wait(bar, n - 1 + max(wide - 1, 0))


class Line:
    def __init__(self, n, C, S):
        self.n, self.C, self.S = n, C, S
        self.pieces, self.rows = C * HALVES, S // HALVES
        self.w, self.z = lax.axis_index("wide"), lax.axis_index("narrow")

    def at(self, ref, chunk, p):
        start = chunk * self.S + (p % HALVES) * self.rows
        return ref.at[p // HALVES, pl.ds(pl.multiple_of(start, self.rows), self.rows)]


class Gather(Line):
    def __init__(self, n, C, S, full, ssem, rsem):
        super().__init__(n, C, S)
        self.full, self.ssem, self.rsem = full, ssem, rsem

    def copy(self, way, hop, p):
        chunk = self.z - hop if way == 0 else self.z + hop
        where = self.at(self.full, chunk, p)
        z_to = self.z + 1 if way == 0 else self.z - 1
        return remote(where, where, self.ssem.at[way, hop, p], self.rsem.at[way, hop, p], self.w, z_to)

    def arrival(self, way, hop, p):
        chunk = self.z - hop - 1 if way == 0 else self.z + hop + 1
        where = self.at(self.full, chunk, p)
        z_to = self.z + 1 if way == 0 else self.z - 1
        return remote(where, where, self.ssem.at[way, hop, p], self.rsem.at[way, hop, p], self.w, z_to)

    def has(self, way, hop):
        return self.z >= hop if way == 0 else self.z + hop <= self.n - 1

    def can_send(self, way, hop):
        edge = self.z < self.n - 1 if way == 0 else self.z > 0
        return both(self.has(way, hop), edge, hop < self.n - 1)

    def send(self, hop, p, ok=True):
        known = isinstance(hop, int)
        for way in (0, 1):
            if not (known and hop == 0):
                @when(both(ok, hop > 0, self.has(way, hop)))
                def _():
                    self.arrival(way, hop - 1, p).wait_recv()

            if not (known and hop >= self.n - 1):
                @when(both(ok, self.can_send(way, hop)))
                def _():
                    self.copy(way, hop, p).start()

    def drain(self):
        def step(t, carry):
            hop, p = t // self.pieces, t % self.pieces
            for way in (0, 1):
                @when(self.can_send(way, hop))
                def _():
                    self.copy(way, hop, p).wait_send()
            return carry

        lax.fori_loop(0, (self.n - 1) * self.pieces, step, 0)


class Scatter(Line):
    def __init__(self, n, C, S, partial, sbuf, rbuf, ssem, rsem):
        super().__init__(n, C, S)
        self.partial, self.sbuf, self.rbuf, self.ssem, self.rsem = partial, sbuf, rbuf, ssem, rsem

    def copy(self, way, d, p):
        z_to = self.z + 1 - 2 * way
        slot = jnp.where(both(way == 1, d == z_to), self.n, d)
        return remote(
            self.at(self.sbuf, d, p), self.at(self.rbuf, slot, p), self.ssem.at[d, p], self.rsem.at[way, d, p], self.w, z_to
        )

    def slot(self, way, d):
        return jnp.where(both(way == 1, d == self.z), self.n, d)

    def arrived(self, way, d, p):
        where = self.at(self.rbuf, self.slot(way, d), p)
        remote(where, where, self.ssem.at[d, p], self.rsem.at[way, d, p], self.w, self.z).wait_recv()
        return where[...].astype(F32)

    def originate(self, p):
        def step(i, carry):
            way = jnp.where(self.z == 0, 0, 1)
            d = jnp.where(self.z == 0, self.n - 1 - i, i)

            @when(jnp.logical_or(self.z == 0, self.z == self.n - 1))
            def _():
                if self.partial is not self.sbuf:
                    self.at(self.sbuf, d, p)[...] = self.at(self.partial, d, p)[...].astype(BF16)
                self.copy(way, d, p).start()

            return carry

        lax.fori_loop(0, self.n - 1, step, 0)

    def pass_on(self, order, p, ok=True):
        inner = both(ok, self.z > 0, self.z < self.n - 1)

        @when(inner)
        def _():
            def step(i, carry):
                way = jnp.where(self.z < self.n // 2, order, 1 - order)
                d = jnp.where(way == 0, self.n - 1 - i, i)

                @when(jnp.where(way == 0, d > self.z, d < self.z))
                def _():
                    value = self.arrived(way, d, p) + self.at(self.partial, d, p)[...].astype(F32)
                    self.at(self.sbuf, d, p)[...] = value.astype(BF16)
                    self.copy(way, d, p).start()

                return carry

            lax.fori_loop(0, self.n - 1, step, 0)

    def final(self, p, acc):
        acc[...] = self.at(self.partial, self.z, p)[...].astype(F32)
        for way, there in ((0, self.z > 0), (1, self.z < self.n - 1)):
            @when(there)
            def _():
                acc[...] += self.arrived(way, self.z, p)

    def drain(self, lo=0, hi=None):
        hi = self.pieces if hi is None else hi

        def step(t, carry):
            d, p = t // (hi - lo), lo + t % (hi - lo)

            @when(d != self.z)
            def _():
                self.copy(jnp.where(d > self.z, 0, 1), d, p).wait_send()

            return carry

        lax.fori_loop(0, self.n * (hi - lo), step, 0)


def rms_scale(values):
    return lax.rsqrt(jnp.mean(values * values, axis=-1, keepdims=True) + norm_eps)


def rms_back(grad_in, hat, scale_rows):
    return scale_rows * (grad_in - hat * jnp.mean(grad_in * hat, axis=-1, keepdims=True))


def rope(v, cos2, sin2):
    return v * cos2 + pltpu.roll(v, v.shape[-1] // 2, axis=1) * sin2


def chain(k, lo, hi, scat, gath, finish, n):
    def within(p):
        return both(p >= lo, p < hi)

    f = lo + k - 2

    @when(within(f))
    def _():
        finish(f)
        if gath is not None:
            gath.send(0, f)

    scat.pass_on(1, lo + k - 1, within(lo + k - 1))
    scat.pass_on(0, lo + k, within(lo + k))
    if gath is not None:
        for hop in range(1, n):
            gath.send(hop, f - hop, within(f - hop))


class Square:
    def __init__(self, stage, transit, recv, ssem, rsem):
        self.stage, self.transit, self.recv, self.ssem, self.rsem = stage, transit, recv, ssem, rsem
        w = lax.axis_index("wide")
        self.z = lax.axis_index("narrow")
        core, chip = w % 2, w // 2
        self.beside = 2 * (chip + 1 - 2 * (chip % 2)) + core
        self.below = 2 * (chip + 2 - 4 * (chip // 2)) + core
        self.far = 2 * (3 - chip) + core
        self.owners = (self.far, self.beside, self.below)

    def copy(self, m):
        N = self.transit.shape[1]
        h0, h1 = pl.ds(0, N // 2), pl.ds(N // 2, N // 2)
        block, half, there = ((0, h0, 0), (0, h1, 0), (1, h0, 1), (2, h1, 1), (2, h0, 2), (1, h1, 2))[m]
        to = (self.beside, self.below, self.beside, self.below, self.below, self.beside)[m]
        dst = self.transit.at[:, half] if there == 0 else self.recv.at[there - 1, :, half]
        return remote(self.stage.at[block, :, half], dst, self.ssem.at[m], self.rsem.at[m], to, self.z)

    def put(self, block):
        for m in ((0, 1), (2,), (3,))[block]:
            self.copy(m).start()

    def pass_on(self):
        N = self.transit.shape[1]
        for m, block, half in ((0, 2, pl.ds(0, N // 2)), (1, 1, pl.ds(N // 2, N // 2))):
            self.copy(m).wait_recv()
            value = self.stage[block, :, half].astype(F32) + self.transit[:, half].astype(F32)
            self.stage[block, :, half] = value.astype(BF16)
            self.copy(4 + m).start()

    def drain(self):
        for m in range(6):
            self.copy(m).wait_send()
        for m in range(2, 6):
            self.copy(m).wait_recv()


def for_arrived(gath, hop, body):
    z, n = gath.z, gath.n
    if hop == 0:
        body(z)
        return
    left = (z >= hop).astype(jnp.int32)
    right = (z + hop <= n - 1).astype(jnp.int32)

    def step(i, carry):
        use_left = both(left == 1, i == 0)
        body(jnp.where(use_left, z - hop, z + hop))
        return carry

    lax.fori_loop(0, left + right, step, 0)


def row_of(ref):
    return ref[...].astype(F32).reshape(1, ref.shape[0])


def front_kernel(n, C, S, HD, docs,
                 lens_ref, gain_ref, qg_ref, kg_ref, freq_ref, x_hbm, wq_hbm, wk_hbm, wv_hbm,
                 normed_out, q_out, k_out, qrot_out, krot_out, v_out, prob_out, mix_out, cos_out, sin_out,
                 x_ref, normed_ref, q_ref, k_ref, qrot_ref, krot_ref, v_ref, prob_ref, mix_ref, cos_ref, sin_ref,
                 wq, wk, wv, bias, ssem, rsem, wsem, osem):
    R, D = n * S, x_ref.shape[2]
    QC, KC = wq.shape[1], wk.shape[1]
    G = QC // KC
    KH = KC // HD
    loads = [pltpu.make_async_copy(a, b, wsem.at[i]) for i, (a, b) in enumerate(
        ((x_hbm, x_ref), (wq_hbm, wq), (wk_hbm, wk), (wv_hbm, wv)))]
    for load in loads:
        load.start()
    gain, qgain, kgain, freq = [row_of(v) for v in (gain_ref, qg_ref, kg_ref, freq_ref)]
    saved = ((q_ref, q_out), (k_ref, k_out), (qrot_ref, qrot_out), (krot_ref, krot_out), (v_ref, v_out),
             (prob_ref, prob_out), (mix_ref, mix_out), (cos_ref, cos_out), (sin_ref, sin_out), (normed_ref, normed_out))

    def saves(part):
        return [pltpu.make_async_copy(a.at[part], b.at[part], osem.at[i, part]) for i, (a, b) in enumerate(saved)]

    gath = Gather(n, C, S, normed_ref, ssem, rsem)
    z = gath.z
    loads[0].wait()
    for part in range(C):
        x = x_ref[part].astype(F32)
        normed_ref[part, rows_at(z, S)] = (x * rms_scale(x) * gain).astype(BF16)
    barrier(n)
    for p in range(gath.pieces):
        gath.send(0, p)
    for part in range(C):
        t = lax.broadcasted_iota(jnp.int32, (R, HD), 0)
        row = lax.broadcasted_iota(jnp.int32, (R, R), 0)
        col = lax.broadcasted_iota(jnp.int32, (R, R), 1)
        first = jnp.zeros((R, HD), jnp.int32)
        first_wide = jnp.zeros((R, R), jnp.int32)
        end = jnp.int32(0)
        for d in range(docs):
            end = end + lens_ref[part, d]
            first = jnp.where(t >= end, end, first)
            first_wide = jnp.where(row >= end, end, first_wide)
        angle = (t - first).astype(F32) * freq
        sign = jnp.where(lax.broadcasted_iota(jnp.int32, (R, HD), 1) < HD // 2, -1.0, 1.0)
        cos_ref[part] = jnp.cos(angle)
        sin_ref[part] = jnp.sin(angle) * sign
        bias[part] = jnp.where(both(col <= row, col >= first_wide), 0.0, masked_score)
    for load in loads[1:]:
        load.wait()

    def project(chunk, parts):
        rows = rows_at(chunk, S)
        lhs = jnp.concatenate([normed_ref[p, rows] for p in parts], axis=0)
        for w, out in ((wq, q_ref), (wk, k_ref), (wv, v_ref)):
            res = dot(lhs, w[...], 1, 0).astype(out.dtype)
            for i, p in enumerate(parts):
                out[p, rows] = res[i * S:(i + 1) * S]

    def attend(part):
        def heads(k, carry):
            cos2, sin2 = cos_ref[part], sin_ref[part]

            def turned(src, head_gain, col):
                raw = src[part, :, lanes(col, HD)]
                return rope(raw * rms_scale(raw) * head_gain, cos2, sin2).astype(BF16)

            kr = turned(k_ref, kgain, k)
            krot_ref[part, :, lanes(k, HD)] = kr
            for g in range(G):
                qr = turned(q_ref, qgain, k * G + g)
                qrot_ref[part, :, lanes(k * G + g, HD)] = qr
                s = dot(qr, kr, 1, 1) * HD ** (-0.5) + bias[part]
                ex = jnp.exp(s - jnp.max(s, axis=-1, keepdims=True))
                prob = ex / jnp.sum(ex, axis=-1, keepdims=True)
                prob_ref[part, k * G + g] = prob
                mix = dot(prob.astype(BF16), v_ref[part, :, lanes(k, HD)], 1, 0)
                mix_ref[part, :, lanes(k * G + g, HD)] = mix.astype(BF16)
            return carry

        lax.fori_loop(0, KH, heads, 0)

    for hop in range(n - 1):
        if hop > 0:
            for p in range(gath.pieces):
                gath.send(hop, p)
        for_arrived(gath, hop, lambda chunk: project(chunk, tuple(range(C))))
    for part in range(C):
        for h in range(HALVES):
            gath.send(n - 1, part * HALVES + h)
        for_arrived(gath, n - 1, lambda chunk: project(chunk, (part,)))
        attend(part)
        for save in saves(part):
            save.start()
    gath.drain()
    for part in range(C):
        for save in saves(part):
            save.wait()


def weight_block(A, B, sib_a, sib_b, cols):
    total = None
    for part in range(A.shape[0]):
        for term in (dot(A[part, :, cols], B[part], 0, 0), dot(sib_a(part), sib_b[part], 0, 0)):
            total = term if total is None else total + term
    return total


def middle_kernel(n, C, S, W, push, *refs):
    (gain_ref, x_hbm, cot_hbm_in, mix_hbm, wout_hbm, wgate_hbm, wup_hbm, wdown_hbm,
     middle_hbm, dmid_hbm, gaing_ref, dmix_hbm, db_hbm, mlp_hbm, out_hbm) = refs[:15]
    rest = list(refs[15:])
    if push:
        sib_n2, sib_cot, sib_act, sib_dg, sib_du, recv_down, recv_gate, blk_up, own_down, own_gate, own_up = rest[:11]
        rest = rest[11:]
    else:
        n2_hbm, cot_hbm, act_hbm, dg_hbm, du_hbm = rest[:5]
        rest = rest[5:]
    (x_ref, cot_ref, middle_ref, dmid_ref, out_ref, dmix_ref, mixv, wout, wgate, wup, wdown, cotf, n2f, dbf, partial, sbuf, rbuf, sbufm,
     dact, act, dg, du, acc, wsem, cs, cr, s1s, s1r, g2s, g2r, s2s, s2r, g3s, g3r, sms, smr, osem) = rest[:37]
    rest = rest[37:]
    if push:
        (stage_d, stage_g, stage_u, transit_d, transit_g, stage32, cols_sib, b_sib, sib_ss, sib_rs,
         down_ss, down_rs, gate_ss, gate_rs, lsem, ssem32) = rest
    R = n * S
    D = x_ref.shape[2]
    FC = wgate.shape[1]
    TN = 512
    nt, nd = FC // TN, D // TN
    P_ = C * HALVES
    rows = S // HALVES
    w, z = lax.axis_index("wide"), lax.axis_index("narrow")
    loads = [pltpu.make_async_copy(a, b, wsem.at[i]) for i, (a, b) in enumerate(
        ((mix_hbm, mixv), (wout_hbm, wout), (wdown_hbm, wdown), (wgate_hbm, wgate), (wup_hbm, wup), (cot_hbm_in, cot_ref),
         (x_hbm, x_ref)))]
    for index in (5, 0, 1, 6, 2, 3, 4):
        loads[index].start()
    gain = row_of(gain_ref)
    loads[5].wait()
    for part in range(C):
        cotf[part, rows_at(z, S)] = cot_ref[part]
    barrier(n, W if push else 0)
    gc = Gather(n, C, S, cotf, cs, cr)
    g2 = Gather(n, C, S, n2f, g2s, g2r)
    g3 = Gather(n, C, S, dbf, g3s, g3r)
    s1 = Scatter(n, C, S, partial, sbuf, rbuf, s1s, s1r)
    s2 = Scatter(n, C, S, partial, sbuf, rbuf, s2s, s2r)
    sm = Scatter(n, C, S, sbufm, sbufm, rbuf, sms, smr)
    loads[0].wait()
    loads[1].wait()
    loads[6].wait()

    def tiles(count, body):
        def step(j, carry):
            body(j)
            return carry

        lax.fori_loop(0, count, step, 0)

    for part in range(C):
        def out_tile(j):
            partial[part, :, lanes(j, TN)] = dot(mixv[part], wout[:, lanes(j, TN)], 1, 0)

        tiles(nd, out_tile)
        if part == 0:
            for p in range(2):
                s1.originate(p)
                gc.send(0, p)

    def mid_row(p):
        return p // HALVES, rows_at(p % HALVES, rows)

    def after_attention(p):
        s1.final(p, acc)
        part, rr = mid_row(p)
        middle = x_ref[part, rr].astype(F32) + acc[...]
        middle_ref[part, rr] = middle
        g2.at(n2f, z, p)[...] = (middle * rms_scale(middle) * gain).astype(BF16)

    def phase_one(k):
        @when(k + 2 < P_)
        def _():
            s1.originate(k + 2)
            gc.send(0, k + 2)

        chain(k, 0, P_, s1, g2, after_attention, n)
        for hop in range(1, n):
            gc.send(hop, k + 1 - hop, both(k + 1 - hop >= 0, k + 1 - hop < P_))

    def dact_tile(part, j):
        dact[:, lanes(j, TN)] = dot(cotf[part], wdown[rows_at(j, TN), :], 1, 1)

    first_in = HALVES + n + 1
    ready = HALVES + n - 3

    def early(k):
        phase_one(k)

        @when(k == ready - 1)
        def _():
            loads[2].wait()

        @when(both(k >= ready, k < ready + nt))
        def _():
            dact_tile(0, k - ready)

    tiles(first_in, early)
    for j in range(max(first_in - ready, 0), nt):
        dact_tile(0, j)
    loads[3].wait()
    loads[4].wait()
    late = P_ + n + 1 - first_in
    if push:
        core = w % 2
        mate = w + 1 - 2 * core

        def swap(index, src, dst, part):
            return remote(src.at[part], dst.at[part], sib_ss.at[index, part], sib_rs.at[index, part], mate, z)

    def after_feed(p):
        s2.final(p, acc)
        part, rr = mid_row(p)
        dn2 = acc[...]
        middle = middle_ref[part, rr]
        scale = rms_scale(middle)
        hat = middle * scale
        gaing_ref[...] += jnp.sum(dn2 * hat, axis=0, keepdims=True)
        dmid = cot_ref[part, rr].astype(F32) + rms_back(dn2 * gain, hat, scale)
        dmid_ref[part, rr] = dmid
        g3.at(dbf, z, p)[...] = dmid.astype(BF16)

    gaing_ref[...] = jnp.zeros_like(gaing_ref)
    steps = HALVES + n + 1

    def feed(part):
        def service(e):
            @when(both(part == 0, e % 2 == 1, e // 2 < late))
            def _():
                phase_one(first_in + e // 2)

            @when(both(part > 0, e < steps))
            def _():
                chain(e, 0, HALVES, s2, g3, after_feed, n)

        def gate_tile(j):
            @when(part > 0)
            def _():
                dact_tile(part, j)

            at = lanes(j, TN)
            gate = dot(n2f[part], wgate[:, at], 1, 0)
            up = dot(n2f[part], wup[:, at], 1, 0)
            sig = jax.nn.sigmoid(gate)
            silu = gate * sig
            d_act = dact[:, at]
            act[part, :, at] = (silu * up).astype(BF16)
            dg[part, :, at] = (d_act * up * sig * (1.0 + gate * (1.0 - sig))).astype(BF16)
            du[part, :, at] = (d_act * silu).astype(BF16)
            service(j)

        tiles(nt, gate_tile)
        if push:
            for index, (a, b) in enumerate(((n2f, sib_n2), (cotf, sib_cot), (act, sib_act), (dg, sib_dg), (du, sib_du))):
                swap(index, a, b, part).start()

        def back_tile(j):
            at = rows_at(j, TN)
            partial[part, :, lanes(j, TN)] = dot(dg[part], wgate[at, :], 1, 1) + dot(du[part], wup[at, :], 1, 1)
            service(nt + j)

        tiles(nd, back_tile)
        tiles(max(steps, 2 * late) - nt - nd, lambda e: service(nt + nd + e))

        @when(part == 0)
        def _():
            s1.drain()

        for h in range(HALVES):
            s2.originate(part * HALVES + h)

    tiles(C, feed)

    def tail(k):
        chain(k, HALVES, P_, s2, g3, after_feed, n)

    def mlp_sums(part):
        for j in range(nd):
            sbufm[part, :, lanes(j, TN)] = dot(act[part], wdown[:, lanes(j, TN)], 1, 0).astype(BF16)

    def mlp_step(k):
        chain(k, 0, HALVES, sm, None, mlp_done, n)

    def mlp_done(p):
        sm.final(p, acc)
        part, rr = mid_row(p)
        out_ref[part, rr] = middle_ref[part, rr] + acc[...]

    mlp_begun = 2

    def mlp_start():
        mlp_sums(0)
        for h in range(HALVES):
            sm.originate(h)

    def mix_back(part):
        dmix_ref[part] = dot(dbf[part], wout[...], 1, 1).astype(BF16)

    if push:
        width = D // W
        down = Square(stage_d, transit_d, recv_down, down_ss, down_rs)
        gate = Square(stage_g, transit_g, recv_gate, gate_ss, gate_rs)
        owners = down.owners

        def fetch(cols, b):
            copies = []
            if cols is not None:
                for q, owner in enumerate(owners + (w,)):
                    for part in range(C):
                        copies.append(pltpu.make_async_copy(
                            cols.at[part, :, lanes(owner, width)], cols_sib.at[q, part], lsem.at[0, q, part]))
            for part in range(C):
                copies.append(pltpu.make_async_copy(b.at[part], b_sib.at[part], lsem.at[1, 0, part]))
            for copy in copies:
                copy.start()
            for copy in copies:
                copy.wait()

        def block(A, B, q):
            return weight_block(A, B, lambda part: cols_sib[q, part], b_sib, lanes((owners + (w,))[q], width))

        def own_copy(dst, index):
            return pltpu.make_async_copy(stage32, dst, ssem32.at[index])

        def up_copy(q):
            return pltpu.make_async_copy(stage_u.at[q % 2], blk_up.at[q], osem.at[6 + q])

        def arrive(*pairs):
            for part in range(C):
                for index, dst in pairs:
                    swap(index, dst, dst, part).wait_recv()

        def down_block(q):
            if q == 0:
                arrive((1, sib_cot), (2, sib_act))
                fetch(sib_cot, sib_act)
            if q < 3:
                stage_d[q] = block(cotf, act, q).astype(BF16)
                down.put(q)
            else:
                stage32[...] = block(cotf, act, q)
                own_copy(own_down, 0).start()

        def gate_block(q):
            if q == 0:
                arrive((0, sib_n2), (3, sib_dg))
                fetch(sib_n2, sib_dg)
            if q < 3:
                stage_g[q] = block(n2f, dg, q).astype(BF16)
                gate.put(q)
            else:
                own_copy(own_down, 0).wait()
                stage32[...] = block(n2f, dg, q)
                own_copy(own_gate, 1).start()

        def up_block(q):
            if q == 0:
                arrive((4, sib_du))
                fetch(None, sib_du)
            if q < 3:
                if q == 2:
                    up_copy(0).wait()
                stage_u[q % 2] = block(n2f, du, q).astype(BF16)
                up_copy(q).start()
            else:
                own_copy(own_gate, 1).wait()
                stage32[...] = block(n2f, du, q)
                own_copy(own_up, 2).start()

        work = [[(down_block, 0), (down_block, 1)], [(down_block, 2), (down_block, 3)],
                [(gate_block, 0), (gate_block, 1)], [(gate_block, 2), (down.pass_on,)],
                [(gate_block, 3), (up_block, 0), (up_block, 1)], [(up_block, 2), (up_block, 3)],
                [(gate.pass_on,), (mlp_sums, 1), (mix_back, 0)]]
    else:
        outs = [pltpu.make_async_copy(a, b, osem.at[6 + i]) for i, (a, b) in enumerate(
            ((n2f, n2_hbm), (cotf, cot_hbm), (act, act_hbm), (dg, dg_hbm), (du, du_hbm)))]
        for out in outs:
            out.start()
        work = [[] for _ in range(steps - 1)] + [[(mlp_sums, 1), (mix_back, 0)]]
    work += [[]] * (steps - len(work))
    for k in range(steps):
        if k == mlp_begun - 1:
            mlp_start()
        tail(k)
        if k >= mlp_begun:
            mlp_step(k - mlp_begun)
        for piece in work[k]:
            piece[0](*piece[1:])
    for k in range(steps - mlp_begun, HALVES + 2):
        mlp_step(k)
    ends = [pltpu.make_async_copy(a, b, osem.at[i]) for i, (a, b) in enumerate(
        ((sbufm, mlp_hbm), (dbf, db_hbm), (middle_ref, middle_hbm), (dmid_ref, dmid_hbm), (out_ref, out_hbm), (dmix_ref, dmix_hbm)))]
    for end in ends[:5]:
        end.start()
    for part in range(1, C):
        mix_back(part)
    ends[5].start()
    gc.drain()
    g2.drain()
    g3.drain()
    s2.drain()
    sm.drain(0, HALVES)
    for end in ends:
        end.wait()
    if push:
        for part in range(C):
            for index, (a, b) in enumerate(((n2f, sib_n2), (cotf, sib_cot), (act, sib_act), (dg, sib_dg), (du, sib_du))):
                swap(index, a, b, part).wait_send()
        for q in (1, 2):
            up_copy(q).wait()
        own_copy(own_up, 2).wait()
        down.drain()
        gate.drain()
    else:
        for out in outs:
            out.wait()


def last_kernel(n, C, S, W, HD, push, *refs):
    gain_ref, qg_ref, kg_ref, gmlp_ref = refs[:4]
    sources = refs[4:20]
    rest = list(refs[20:])
    if push:
        mix_hbm, db_hbm, normed_hbm, blk_up = rest[:4]
        rest = rest[4:]
    out_hbm, in_hbm, ga_ref, gm_ref, gq_ref, gk_ref = rest[:6]
    rest = rest[6:]
    if push:
        recv_up, recv_out, recv_qkv, own_out, own_qkv = rest[:5]
        rest = rest[5:]
    else:
        dproj_hbm = rest[0]
        rest = rest[1:]
    held = rest[:18]
    (sbufm, q_ref, k_ref, qrot_ref, krot_ref, v_ref, prob_ref, cos_ref, sin_ref, dmix_ref, wq, wk, wv,
     middle_ref, dmid_ref, x_ref) = held[:16]
    out_ref, in_ref = held[16:18]
    rest = rest[18:]
    (dproj, partial, sbuf, rbuf, rbufm, acc, gains, small, small_two,
     lsem, s3s, s3r, sms, smr, gs1, gr1, gs2, gr2, osem) = rest[:19]
    rest = rest[19:]
    if push:
        (mixv, dbv, normv, sib_mix, sib_db, sib_norm, sib_dproj, sib_ss, sib_rs) = rest[:9]
        squares = rest[9:]
    R, D = n * S, x_ref.shape[2]
    QC, KC = wq.shape[1], wk.shape[1]
    G, KH = QC // KC, KC // HD
    TN = 512
    nd = D // TN
    P_ = C * HALVES
    rows = S // HALVES
    w, z = lax.axis_index("wide"), lax.axis_index("narrow")
    loads = [pltpu.make_async_copy(a, b, lsem.at[i]) for i, (a, b) in enumerate(zip(sources, held[:16]))]
    for load in loads:
        load.start()
    if push:
        extra = [pltpu.make_async_copy(a, b, lsem.at[16 + i]) for i, (a, b) in enumerate(
            ((mix_hbm, mixv), (db_hbm, dbv), (normed_hbm, normv)))]
        for load in extra:
            load.start()
    barrier(n, W)
    sm = Scatter(n, C, S, sbufm, sbufm, rbufm, sms, smr)
    s3 = Scatter(n, C, S, partial, sbuf, rbuf, s3s, s3r)
    if push:
        core = w % 2
        mate = w + 1 - 2 * core
        width = D // W
        up_sums, out_sums, qkv_sums = [
            Square(squares[i], squares[i + 1], recv, squares[i + 2], squares[i + 3])
            for i, recv in ((0, recv_up), (4, recv_out), (8, recv_qkv))]
        stage_up, stage_out, stage_qkv = squares[0], squares[4], squares[8]
        blocks = [pltpu.make_async_copy(blk_up.at[q], stage_up.at[q], lsem.at[19 + q]) for q in range(3)]
        for q in range(3):
            blocks[q].start()

        def swap(index, src, dst, part):
            return remote(src.at[part], dst.at[part], sib_ss.at[index, part], sib_rs.at[index, part], mate, z)

    loads[0].wait()
    for p in range(HALVES, P_):
        sm.originate(p)
    if push:
        for q in range(3):
            blocks[q].wait()
            up_sums.put(q)
        for load in extra:
            load.wait()
        for part in range(C):
            for index, (a, b) in enumerate(((mixv, sib_mix), (dbv, sib_db), (normv, sib_norm))):
                swap(index, a, b, part).start()

    def piece_row(p):
        return p // HALVES, rows_at(p % HALVES, rows)

    def mlp_done(p):
        sm.final(p, acc)
        part, rr = piece_row(p)
        out_ref[0, rr] = middle_ref[part, rr] + acc[...]

    gain, qgain, kgain = [row_of(v) for v in (gain_ref, qg_ref, kg_ref)]

    def grad_done(p):
        s3.final(p, acc)
        part, rr = piece_row(p)
        dn = acc[...]
        x = x_ref[part, rr].astype(F32)
        scale = rms_scale(x)
        hat = x * scale
        gains[0:1, :] += jnp.sum(dn * hat, axis=0, keepdims=True)
        in_ref[part, rr] = dmid_ref[part, rr] + rms_back(dn * gain, hat, scale)

    gains[...] = jnp.zeros_like(gains)
    scale = HD ** (-0.5)
    for load in loads[1:]:
        load.wait()

    def unit(part, k):
        cos2, sin2 = cos_ref[part], sin_ref[part]
        kr, vr = krot_ref[part, :, lanes(k, HD)], v_ref[part, :, lanes(k, HD)]

        def unturned(grad, raw, head_gain, at):
            d_n = grad * cos2 - pltpu.roll(grad, HD // 2, axis=1) * sin2
            r = rms_scale(raw)
            hat = raw * r
            gains[at:at + 1, :HD] += jnp.sum(d_n * hat, axis=0, keepdims=True)
            return rms_back(d_n * head_gain, hat, r).astype(BF16)

        dk, dv = None, None
        for g in range(G):
            h = k * G + g
            pr = prob_ref[part, h]
            dm = dmix_ref[part, :, lanes(h, HD)]
            dp = dot(dm, vr, 1, 1)
            one = dot(pr.astype(BF16), dm, 0, 0)
            dv = one if dv is None else dv + one
            ds = (pr * (dp - jnp.sum(pr * dp, axis=-1, keepdims=True))).astype(BF16)
            one = dot(ds, qrot_ref[part, :, lanes(h, HD)], 0, 0)
            dk = one if dk is None else dk + one
            dq = dot(ds, kr, 1, 0) * scale
            dproj[part, :, lanes(h, HD)] = unturned(dq, q_ref[part, :, lanes(h, HD)], qgain, 1)
        dproj[part, :, lanes(QC // HD + k, HD)] = unturned(dk * scale, k_ref[part, :, lanes(k, HD)], kgain, 2)
        dproj[part, :, lanes(QC // HD + KH + k, HD)] = dv.astype(BF16)

    per_part = KH + 1

    def between(e):
        chain(e, HALVES, P_, sm, None, mlp_done, n)
        chain(e - per_part, 0, HALVES, s3, None, grad_done, n)
        if push:
            @when(e == per_part)
            def _():
                up_sums.pass_on()

    def backward(part):
        def heads(k, carry):
            unit(part, k)
            between(part * per_part + k)
            return carry

        lax.fori_loop(0, KH, heads, 0)
        if push:
            swap(3, dproj, sib_dproj, part).start()

        def back_tile(j, carry):
            at = rows_at(j, TN)
            partial[part, :, lanes(j, TN)] = (
                dot(dproj[part, :, 0:QC], wq[at, :], 1, 1) + dot(dproj[part, :, QC:QC + KC], wk[at, :], 1, 1)
                + dot(dproj[part, :, QC + KC:QC + 2 * KC], wv[at, :], 1, 1))
            return carry

        lax.fori_loop(0, nd, back_tile, 0)
        for h in range(HALVES):
            s3.originate(part * HALVES + h)
        between(part * per_part + KH)

    def both_parts(part, carry):
        backward(part)
        return carry

    lax.fori_loop(0, C, both_parts, 0)
    done = C * per_part
    for e in range(done, max(HALVES + 2, per_part + HALVES + 2)):
        between(e)
    steps = HALVES + 2
    if push:
        def block(A, B, sib_a, sib_b, owner):
            cols = lanes(owner, width)
            return weight_block(A, B, lambda part: sib_a[part, :, cols], sib_b, cols)

        def out_block(q):
            if q == 0:
                for part in range(C):
                    for index, (a, b) in enumerate(((mixv, sib_mix), (dbv, sib_db), (normv, sib_norm), (dproj, sib_dproj))):
                        swap(index, a, b, part).wait_recv()
            if q < 3:
                stage_out[q] = block(dbv, mixv, sib_db, sib_mix, out_sums.owners[q]).astype(BF16)
                out_sums.put(q)
            else:
                own_out[...] = block(dbv, mixv, sib_db, sib_mix, w)

        def qkv_block(q):
            if q < 3:
                stage_qkv[q] = block(normv, dproj, sib_norm, sib_dproj, qkv_sums.owners[q]).astype(BF16)
                qkv_sums.put(q)
            else:
                own_qkv[...] = block(normv, dproj, sib_norm, sib_dproj, w)

        work = [[(out_block, 0), (qkv_block, 0)], [(qkv_block, 1), (qkv_block, 2)], [(out_block, 1), (out_block, 2)],
                [(qkv_block, 3), (out_block, 3), (qkv_sums.pass_on,), (out_sums.pass_on,)]]
        assert len(work) == steps
    else:
        work = [[]] * steps
    for k in range(steps):
        chain(k, HALVES, P_, s3, None, grad_done, n)
        for piece in work[k]:
            piece[0](*piece[1:])
    if not push:
        out = pltpu.make_async_copy(dproj, dproj_hbm, lsem.at[16])
        out.start()
    ends = [pltpu.make_async_copy(a, b, osem.at[i]) for i, (a, b) in enumerate(((out_ref, out_hbm), (in_ref, in_hbm)))]
    for end in ends:
        end.start()
    L = 2 * D + 2 * HD
    small[w, :, 0:D] = gains[0:1, :]
    small[w, :, D:2 * D] = gmlp_ref[...]
    small[w, :, 2 * D:2 * D + HD] = gains[1:2, :HD]
    small[w, :, 2 * D + HD:L] = gains[2:3, :HD]

    def to_wide(s):
        return remote(small.at[w], small.at[w], gs1.at[s], gr1.at[s], lax.rem(w + s, W), z)

    def to_narrow(s):
        return remote(small_two.at[z], small_two.at[z], gs2.at[s], gr2.at[s], w, lax.rem(z + s, n))

    for s in range(1, W):
        to_wide(s).start()
    for s in range(1, W):
        to_wide(s).wait_recv()
    total = small[0]
    for s in range(1, W):
        total = total + small[s]
    small_two[z] = total
    for s in range(1, n):
        to_narrow(s).start()
    for s in range(1, n):
        to_narrow(s).wait_recv()
    total = small_two[0]
    for s in range(1, n):
        total = total + small_two[s]
    for ref, lo, hi in ((ga_ref, 0, D), (gm_ref, D, 2 * D), (gq_ref, 2 * D, 2 * D + HD), (gk_ref, 2 * D + HD, L)):
        ref[...] = total[:, lo:hi].reshape(hi - lo)
    for s in range(1, W):
        to_wide(s).wait_send()
    for s in range(1, n):
        to_narrow(s).wait_send()
    sm.drain(HALVES, P_)
    s3.drain()
    for end in ends:
        end.wait()
    if push:
        for part in range(C):
            for index, (a, b) in enumerate(((mixv, sib_mix), (dbv, sib_db), (normv, sib_norm), (dproj, sib_dproj))):
                swap(index, a, b, part).wait_send()
        for sums in (up_sums, out_sums, qkv_sums):
            sums.drain()
    else:
        out.wait()


def finish_kernel(*refs):
    own_down, recv_down, own_out, recv_out, own_gate, recv_gate, own_up, recv_up, own_qkv, recv_qkv = refs[:10]
    low, high = refs[10:12]
    passed = refs[12:17]
    down, out_g, gate, up, g_q, g_k, g_v, out_ref = refs[17:25]
    out_ref[0], out_ref[1] = low[0], high[0]

    def total(own, parts):
        value = own[...]
        for i in range(parts.shape[0]):
            value = value + parts[i].astype(F32)
        return value

    down[...] = total(own_down, recv_down).T
    out_g[...] = total(own_out, recv_out).T
    gate[...] = total(own_gate, recv_gate)
    up[...] = total(own_up, recv_up)
    qkv = total(own_qkv, recv_qkv)
    first, second = g_q.shape[1], g_q.shape[1] + g_k.shape[1]
    g_q[...], g_k[...], g_v[...] = qkv[:, :first], qkv[:, first:second], qkv[:, second:]
    for a, b in zip(passed, refs[25:]):
        b[...] = a[...]


def local(W, layer_input, document_lengths, attn_gain, w_query, w_key, w_value, query_gain, key_gain, w_out, mlp_gain,
          w_gate, w_up, w_down, output_cotangent):
    n = lax.axis_size("narrow")
    C, _, S, D = layer_input.shape
    R = n * S
    T = C * R
    HD = query_gain.shape[0]
    QC, KC = w_query.shape[1], w_key.shape[1]
    QH = QC // HD
    FC = w_gate.shape[1]
    docs = document_lengths.shape[2]
    P_ = C * HALVES
    grid = 4
    push = (W == 8 and (D // W) % 128 == 0 and FC % (128 * grid) == 0 and QC % (128 * grid) == 0
            and S % (8 * grid) == 0)
    assert C == 2
    width = D // W
    x_own, cot_own = layer_input[:, 0], output_cotangent[:, 0]
    sds = jax.ShapeDtypeStruct
    dma = pltpu.SemaphoreType.DMA
    gsem = lambda: dma((2, n - 1, P_))
    half = np.arange(HD) % (HD // 2)
    freq = jnp.asarray(np.power(np.float32(1000000.0), np.float32(-2.0) * half.astype(np.float32) / np.float32(HD)), F32)
    vm = pl.BlockSpec(memory_space=pltpu.VMEM)
    hbm = pl.BlockSpec(memory_space=pl.ANY)
    smem = pl.BlockSpec(memory_space=pltpu.SMEM)
    VM = pltpu.VMEM

    shapes = [((C, R, D), BF16), ((C, R, QC), F32), ((C, R, KC), F32), ((C, R, QC), BF16), ((C, R, KC), BF16),
              ((C, R, KC), BF16), ((C, QH, R, R), F32), ((C, R, QC), BF16), ((C, R, HD), F32), ((C, R, HD), F32)]
    normed_full, q_raw, k_raw, q_rot, k_rot, v_rows, prob, mix, cos2, sin2 = pl.pallas_call(
        functools.partial(front_kernel, n, C, S, HD, docs), name="front",
        out_shape=[sds(*one) for one in shapes], in_specs=[smem, vm, vm, vm, vm, hbm, hbm, hbm, hbm], out_specs=[hbm] * 10,
        scratch_shapes=[VM((C, S, D), BF16)] + [VM(*one) for one in shapes]
        + [VM(w_query.shape, BF16), VM(w_key.shape, BF16), VM(w_value.shape, BF16),
           VM((C, R, R), F32), gsem(), gsem(), dma((4,)), dma((10, C))],
        compiler_params=pltpu.CompilerParams(collective_id=0, has_side_effects=True, vmem_limit_bytes=56 << 20),
    )(document_lengths[:, 0], attn_gain, query_gain, key_gain, freq, x_own, w_query, w_key, w_value)

    full, wide_rows = sds((C, R, D), BF16), sds((C, R, FC), BF16)
    outs = [sds((C, S, D), F32), sds((C, S, D), F32), sds((1, D), F32), sds((C, R, QC), BF16), full, full, sds((1, S, D), F32)]
    specs = [hbm, hbm, vm, hbm, hbm, hbm, hbm]
    line = lambda: [VM((C, R, D), BF16), VM((C, R + S, D), BF16)]
    scratch = (
        [VM((C, S, D), BF16), VM((C, S, D), BF16), VM((C, S, D), F32), VM((C, S, D), F32), VM((1, S, D), F32), VM((C, R, QC), BF16)]
        + [VM((C, R, QC), BF16), VM(w_out.shape, BF16), VM(w_gate.shape, BF16), VM(w_up.shape, BF16), VM(w_down.shape, BF16)]
        + [VM((C, R, D), BF16)] * 3 + [VM((C, R, D), F32)] + line()
        + [VM((C, R, D), BF16), VM((R, FC), F32)] + [VM((C, R, FC), BF16)] * 3 + [VM((S // HALVES, D), F32)]
        + [dma((7,)), gsem(), gsem(), dma((n, P_)), dma((2, n, P_)), gsem(), gsem(), dma((n, P_)), dma((2, n, P_)),
           gsem(), gsem(), dma((n, P_)), dma((2, n, P_)), dma((11,))]
    )
    if push:
        sums, own = sds((2, width, FC), BF16), sds((width, FC), F32)
        outs += [full, full, wide_rows, wide_rows, wide_rows, sums, sums, sds((3, width, FC), BF16), own, own, own]
        scratch += [VM((3, width, FC), BF16), VM((3, width, FC), BF16), VM((2, width, FC), BF16), VM((width, FC), BF16),
                    VM((width, FC), BF16), VM((width, FC), F32), VM((4, C, R, width), BF16), VM((C, R, FC), BF16),
                    dma((5, C)), dma((5, C)), dma((6,)), dma((6,)), dma((6,)), dma((6,)), dma((2, 4, C)), dma((3,))]
    else:
        outs += [full, full, wide_rows, wide_rows, wide_rows]
    res = pl.pallas_call(
        functools.partial(middle_kernel, n, C, S, W, push), name="middle", out_shape=outs,
        in_specs=[vm] + [hbm] * 7, out_specs=specs + [hbm] * (len(outs) - len(specs)), scratch_shapes=scratch,
        compiler_params=pltpu.CompilerParams(collective_id=1, has_side_effects=True, vmem_limit_bytes=63 << 20),
    )(mlp_gain, x_own, cot_own, mix, w_out, w_gate, w_up, w_down)
    middle, d_middle, gmlp, d_mix, db_full, mlp_sums, out_low = res[:7]

    args = [attn_gain, query_gain, key_gain, gmlp, mlp_sums, q_raw, k_raw, q_rot, k_rot, v_rows, prob, cos2, sin2, d_mix, w_query, w_key, w_value,
            middle, d_middle, x_own]
    in_specs = [vm] * 4 + [hbm] * 16
    held = [VM(v.shape, v.dtype) for v in args[4:]] + [VM((1, S, D), F32), VM((C, S, D), F32)]
    own_rows = sds((C, S, D), F32)
    outs = [sds((1, S, D), F32), own_rows, sds((D,), F32), sds((D,), F32), sds((HD,), F32), sds((HD,), F32)]
    specs = [hbm] * 2 + [vm] * 4
    PC = QC + 2 * KC
    L = 2 * D + 2 * HD
    scratch = (
        held + [VM((C, R, PC), BF16), VM((C, R, D), F32)]
        + line() + line()[1:] + [VM((S // HALVES, D), F32), VM((8, D), F32), VM((W, 1, L), F32), VM((n, 1, L), F32)]
        + [dma((22,)), dma((n, P_)), dma((2, n, P_)), dma((n, P_)), dma((2, n, P_)), dma((W,)), dma((W,)), dma((n,)), dma((n,)),
           dma((2,))]
    )
    if push:
        sib_n2, sib_cot, sib_act, sib_dg, sib_du, recv_down, recv_gate, blk_up, own_down, own_gate, own_up = res[7:]
        args += [mix, db_full, normed_full, blk_up]
        in_specs += [hbm] * 4
        outs += [sds((2, width, FC), BF16)] + [sds((2, width, QC), BF16), sds((2, width, PC), BF16),
                                                       sds((width, QC), F32), sds((width, PC), F32)]
        specs += [hbm] * 3 + [vm] * 2
        scratch += [VM((C, R, QC), BF16), VM((C, R, D), BF16), VM((C, R, D), BF16)]
        scratch += [VM((C, R, QC), BF16), VM((C, R, D), BF16), VM((C, R, D), BF16), VM((C, R, PC), BF16)]
        scratch += [dma((4, C)), dma((4, C))]
        for cols in (FC, QC, PC):
            scratch += [VM((3, width, cols), BF16), VM((width, cols), BF16), dma((6,)), dma((6,))]
    else:
        outs += [sds((C, R, PC), BF16)]
        specs += [hbm]
    last = pl.pallas_call(
        functools.partial(last_kernel, n, C, S, W, HD, push), name="last", out_shape=outs, in_specs=in_specs, out_specs=specs,
        scratch_shapes=scratch,
        compiler_params=pltpu.CompilerParams(collective_id=2, has_side_effects=True, vmem_limit_bytes=60 << 20),
    )(*args)
    out_high, in_own, g_attn, g_mlp, g_query, g_key = last[:6]
    if push:
        recv_up, recv_out, recv_qkv, own_out, own_qkv = last[6:]

        def by_rows(rows, cols, lead=None):
            if lead is None:
                return pl.BlockSpec((rows // grid, cols), lambda i: (i, 0))
            return pl.BlockSpec((lead, rows // grid, cols), lambda i: (0, i, 0))

        def by_cols(rows, cols, lead=None):
            if lead is None:
                return pl.BlockSpec((rows, cols // grid), lambda i: (0, i))
            return pl.BlockSpec((lead, rows, cols // grid), lambda i: (0, 0, i))

        def shard(parts):
            return pl.BlockSpec((parts, S // grid, D), lambda i: (0, i, 0))

        same = [shard(C)] + [pl.BlockSpec(v.shape, lambda i: (0,)) for v in last[2:6]]
        down, out_g, gate, up, g_q, g_k, g_v, out_own, in_own, g_attn, g_mlp, g_query, g_key = pl.pallas_call(
            finish_kernel, name="finish", grid=(grid,),
            out_shape=[sds((FC, width), F32), sds((QC, width), F32), sds((width, FC), F32), sds((width, FC), F32),
                       sds((width, QC), F32), sds((width, KC), F32), sds((width, KC), F32)]
            + [own_rows] + [sds(v.shape, v.dtype) for v in last[1:6]],
            in_specs=[by_cols(width, FC), by_cols(width, FC, 2), by_cols(width, QC), by_cols(width, QC, 2),
                      by_rows(width, FC), by_rows(width, FC, 2), by_rows(width, FC), by_rows(width, FC, 2),
                      by_rows(width, PC), by_rows(width, PC, 2), shard(1), shard(1)] + same,
            out_specs=[by_rows(FC, width), by_rows(QC, width), by_rows(width, FC), by_rows(width, FC), by_rows(width, QC),
                       by_rows(width, KC), by_rows(width, KC), shard(C)] + same,
            compiler_params=pltpu.CompilerParams(vmem_limit_bytes=62 << 20),
        )(own_down, recv_down, own_out, recv_out, own_gate, recv_gate, own_up, recv_up, own_qkv, recv_qkv, out_low, *last[:6])
        projections = (g_q, g_k, g_v)
    else:
        n2, cot, act, dg, du = [v.reshape(T, -1) for v in res[7:]]
        d_proj = last[6].reshape(T, PC)
        db, mixed, normed = db_full.reshape(T, D), mix.reshape(T, QC), normed_full.reshape(T, D)

        def scatter(a, b, dim):
            return lax.psum_scatter(dot(a, b, 0, 0).astype(BF16), "wide", scatter_dimension=dim, tiled=True).astype(F32)

        down, gate, up = scatter(act, cot, 1), scatter(n2, dg, 0), scatter(n2, du, 0)
        out_g, qkv = scatter(mixed, db, 1), scatter(normed, d_proj, 0)
        out_own = jnp.concatenate([out_low, out_high], axis=0)
        projections = (qkv[:, :QC], qkv[:, QC:QC + KC], qkv[:, QC + KC:])
    return (
        out_own[:, None], in_own[:, None], g_attn, *projections,
        g_query, g_key, out_g, g_mlp, gate, up, down,
    )


def solution(mesh):
    rows = P(None, "wide", "narrow", None)
    cols, tall = P(None, "narrow"), P("narrow", None)
    in_specs = (rows, P(None, "wide", None), P(), cols, cols, cols, P(), P(), tall, P(), cols, cols, tall, rows)
    both_ways, turned = P("wide", "narrow"), P("narrow", "wide")
    out_specs = (rows, rows, P(), both_ways, both_ways, both_ways, P(), P(), turned, P(), both_ways, both_ways, turned)
    body = functools.partial(local, mesh.shape["wide"])
    return jax.shard_map(body, mesh=mesh, in_specs=in_specs, out_specs=out_specs, check_vma=False)
```

```python
import functools

import jax
import jax.numpy as jnp
import numpy as np
from jax import lax
from jax.experimental import pallas as pl
from jax.experimental.pallas import tpu as pltpu
from jax.sharding import PartitionSpec as P

MESH = pl.DeviceIdType.MESH
F32 = jnp.float32
BF16 = jnp.bfloat16
norm_eps = 1e-06
masked_score = -1e30
HALVES = 2


def both(*conds):
    out = True
    for cond in conds:
        if isinstance(cond, bool):
            if not cond:
                return False
        else:
            out = cond if out is True else jnp.logical_and(out, cond)
    return out


def when(cond):
    if isinstance(cond, bool):
        return (lambda body: body()) if cond else (lambda body: None)
    return pl.when(cond)


def rows_at(index, rows):
    return pl.ds(pl.multiple_of(index * rows, rows), rows)


def lanes(index, width):
    return pl.ds(pl.multiple_of(index * width, width), width)


def dot(a, b, ca, cb):
    return lax.dot_general(a, b, (((ca,), (cb,)), ((), ())), preferred_element_type=F32)


def remote(src, dst, ssem, rsem, wide, narrow):
    return pltpu.make_async_remote_copy(
        src_ref=src, dst_ref=dst, send_sem=ssem, recv_sem=rsem, device_id=(wide, narrow), device_id_type=MESH
    )


def barrier(n, wide=0):
    w, z = lax.axis_index("wide"), lax.axis_index("narrow")
    bar = pltpu.get_barrier_semaphore()
    for step in range(1, n):
        pl.semaphore_signal(bar, inc=1, device_id=(w, lax.rem(z + step, n)), device_id_type=MESH)
    for step in range(1, wide):
        pl.semaphore_signal(bar, inc=1, device_id=(lax.rem(w + step, wide), z), device_id_type=MESH)
    pl.semaphore_wait(bar, n - 1 + max(wide - 1, 0))


class Line:
    def __init__(self, n, C, S):
        self.n, self.C, self.S = n, C, S
        self.pieces, self.rows = C * HALVES, S // HALVES
        self.w, self.z = lax.axis_index("wide"), lax.axis_index("narrow")

    def at(self, ref, chunk, p):
        start = chunk * self.S + (p % HALVES) * self.rows
        return ref.at[p // HALVES, pl.ds(pl.multiple_of(start, self.rows), self.rows)]


class Gather(Line):
    def __init__(self, n, C, S, full, ssem, rsem):
        super().__init__(n, C, S)
        self.full, self.ssem, self.rsem = full, ssem, rsem

    def copy(self, way, hop, p):
        chunk = self.z - hop if way == 0 else self.z + hop
        where = self.at(self.full, chunk, p)
        z_to = self.z + 1 if way == 0 else self.z - 1
        return remote(where, where, self.ssem.at[way, hop, p], self.rsem.at[way, hop, p], self.w, z_to)

    def arrival(self, way, hop, p):
        chunk = self.z - hop - 1 if way == 0 else self.z + hop + 1
        where = self.at(self.full, chunk, p)
        z_to = self.z + 1 if way == 0 else self.z - 1
        return remote(where, where, self.ssem.at[way, hop, p], self.rsem.at[way, hop, p], self.w, z_to)

    def has(self, way, hop):
        return self.z >= hop if way == 0 else self.z + hop <= self.n - 1

    def can_send(self, way, hop):
        edge = self.z < self.n - 1 if way == 0 else self.z > 0
        return both(self.has(way, hop), edge, hop < self.n - 1)

    def send(self, hop, p, ok=True):
        known = isinstance(hop, int)
        for way in (0, 1):
            if not (known and hop == 0):
                @when(both(ok, hop > 0, self.has(way, hop)))
                def _():
                    self.arrival(way, hop - 1, p).wait_recv()

            if not (known and hop >= self.n - 1):
                @when(both(ok, self.can_send(way, hop)))
                def _():
                    self.copy(way, hop, p).start()

    def drain(self):
        def step(t, carry):
            hop, p = t // self.pieces, t % self.pieces
            for way in (0, 1):
                @when(self.can_send(way, hop))
                def _():
                    self.copy(way, hop, p).wait_send()
            return carry

        lax.fori_loop(0, (self.n - 1) * self.pieces, step, 0)


class Scatter(Line):
    def __init__(self, n, C, S, partial, sbuf, rbuf, ssem, rsem):
        super().__init__(n, C, S)
        self.partial, self.sbuf, self.rbuf, self.ssem, self.rsem = partial, sbuf, rbuf, ssem, rsem

    def copy(self, way, d, p):
        z_to = self.z + 1 - 2 * way
        slot = jnp.where(both(way == 1, d == z_to), self.n, d)
        return remote(
            self.at(self.sbuf, d, p), self.at(self.rbuf, slot, p), self.ssem.at[d, p], self.rsem.at[way, d, p], self.w, z_to
        )

    def slot(self, way, d):
        return jnp.where(both(way == 1, d == self.z), self.n, d)

    def arrived(self, way, d, p):
        where = self.at(self.rbuf, self.slot(way, d), p)
        remote(where, where, self.ssem.at[d, p], self.rsem.at[way, d, p], self.w, self.z).wait_recv()
        return where[...].astype(F32)

    def originate(self, p):
        def step(i, carry):
            way = jnp.where(self.z == 0, 0, 1)
            d = jnp.where(self.z == 0, self.n - 1 - i, i)

            @when(jnp.logical_or(self.z == 0, self.z == self.n - 1))
            def _():
                if self.partial is not self.sbuf:
                    self.at(self.sbuf, d, p)[...] = self.at(self.partial, d, p)[...].astype(BF16)
                self.copy(way, d, p).start()

            return carry

        lax.fori_loop(0, self.n - 1, step, 0)

    def pass_on(self, order, p, ok=True):
        inner = both(ok, self.z > 0, self.z < self.n - 1)

        @when(inner)
        def _():
            def step(i, carry):
                way = jnp.where(self.z < self.n // 2, order, 1 - order)
                d = jnp.where(way == 0, self.n - 1 - i, i)

                @when(jnp.where(way == 0, d > self.z, d < self.z))
                def _():
                    value = self.arrived(way, d, p) + self.at(self.partial, d, p)[...].astype(F32)
                    self.at(self.sbuf, d, p)[...] = value.astype(BF16)
                    self.copy(way, d, p).start()

                return carry

            lax.fori_loop(0, self.n - 1, step, 0)

    def final(self, p, acc):
        acc[...] = self.at(self.partial, self.z, p)[...].astype(F32)
        for way, there in ((0, self.z > 0), (1, self.z < self.n - 1)):
            @when(there)
            def _():
                acc[...] += self.arrived(way, self.z, p)

    def drain(self, lo=0, hi=None):
        hi = self.pieces if hi is None else hi

        def step(t, carry):
            d, p = t // (hi - lo), lo + t % (hi - lo)

            @when(d != self.z)
            def _():
                self.copy(jnp.where(d > self.z, 0, 1), d, p).wait_send()

            return carry

        lax.fori_loop(0, self.n * (hi - lo), step, 0)


def rms_scale(values):
    return lax.rsqrt(jnp.mean(values * values, axis=-1, keepdims=True) + norm_eps)


def rms_back(grad_in, hat, scale_rows):
    return scale_rows * (grad_in - hat * jnp.mean(grad_in * hat, axis=-1, keepdims=True))


def rope(v, cos2, sin2):
    return v * cos2 + pltpu.roll(v, v.shape[-1] // 2, axis=1) * sin2


def chain(k, lo, hi, scat, gath, finish, n):
    def within(p):
        return both(p >= lo, p < hi)

    f = lo + k - 2

    @when(within(f))
    def _():
        finish(f)
        if gath is not None:
            gath.send(0, f)

    scat.pass_on(1, lo + k - 1, within(lo + k - 1))
    scat.pass_on(0, lo + k, within(lo + k))
    if gath is not None:
        for hop in range(n - 1, 0, -1):
            gath.send(hop, f - hop, within(f - hop))


class Square:
    def __init__(self, stage, transit, recv, ssem, rsem):
        self.stage, self.transit, self.recv, self.ssem, self.rsem = stage, transit, recv, ssem, rsem
        w = lax.axis_index("wide")
        self.z = lax.axis_index("narrow")
        core, chip = w % 2, w // 2
        self.beside = 2 * (chip + 1 - 2 * (chip % 2)) + core
        self.below = 2 * (chip + 2 - 4 * (chip // 2)) + core
        self.far = 2 * (3 - chip) + core
        self.owners = (self.far, self.beside, self.below)

    def copy(self, m):
        N = self.transit.shape[1]
        h0, h1 = pl.ds(0, N // 2), pl.ds(N // 2, N // 2)
        block, half, there = ((0, h0, 0), (0, h1, 0), (1, h0, 1), (2, h1, 1), (2, h0, 2), (1, h1, 2))[m]
        to = (self.beside, self.below, self.beside, self.below, self.below, self.beside)[m]
        dst = self.transit.at[:, half] if there == 0 else self.recv.at[there - 1, :, half]
        return remote(self.stage.at[block, :, half], dst, self.ssem.at[m], self.rsem.at[m], to, self.z)

    def put(self, block):
        for m in ((0, 1), (2,), (3,))[block]:
            self.copy(m).start()

    def pass_on(self):
        N = self.transit.shape[1]
        for m, block, half in ((0, 2, pl.ds(0, N // 2)), (1, 1, pl.ds(N // 2, N // 2))):
            self.copy(m).wait_recv()
            value = self.stage[block, :, half].astype(F32) + self.transit[:, half].astype(F32)
            self.stage[block, :, half] = value.astype(BF16)
            self.copy(4 + m).start()

    def drain(self):
        for m in range(6):
            self.copy(m).wait_send()
        for m in range(2, 6):
            self.copy(m).wait_recv()


def row_of(ref):
    return ref[...].astype(F32).reshape(1, ref.shape[0])


def weight_block(A, B, sib_a, sib_b, cols):
    total = None
    for part in range(A.shape[0]):
        for term in (dot(A[part, :, cols], B[part], 0, 0), dot(sib_a(part), sib_b[part], 0, 0)):
            total = term if total is None else total + term
    return total


def middle_kernel(n, C, S, W, HD, docs, push, *refs):
    (lens_ref, attn_gain_ref, qg_ref, kg_ref, freq_ref, gain_ref, x_hbm, cot_hbm_in, wq_hbm, wk_hbm, wv_hbm,
     wout_hbm, wgate_hbm, wup_hbm, wdown_hbm) = refs[:15]
    (raws_hbm, prob_hbm, rots_hbm, tabs_hbm, mix_hbm, normed_hbm,
     middle_hbm, dmid_hbm, gaing_ref, dmix_hbm, db_hbm, mlp_hbm, out_hbm) = refs[15:28]
    rest = list(refs[28:])
    if push:
        sib_n2, sib_cot, sib_act, sib_dg, sib_du, recv_down, recv_gate, blk_up, own_down, own_gate, own_up = rest[:11]
        rest = rest[11:]
    else:
        n2_hbm, cot_hbm, act_hbm, dg_hbm, du_hbm = rest[:5]
        rest = rest[5:]
    (x_ref, cot_ref, middle_ref, dmid_ref, out_ref, dmix_ref, mixv, wout, wgate, wup, wdown, cotf, n2f, dbf, partial, sbuf, rbuf, sbufm,
     dact, act, dg, du, acc, wsem, g1s, g1r, cs, cr, s1s, s1r, g2s, g2r, s2s, s2r, g3s, g3r, sms, smr, osem, vsem) = rest[:40]
    rest = rest[40:]
    if push:
        (stage_d, stage_g, stage_u, transit_d, transit_g, stage32, cols_sib, b_sib, sib_ss, sib_rs,
         down_ss, down_rs, gate_ss, gate_rs, lsem, ssem32) = rest
    R = n * S
    D = x_ref.shape[2]
    FC = wgate.shape[1]
    TN = 512
    nt, nd = FC // TN, D // TN
    P_ = C * HALVES
    rows = S // HALVES
    w, z = lax.axis_index("wide"), lax.axis_index("narrow")
    QC, KC = mixv.shape[2], wk_hbm.shape[1]
    QH, KH = QC // HD, KC // HD
    G = QH // KH
    PC = QC + 2 * KC
    table_lanes = C * 2 * HD
    assert table_lanes % R == 0 and table_lanes + C * R <= FC and PC <= FC
    assert D % R == 0 and QC + KC <= D - QH * R
    prob_at = D // R - QH

    def tiles(count, body):
        def step(j, carry):
            body(j)
            return carry

        lax.fori_loop(0, count, step, 0)

    loads = [pltpu.make_async_copy(a, b, wsem.at[i]) for i, (a, b) in enumerate(
        ((x_hbm, x_ref), (cot_hbm_in, cot_ref), (wq_hbm, wgate.at[:, 0:QC]), (wk_hbm, wgate.at[:, QC:QC + KC]),
         (wv_hbm, wgate.at[:, QC + KC:PC]), (wout_hbm, wout), (wdown_hbm, wdown), (wup_hbm, wup), (wgate_hbm, wgate)))]
    for load in loads[:8]:
        load.start()
    gain, again, qgain, kgain, freq = [row_of(v) for v in (gain_ref, attn_gain_ref, qg_ref, kg_ref, freq_ref)]
    loads[0].wait()
    for part in range(C):
        x = x_ref[part].astype(F32)
        dbf[part, rows_at(z, S)] = (x * rms_scale(x) * again).astype(BF16)
    barrier(n, W if push else 0)
    g1 = Gather(n, C, S, dbf, g1s, g1r)
    gc = Gather(n, C, S, cotf, cs, cr)
    g2 = Gather(n, C, S, n2f, g2s, g2r)
    g3 = Gather(n, C, S, dbf, g3s, g3r)
    s1 = Scatter(n, C, S, partial, sbuf, rbuf, s1s, s1r)
    s2 = Scatter(n, C, S, partial, sbuf, rbuf, s2s, s2r)
    sm = Scatter(n, C, S, sbufm, sbufm, rbuf, sms, smr)
    for p in range(2):
        g1.send(0, p)
    loads[1].wait()
    for part in range(C):
        cotf[part, rows_at(z, S)] = cot_ref[part]
    for part in range(C):
        t = lax.broadcasted_iota(jnp.int32, (R, HD), 0)
        row = lax.broadcasted_iota(jnp.int32, (R, R), 0)
        col = lax.broadcasted_iota(jnp.int32, (R, R), 1)
        first = jnp.zeros((R, HD), jnp.int32)
        first_wide = jnp.zeros((R, R), jnp.int32)
        end = jnp.int32(0)
        for d in range(docs):
            end = end + lens_ref[part, d]
            first = jnp.where(t >= end, end, first)
            first_wide = jnp.where(row >= end, end, first_wide)
        angle = (t - first).astype(F32) * freq
        sign = jnp.where(lax.broadcasted_iota(jnp.int32, (R, HD), 1) < HD // 2, -1.0, 1.0)
        dact[:, lanes(2 * part, HD)] = jnp.cos(angle)
        dact[:, lanes(2 * part + 1, HD)] = jnp.sin(angle) * sign
        dact[:, lanes(table_lanes // R + part, R)] = jnp.where(both(col <= row, col >= first_wide), 0.0, masked_score)

    cot_from = HALVES + n - 1

    def cot_low(t):
        @when(t == cot_from)
        def _():
            for p in range(HALVES):
                gc.send(0, p)

        for hop in range(n - 1, 0, -1):
            p = t - cot_from - 1 - hop
            gc.send(hop, p, both(p >= 0, p < HALVES))

    def first_step(t):
        for hop in range(n - 1, 0, -1):
            p = t - hop
            g1.send(hop, p, both(p >= 0, p < P_))

        @when(t + 1 < P_)
        def _():
            g1.send(0, t + 1)

        cot_low(t)

    half_in = HALVES + n - 2
    all_in = P_ + n - 2
    tiles(half_in, lambda i: first_step(i + 1))
    for load in loads[2:5]:
        load.wait()

    def project(part):
        lhs = dbf[part]
        partial[part, :, 0:QC + KC] = dot(lhs, wgate[:, 0:QC + KC], 1, 0)
        act[part, :, QC + KC:PC] = dot(lhs, wgate[:, QC + KC:PC], 1, 0).astype(BF16)

    def attend(part, k):
        cos2, sin2 = dact[:, lanes(2 * part, HD)], dact[:, lanes(2 * part + 1, HD)]

        def turned(index, head_gain):
            raw = partial[part, :, lanes(index, HD)]
            value = rope(raw * rms_scale(raw) * head_gain, cos2, sin2).astype(BF16)
            act[part, :, lanes(index, HD)] = value
            return value

        kr = turned(QH + k, kgain)
        for g in range(G):
            h = k * G + g
            qr = turned(h, qgain)
            s = dot(qr, kr, 1, 1) * HD ** (-0.5) + dact[:, lanes(table_lanes // R + part, R)]
            ex = jnp.exp(s - jnp.max(s, axis=-1, keepdims=True))
            prob = ex / jnp.sum(ex, axis=-1, keepdims=True)
            partial[part, :, lanes(prob_at + h, R)] = prob
            mix = dot(prob.astype(BF16), act[part, :, lanes(QH + KH + k, HD)], 1, 0)
            mixv[part, :, lanes(h, HD)] = mix.astype(BF16)

    def saves(part, lo=0, hi=6):
        return [pltpu.make_async_copy(a, b, vsem.at[i, part]) for i, (a, b) in list(enumerate((
            (partial.at[part, :, 0:QC + KC], raws_hbm.at[part]), (partial.at[part, :, prob_at * R:D], prob_hbm.at[part]),
            (act.at[part, :, 0:PC], rots_hbm.at[part]), (dact.at[:, lanes(part, 2 * HD)], tabs_hbm.at[part]),
            (mixv.at[part], mix_hbm.at[part]), (dbf.at[part], normed_hbm.at[part]))))[lo:hi]]

    def out_project(part):
        for save in saves(part, 0, 2):
            save.wait()

        def out_tile(j):
            partial[part, :, lanes(j, TN)] = dot(mixv[part], wout[:, lanes(j, TN)], 1, 0)

        tiles(nd, out_tile)
        for h in range(HALVES):
            s1.originate(part * HALVES + h)

    def mid_row(p):
        return p // HALVES, rows_at(p % HALVES, rows)

    def after_attention(p):
        s1.final(p, acc)
        part, rr = mid_row(p)
        middle = x_ref[part, rr].astype(F32) + acc[...]
        middle_ref[part, rr] = middle
        g2.at(n2f, z, p)[...] = (middle * rms_scale(middle) * gain).astype(BF16)

    def phase_one(k):
        chain(k, 0, P_, s1, g2, after_attention, n)
        cot_low(all_in + 1 + k)

    def cot_high(e):
        @when(e == 0)
        def _():
            for h in range(HALVES):
                gc.send(0, HALVES + h)

        step = jnp.where(e < 4, e - 1, e - 2)
        for hop in range(n - 1, 0, -1):
            p = HALVES + step - hop
            gc.send(hop, p, both(e != 4, step > 0, p >= HALVES, p < P_))

    def dact_tile(part, j):
        dact[:, lanes(j, TN)] = dot(cotf[part], wdown[rows_at(j, TN), :], 1, 1)

    project(0)
    for k in range(max(KH, all_in - half_in)):
        if half_in + 1 + k <= all_in:
            first_step(half_in + 1 + k)
        if k < KH:
            attend(0, k)
    for save in saves(0):
        save.start()
    project(1)
    loads[8].start()
    loads[5].wait()
    out_project(0)
    for k in range(KH):
        attend(1, k)
        if k == KH - 1:
            for save in saves(1):
                save.start()
        if k < 2:
            phase_one(k)
    for k in range(KH, 2):
        phase_one(k)
    out_project(1)
    first_in = HALVES + n + 1
    ready = max(2, cot_from + HALVES + n - 2 - all_in)
    loads[6].wait()
    for part in range(C):
        for save in saves(part, 2, 6):
            save.wait()

    def early(k):
        phase_one(2 + k)

        @when(both(2 + k >= ready, 2 + k < ready + nt))
        def _():
            dact_tile(0, 2 + k - ready)

    tiles(first_in - 2, early)
    for j in range(max(first_in - ready, 0), nt):
        dact_tile(0, j)
    loads[7].wait()
    loads[8].wait()
    g1.drain()
    late = P_ + n + 1 - first_in
    if push:
        core = w % 2
        mate = w + 1 - 2 * core

        def swap(index, src, dst, part):
            return remote(src.at[part], dst.at[part], sib_ss.at[index, part], sib_rs.at[index, part], mate, z)

    def after_feed(p):
        s2.final(p, acc)
        part, rr = mid_row(p)
        dn2 = acc[...]
        middle = middle_ref[part, rr]
        scale = rms_scale(middle)
        hat = middle * scale
        gaing_ref[...] += jnp.sum(dn2 * hat, axis=0, keepdims=True)
        dmid = cot_ref[part, rr].astype(F32) + rms_back(dn2 * gain, hat, scale)
        dmid_ref[part, rr] = dmid
        g3.at(dbf, z, p)[...] = dmid.astype(BF16)

    gaing_ref[...] = jnp.zeros_like(gaing_ref)
    early_steps = (2, 5)
    assert nt + nd == 7 and HALVES + n - 1 == 5 and late == 2

    def feed(part):
        def service(e):
            @when(both(part == 0, e % 2 == 1, e // 2 < late))
            def _():
                phase_one(first_in + e // 2)

            @when(part == 0)
            def _():
                cot_high(e)

            for step, at in enumerate(early_steps):
                @when(both(part > 0, e == at))
                def _():
                    chain(step, 0, P_, s2, g3, after_feed, n)

        def gate_tile(j):
            @when(part > 0)
            def _():
                dact_tile(part, j)

            at = lanes(j, TN)
            gate = dot(n2f[part], wgate[:, at], 1, 0)
            up = dot(n2f[part], wup[:, at], 1, 0)
            sig = jax.nn.sigmoid(gate)
            silu = gate * sig
            d_act = dact[:, at]
            act[part, :, at] = (silu * up).astype(BF16)
            dg[part, :, at] = (d_act * up * sig * (1.0 + gate * (1.0 - sig))).astype(BF16)
            du[part, :, at] = (d_act * silu).astype(BF16)
            service(j)

        tiles(nt, gate_tile)
        if push:
            for index, (a, b) in enumerate(((n2f, sib_n2), (cotf, sib_cot), (act, sib_act), (dg, sib_dg), (du, sib_du))):
                swap(index, a, b, part).start()

        def back_tile(j):
            at = rows_at(j, TN)
            partial[part, :, lanes(j, TN)] = dot(dg[part], wgate[at, :], 1, 1) + dot(du[part], wup[at, :], 1, 1)
            service(nt + j)

        tiles(nd, back_tile)
        @when(part == 0)
        def _():
            s1.drain()

        for h in range(HALVES):
            s2.originate(part * HALVES + h)

    tiles(C, feed)

    def tail(k):
        chain(k, 0, P_, s2, g3, after_feed, n)

    def mlp_sums(part):
        for j in range(nd):
            sbufm[part, :, lanes(j, TN)] = dot(act[part], wdown[:, lanes(j, TN)], 1, 0).astype(BF16)

    def mlp_step(k):
        chain(k, 0, HALVES, sm, None, mlp_done, n)

    def mlp_done(p):
        sm.final(p, acc)
        part, rr = mid_row(p)
        out_ref[part, rr] = middle_ref[part, rr] + acc[...]

    begin, steps = len(early_steps), P_ + n + 1
    mlp_begun = 5

    def mlp_start():
        mlp_sums(0)
        for h in range(HALVES):
            sm.originate(h)

    def mix_back(part):
        dmix_ref[part] = dot(dbf[part], wout[...], 1, 1).astype(BF16)

    if push:
        width = D // W
        down = Square(stage_d, transit_d, recv_down, down_ss, down_rs)
        gate = Square(stage_g, transit_g, recv_gate, gate_ss, gate_rs)
        owners = down.owners

        def fetch(cols, b):
            copies = []
            if cols is not None:
                for q, owner in enumerate(owners + (w,)):
                    for part in range(C):
                        copies.append(pltpu.make_async_copy(
                            cols.at[part, :, lanes(owner, width)], cols_sib.at[q, part], lsem.at[0, q, part]))
            for part in range(C):
                copies.append(pltpu.make_async_copy(b.at[part], b_sib.at[part], lsem.at[1, 0, part]))
            for copy in copies:
                copy.start()
            for copy in copies:
                copy.wait()

        def block(A, B, q):
            return weight_block(A, B, lambda part: cols_sib[q, part], b_sib, lanes((owners + (w,))[q], width))

        def own_copy(dst, index):
            return pltpu.make_async_copy(stage32, dst, ssem32.at[index])

        def up_copy(q):
            return pltpu.make_async_copy(stage_u.at[q % 2], blk_up.at[q], osem.at[6 + q])

        def arrive(*pairs):
            for part in range(C):
                for index, dst in pairs:
                    swap(index, dst, dst, part).wait_recv()

        def down_block(q):
            if q == 0:
                arrive((1, sib_cot), (2, sib_act))
                fetch(sib_cot, sib_act)
            if q < 3:
                stage_d[q] = block(cotf, act, q).astype(BF16)
                down.put(q)
            else:
                stage32[...] = block(cotf, act, q)
                own_copy(own_down, 0).start()

        def gate_block(q):
            if q == 0:
                arrive((0, sib_n2), (3, sib_dg))
                fetch(sib_n2, sib_dg)
            if q < 3:
                stage_g[q] = block(n2f, dg, q).astype(BF16)
                gate.put(q)
            else:
                own_copy(own_down, 0).wait()
                stage32[...] = block(n2f, dg, q)
                own_copy(own_gate, 1).start()

        def up_block(q):
            if q == 0:
                arrive((4, sib_du))
                fetch(None, sib_du)
            if q < 3:
                if q == 2:
                    up_copy(0).wait()
                stage_u[q % 2] = block(n2f, du, q).astype(BF16)
                up_copy(q).start()
            else:
                own_copy(own_gate, 1).wait()
                stage32[...] = block(n2f, du, q)
                own_copy(own_up, 2).start()

        work = [[(down_block, 0), (down_block, 1)], [(down_block, 2), (down_block, 3)],
                [(gate_block, 0), (gate_block, 1)], [(gate_block, 2), (down.pass_on,)],
                [(gate_block, 3), (up_block, 0), (up_block, 1)], [(up_block, 2), (gate.pass_on,), (mix_back, 0)],
                [(up_block, 3), (mlp_sums, 1)]]
    else:
        outs = [pltpu.make_async_copy(a, b, osem.at[6 + i]) for i, (a, b) in enumerate(
            ((n2f, n2_hbm), (cotf, cot_hbm), (act, act_hbm), (dg, dg_hbm), (du, du_hbm)))]
        for out in outs:
            out.start()
        work = [[] for _ in range(steps - begin - 1)] + [[(mlp_sums, 1), (mix_back, 0)]]
    assert len(work) == steps - begin
    for k in range(begin, steps):
        tail(k)
        if k == mlp_begun - 1:
            mlp_start()
        if k >= mlp_begun:
            mlp_step(k - mlp_begun)
        for piece in work[k - begin]:
            piece[0](*piece[1:])
    for k in range(steps - mlp_begun, HALVES + 2):
        mlp_step(k)
    ends = [pltpu.make_async_copy(a, b, osem.at[i]) for i, (a, b) in enumerate(
        ((sbufm, mlp_hbm), (dbf, db_hbm), (middle_ref, middle_hbm), (dmid_ref, dmid_hbm), (out_ref, out_hbm), (dmix_ref, dmix_hbm)))]
    for end in ends[:5]:
        end.start()
    for part in range(1, C):
        mix_back(part)
    ends[5].start()
    gc.drain()
    g2.drain()
    g3.drain()
    s2.drain()
    sm.drain(0, HALVES)
    for end in ends:
        end.wait()
    if push:
        for part in range(C):
            for index, (a, b) in enumerate(((n2f, sib_n2), (cotf, sib_cot), (act, sib_act), (dg, sib_dg), (du, sib_du))):
                swap(index, a, b, part).wait_send()
        for q in (1, 2):
            up_copy(q).wait()
        own_copy(own_up, 2).wait()
        down.drain()
        gate.drain()
    else:
        for out in outs:
            out.wait()


def last_kernel(n, C, S, W, HD, push, *refs):
    gain_ref, qg_ref, kg_ref, gmlp_ref = refs[:4]
    sources = refs[4:16]
    rest = list(refs[16:])
    if push:
        mix_hbm, db_hbm, normed_hbm, blk_up = rest[:4]
        rest = rest[4:]
    out_hbm, in_hbm, ga_ref, gm_ref, gq_ref, gk_ref = rest[:6]
    rest = rest[6:]
    if push:
        recv_up, recv_out, recv_qkv, own_out, own_qkv = rest[:5]
        rest = rest[5:]
    else:
        dproj_hbm = rest[0]
        rest = rest[1:]
    held = rest[:14]
    (sbufm, raws, rots, prob_ref, tabs, dmix_ref, wq, wk, wv, middle_ref, dmid_ref, x_ref) = held[:12]
    out_ref, in_ref = held[12:14]
    rest = rest[14:]
    (dproj, partial, sbuf, rbuf, rbufm, acc, gains, small, small_two,
     lsem, s3s, s3r, sms, smr, gs1, gr1, gs2, gr2, osem) = rest[:19]
    rest = rest[19:]
    if push:
        (mixv, dbv, normv, sib_mix, sib_db, sib_norm, sib_dproj, sib_ss, sib_rs) = rest[:9]
        squares = rest[9:]
    R, D = n * S, x_ref.shape[2]
    QC, KC = wq.shape[1], wk.shape[1]
    G, KH = QC // KC, KC // HD
    TN = 512
    nd = D // TN
    P_ = C * HALVES
    rows = S // HALVES
    w, z = lax.axis_index("wide"), lax.axis_index("narrow")
    loads = [pltpu.make_async_copy(a, b, lsem.at[i]) for i, (a, b) in enumerate(zip(sources, held[:12]))]
    for load in loads:
        load.start()
    if push:
        extra = [pltpu.make_async_copy(a, b, lsem.at[12 + i]) for i, (a, b) in enumerate(
            ((mix_hbm, mixv), (db_hbm, dbv), (normed_hbm, normv)))]
        for load in extra:
            load.start()
    barrier(n, W)
    sm = Scatter(n, C, S, sbufm, sbufm, rbufm, sms, smr)
    s3 = Scatter(n, C, S, partial, sbuf, rbuf, s3s, s3r)
    if push:
        core = w % 2
        mate = w + 1 - 2 * core
        width = D // W
        up_sums, out_sums, qkv_sums = [
            Square(squares[i], squares[i + 1], recv, squares[i + 2], squares[i + 3])
            for i, recv in ((0, recv_up), (4, recv_out), (8, recv_qkv))]
        stage_up, stage_out, stage_qkv = squares[0], squares[4], squares[8]
        blocks = [pltpu.make_async_copy(blk_up.at[q], stage_up.at[q], lsem.at[15 + q]) for q in range(3)]
        for q in range(3):
            blocks[q].start()

        def swap(index, src, dst, part):
            return remote(src.at[part], dst.at[part], sib_ss.at[index, part], sib_rs.at[index, part], mate, z)

    loads[0].wait()
    for p in range(HALVES, P_):
        sm.originate(p)
    if push:
        for q in range(3):
            blocks[q].wait()
            up_sums.put(q)
        for load in extra:
            load.wait()
        for part in range(C):
            for index, (a, b) in enumerate(((mixv, sib_mix), (dbv, sib_db), (normv, sib_norm))):
                swap(index, a, b, part).start()

    def piece_row(p):
        return p // HALVES, rows_at(p % HALVES, rows)

    def mlp_done(p):
        sm.final(p, acc)
        part, rr = piece_row(p)
        out_ref[0, rr] = middle_ref[part, rr] + acc[...]

    gain, qgain, kgain = [row_of(v) for v in (gain_ref, qg_ref, kg_ref)]

    def grad_done(p):
        s3.final(p, acc)
        part, rr = piece_row(p)
        dn = acc[...]
        x = x_ref[part, rr].astype(F32)
        scale = rms_scale(x)
        hat = x * scale
        gains[0:1, :] += jnp.sum(dn * hat, axis=0, keepdims=True)
        in_ref[part, rr] = dmid_ref[part, rr] + rms_back(dn * gain, hat, scale)

    gains[...] = jnp.zeros_like(gains)
    scale = HD ** (-0.5)
    for load in loads[1:]:
        load.wait()

    def unit(part, k):
        cos2, sin2 = tabs[part, :, 0:HD], tabs[part, :, HD:2 * HD]
        kr, vr = rots[part, :, lanes(QC // HD + k, HD)], rots[part, :, lanes(QC // HD + KH + k, HD)]

        def unturned(grad, raw, head_gain, at):
            d_n = grad * cos2 - pltpu.roll(grad, HD // 2, axis=1) * sin2
            r = rms_scale(raw)
            hat = raw * r
            gains[at:at + 1, :HD] += jnp.sum(d_n * hat, axis=0, keepdims=True)
            return rms_back(d_n * head_gain, hat, r).astype(BF16)

        dk, dv = None, None
        for g in range(G):
            h = k * G + g
            pr = prob_ref[part, :, lanes(h, R)]
            dm = dmix_ref[part, :, lanes(h, HD)]
            dp = dot(dm, vr, 1, 1)
            one = dot(pr.astype(BF16), dm, 0, 0)
            dv = one if dv is None else dv + one
            ds = (pr * (dp - jnp.sum(pr * dp, axis=-1, keepdims=True))).astype(BF16)
            one = dot(ds, rots[part, :, lanes(h, HD)], 0, 0)
            dk = one if dk is None else dk + one
            dq = dot(ds, kr, 1, 0) * scale
            dproj[part, :, lanes(h, HD)] = unturned(dq, raws[part, :, lanes(h, HD)], qgain, 1)
        dproj[part, :, lanes(QC // HD + k, HD)] = unturned(dk * scale, raws[part, :, lanes(QC // HD + k, HD)], kgain, 2)
        dproj[part, :, lanes(QC // HD + KH + k, HD)] = dv.astype(BF16)

    per_part = KH + 1

    def between(e):
        chain(e, HALVES, P_, sm, None, mlp_done, n)
        chain(e - per_part, 0, HALVES, s3, None, grad_done, n)
        if push:
            @when(e == per_part)
            def _():
                up_sums.pass_on()

    if push:
        def block(A, B, sib_a, sib_b, owner):
            cols = lanes(owner, width)
            return weight_block(A, B, lambda part: sib_a[part, :, cols], sib_b, cols)

        def arrive(*pairs):
            for part in range(C):
                for index, dst in pairs:
                    swap(index, dst, dst, part).wait_recv()

        def out_block(q):
            if q == 0:
                arrive((0, sib_mix), (1, sib_db))
            if q < 3:
                stage_out[q] = block(dbv, mixv, sib_db, sib_mix, out_sums.owners[q]).astype(BF16)
                out_sums.put(q)
            else:
                own_out[...] = block(dbv, mixv, sib_db, sib_mix, w)

        def qkv_block(q):
            if q == 0:
                arrive((2, sib_norm), (3, sib_dproj))
            if q < 3:
                stage_qkv[q] = block(normv, dproj, sib_norm, sib_dproj, qkv_sums.owners[q]).astype(BF16)
                qkv_sums.put(q)
            else:
                own_qkv[...] = block(normv, dproj, sib_norm, sib_dproj, w)

    def backward(part):
        def heads(k, carry):
            unit(part, k)
            between(part * per_part + k)
            return carry

        lax.fori_loop(0, KH, heads, 0)
        if push:
            swap(3, dproj, sib_dproj, part).start()

        def back_tile(j, carry):
            at = rows_at(j, TN)
            partial[part, :, lanes(j, TN)] = (
                dot(dproj[part, :, 0:QC], wq[at, :], 1, 1) + dot(dproj[part, :, QC:QC + KC], wk[at, :], 1, 1)
                + dot(dproj[part, :, QC + KC:QC + 2 * KC], wv[at, :], 1, 1))
            return carry

        lax.fori_loop(0, nd, back_tile, 0)
        for h in range(HALVES):
            s3.originate(part * HALVES + h)
        between(part * per_part + KH)
        if push:
            @when(part == 0)
            def _():
                for q in range(3):
                    out_block(q)

    def both_parts(part, carry):
        backward(part)
        return carry

    lax.fori_loop(0, C, both_parts, 0)
    done = C * per_part
    for e in range(done, max(HALVES + 2, per_part + HALVES + 2)):
        between(e)
    steps = HALVES + 2
    if push:
        work = [[(qkv_block, 0), (out_sums.pass_on,)], [(qkv_block, 1), (qkv_block, 2)], [(qkv_block, 3)],
                [(out_block, 3), (qkv_sums.pass_on,)]]
        assert len(work) == steps
    else:
        work = [[]] * steps
    for k in range(steps):
        chain(k, HALVES, P_, s3, None, grad_done, n)
        for piece in work[k]:
            piece[0](*piece[1:])
    if not push:
        out = pltpu.make_async_copy(dproj, dproj_hbm, lsem.at[16])
        out.start()
    ends = [pltpu.make_async_copy(a, b, osem.at[i]) for i, (a, b) in enumerate(((out_ref, out_hbm), (in_ref, in_hbm)))]
    for end in ends:
        end.start()
    L = 2 * D + 2 * HD
    small[w, :, 0:D] = gains[0:1, :]
    small[w, :, D:2 * D] = gmlp_ref[...]
    small[w, :, 2 * D:2 * D + HD] = gains[1:2, :HD]
    small[w, :, 2 * D + HD:L] = gains[2:3, :HD]

    def to_wide(s):
        return remote(small.at[w], small.at[w], gs1.at[s], gr1.at[s], lax.rem(w + s, W), z)

    def to_narrow(s):
        return remote(small_two.at[z], small_two.at[z], gs2.at[s], gr2.at[s], w, lax.rem(z + s, n))

    for s in range(1, W):
        to_wide(s).start()
    for s in range(1, W):
        to_wide(s).wait_recv()
    total = small[0]
    for s in range(1, W):
        total = total + small[s]
    small_two[z] = total
    for s in range(1, n):
        to_narrow(s).start()
    for s in range(1, n):
        to_narrow(s).wait_recv()
    total = small_two[0]
    for s in range(1, n):
        total = total + small_two[s]
    for ref, lo, hi in ((ga_ref, 0, D), (gm_ref, D, 2 * D), (gq_ref, 2 * D, 2 * D + HD), (gk_ref, 2 * D + HD, L)):
        ref[...] = total[:, lo:hi].reshape(hi - lo)
    for s in range(1, W):
        to_wide(s).wait_send()
    for s in range(1, n):
        to_narrow(s).wait_send()
    sm.drain(HALVES, P_)
    s3.drain()
    for end in ends:
        end.wait()
    if push:
        for part in range(C):
            for index, (a, b) in enumerate(((mixv, sib_mix), (dbv, sib_db), (normv, sib_norm), (dproj, sib_dproj))):
                swap(index, a, b, part).wait_send()
        for sums in (up_sums, out_sums, qkv_sums):
            sums.drain()
    else:
        out.wait()


def finish_kernel(*refs):
    own_down, recv_down, own_out, recv_out, own_gate, recv_gate, own_up, recv_up, own_qkv, recv_qkv = refs[:10]
    low, high = refs[10:12]
    passed = refs[12:17]
    down, out_g, gate, up, g_q, g_k, g_v, out_ref = refs[17:25]
    out_ref[0], out_ref[1] = low[0], high[0]

    def total(own, parts):
        value = own[...]
        for i in range(parts.shape[0]):
            value = value + parts[i].astype(F32)
        return value

    down[...] = total(own_down, recv_down).T
    out_g[...] = total(own_out, recv_out).T
    gate[...] = total(own_gate, recv_gate)
    up[...] = total(own_up, recv_up)
    qkv = total(own_qkv, recv_qkv)
    first, second = g_q.shape[1], g_q.shape[1] + g_k.shape[1]
    g_q[...], g_k[...], g_v[...] = qkv[:, :first], qkv[:, first:second], qkv[:, second:]
    for a, b in zip(passed, refs[25:]):
        b[...] = a[...]


def local(W, layer_input, document_lengths, attn_gain, w_query, w_key, w_value, query_gain, key_gain, w_out, mlp_gain,
          w_gate, w_up, w_down, output_cotangent):
    n = lax.axis_size("narrow")
    C, _, S, D = layer_input.shape
    R = n * S
    T = C * R
    HD = query_gain.shape[0]
    QC, KC = w_query.shape[1], w_key.shape[1]
    QH = QC // HD
    FC = w_gate.shape[1]
    docs = document_lengths.shape[2]
    P_ = C * HALVES
    grid = 4
    push = (W == 8 and (D // W) % 128 == 0 and FC % (128 * grid) == 0 and QC % (128 * grid) == 0
            and S % (8 * grid) == 0)
    assert C == 2
    width = D // W
    x_own, cot_own = layer_input[:, 0], output_cotangent[:, 0]
    sds = jax.ShapeDtypeStruct
    dma = pltpu.SemaphoreType.DMA
    gsem = lambda: dma((2, n - 1, P_))
    half = np.arange(HD) % (HD // 2)
    freq = jnp.asarray(np.power(np.float32(1000000.0), np.float32(-2.0) * half.astype(np.float32) / np.float32(HD)), F32)
    vm = pl.BlockSpec(memory_space=pltpu.VMEM)
    hbm = pl.BlockSpec(memory_space=pl.ANY)
    smem = pl.BlockSpec(memory_space=pltpu.SMEM)
    VM = pltpu.VMEM

    PC = QC + 2 * KC
    full, wide_rows = sds((C, R, D), BF16), sds((C, R, FC), BF16)
    kept = [sds((C, R, QC + KC), F32), sds((C, R, QH * R), F32), sds((C, R, PC), BF16), sds((C, R, 2 * HD), F32),
            sds((C, R, QC), BF16), full]
    outs = kept + [sds((C, S, D), F32), sds((C, S, D), F32), sds((1, D), F32), sds((C, R, QC), BF16), full, full, sds((1, S, D), F32)]
    specs = [hbm] * 8 + [vm] + [hbm] * 4
    line = lambda: [VM((C, R, D), BF16), VM((C, R + S, D), BF16)]
    scratch = (
        [VM((C, S, D), BF16), VM((C, S, D), BF16), VM((C, S, D), F32), VM((C, S, D), F32), VM((1, S, D), F32), VM((C, R, QC), BF16)]
        + [VM((C, R, QC), BF16), VM(w_out.shape, BF16), VM(w_gate.shape, BF16), VM(w_up.shape, BF16), VM(w_down.shape, BF16)]
        + [VM((C, R, D), BF16)] * 3 + [VM((C, R, D), F32)] + line()
        + [VM((C, R, D), BF16), VM((R, FC), F32)] + [VM((C, R, FC), BF16)] * 3 + [VM((S // HALVES, D), F32)]
        + [dma((9,)), gsem(), gsem(), gsem(), gsem(), dma((n, P_)), dma((2, n, P_)), gsem(), gsem(), dma((n, P_)), dma((2, n, P_)),
           gsem(), gsem(), dma((n, P_)), dma((2, n, P_)), dma((11,)), dma((6, C))]
    )
    if push:
        sums, own = sds((2, width, FC), BF16), sds((width, FC), F32)
        outs += [full, full, wide_rows, wide_rows, wide_rows, sums, sums, sds((3, width, FC), BF16), own, own, own]
        scratch += [VM((3, width, FC), BF16), VM((3, width, FC), BF16), VM((2, width, FC), BF16), VM((width, FC), BF16),
                    VM((width, FC), BF16), VM((width, FC), F32), VM((4, C, R, width), BF16), VM((C, R, FC), BF16),
                    dma((5, C)), dma((5, C)), dma((6,)), dma((6,)), dma((6,)), dma((6,)), dma((2, 4, C)), dma((3,))]
    else:
        outs += [full, full, wide_rows, wide_rows, wide_rows]
    res = pl.pallas_call(
        functools.partial(middle_kernel, n, C, S, W, HD, docs, push), name="middle", out_shape=outs,
        in_specs=[smem] + [vm] * 5 + [hbm] * 9, out_specs=specs + [hbm] * (len(outs) - len(specs)), scratch_shapes=scratch,
        compiler_params=pltpu.CompilerParams(collective_id=0, has_side_effects=True, vmem_limit_bytes=63 << 20),
    )(document_lengths[:, 0], attn_gain, query_gain, key_gain, freq, mlp_gain, x_own, cot_own, w_query, w_key, w_value, w_out, w_gate, w_up, w_down)
    raws, prob, rots, tabs, mix, normed_full = res[:6]
    res = res[6:]
    middle, d_middle, gmlp, d_mix, db_full, mlp_sums, out_low = res[:7]

    args = [attn_gain, query_gain, key_gain, gmlp, mlp_sums, raws, rots, prob, tabs, d_mix, w_query, w_key, w_value,
            middle, d_middle, x_own]
    in_specs = [vm] * 4 + [hbm] * 12
    held = [VM(v.shape, v.dtype) for v in args[4:]] + [VM((1, S, D), F32), VM((C, S, D), F32)]
    own_rows = sds((C, S, D), F32)
    outs = [sds((1, S, D), F32), own_rows, sds((D,), F32), sds((D,), F32), sds((HD,), F32), sds((HD,), F32)]
    specs = [hbm] * 2 + [vm] * 4
    L = 2 * D + 2 * HD
    scratch = (
        held + [VM((C, R, PC), BF16), VM((C, R, D), F32)]
        + line() + line()[1:] + [VM((S // HALVES, D), F32), VM((8, D), F32), VM((W, 1, L), F32), VM((n, 1, L), F32)]
        + [dma((18,)), dma((n, P_)), dma((2, n, P_)), dma((n, P_)), dma((2, n, P_)), dma((W,)), dma((W,)), dma((n,)), dma((n,)),
           dma((2,))]
    )
    if push:
        sib_n2, sib_cot, sib_act, sib_dg, sib_du, recv_down, recv_gate, blk_up, own_down, own_gate, own_up = res[7:]
        args += [mix, db_full, normed_full, blk_up]
        in_specs += [hbm] * 4
        outs += [sds((2, width, FC), BF16)] + [sds((2, width, QC), BF16), sds((2, width, PC), BF16),
                                                       sds((width, QC), F32), sds((width, PC), F32)]
        specs += [hbm] * 3 + [vm] * 2
        scratch += [VM((C, R, QC), BF16), VM((C, R, D), BF16), VM((C, R, D), BF16)]
        scratch += [VM((C, R, QC), BF16), VM((C, R, D), BF16), VM((C, R, D), BF16), VM((C, R, PC), BF16)]
        scratch += [dma((4, C)), dma((4, C))]
        for cols in (FC, QC, PC):
            scratch += [VM((3, width, cols), BF16), VM((width, cols), BF16), dma((6,)), dma((6,))]
    else:
        outs += [sds((C, R, PC), BF16)]
        specs += [hbm]
    last = pl.pallas_call(
        functools.partial(last_kernel, n, C, S, W, HD, push), name="last", out_shape=outs, in_specs=in_specs, out_specs=specs,
        scratch_shapes=scratch,
        compiler_params=pltpu.CompilerParams(collective_id=1, has_side_effects=True, vmem_limit_bytes=60 << 20),
    )(*args)
    out_high, in_own, g_attn, g_mlp, g_query, g_key = last[:6]
    if push:
        recv_up, recv_out, recv_qkv, own_out, own_qkv = last[6:]

        def by_rows(rows, cols, lead=None):
            if lead is None:
                return pl.BlockSpec((rows // grid, cols), lambda i: (i, 0))
            return pl.BlockSpec((lead, rows // grid, cols), lambda i: (0, i, 0))

        def by_cols(rows, cols, lead=None):
            if lead is None:
                return pl.BlockSpec((rows, cols // grid), lambda i: (0, i))
            return pl.BlockSpec((lead, rows, cols // grid), lambda i: (0, 0, i))

        def shard(parts):
            return pl.BlockSpec((parts, S // grid, D), lambda i: (0, i, 0))

        same = [shard(C)] + [pl.BlockSpec(v.shape, lambda i: (0,)) for v in last[2:6]]
        down, out_g, gate, up, g_q, g_k, g_v, out_own, in_own, g_attn, g_mlp, g_query, g_key = pl.pallas_call(
            finish_kernel, name="finish", grid=(grid,),
            out_shape=[sds((FC, width), F32), sds((QC, width), F32), sds((width, FC), F32), sds((width, FC), F32),
                       sds((width, QC), F32), sds((width, KC), F32), sds((width, KC), F32)]
            + [own_rows] + [sds(v.shape, v.dtype) for v in last[1:6]],
            in_specs=[by_cols(width, FC), by_cols(width, FC, 2), by_cols(width, QC), by_cols(width, QC, 2),
                      by_rows(width, FC), by_rows(width, FC, 2), by_rows(width, FC), by_rows(width, FC, 2),
                      by_rows(width, PC), by_rows(width, PC, 2), shard(1), shard(1)] + same,
            out_specs=[by_rows(FC, width), by_rows(QC, width), by_rows(width, FC), by_rows(width, FC), by_rows(width, QC),
                       by_rows(width, KC), by_rows(width, KC), shard(C)] + same,
            compiler_params=pltpu.CompilerParams(vmem_limit_bytes=62 << 20),
        )(own_down, recv_down, own_out, recv_out, own_gate, recv_gate, own_up, recv_up, own_qkv, recv_qkv, out_low, *last[:6])
        projections = (g_q, g_k, g_v)
    else:
        n2, cot, act, dg, du = [v.reshape(T, -1) for v in res[7:]]
        d_proj = last[6].reshape(T, PC)
        db, mixed, normed = db_full.reshape(T, D), mix.reshape(T, QC), normed_full.reshape(T, D)

        def scatter(a, b, dim):
            return lax.psum_scatter(dot(a, b, 0, 0).astype(BF16), "wide", scatter_dimension=dim, tiled=True).astype(F32)

        down, gate, up = scatter(act, cot, 1), scatter(n2, dg, 0), scatter(n2, du, 0)
        out_g, qkv = scatter(mixed, db, 1), scatter(normed, d_proj, 0)
        out_own = jnp.concatenate([out_low, out_high], axis=0)
        projections = (qkv[:, :QC], qkv[:, QC:QC + KC], qkv[:, QC + KC:])
    return (
        out_own[:, None], in_own[:, None], g_attn, *projections,
        g_query, g_key, out_g, g_mlp, gate, up, down,
    )


def solution(mesh):
    rows = P(None, "wide", "narrow", None)
    cols, tall = P(None, "narrow"), P("narrow", None)
    in_specs = (rows, P(None, "wide", None), P(), cols, cols, cols, P(), P(), tall, P(), cols, cols, tall, rows)
    both_ways, turned = P("wide", "narrow"), P("narrow", "wide")
    out_specs = (rows, rows, P(), both_ways, both_ways, both_ways, P(), P(), turned, P(), both_ways, both_ways, turned)
    body = functools.partial(local, mesh.shape["wide"])
    return jax.shard_map(body, mesh=mesh, in_specs=in_specs, out_specs=out_specs, check_vma=False)
```

```python
import functools

import jax
import jax.numpy as jnp
import numpy as np
from jax import lax
from jax.experimental import pallas as pl
from jax.experimental.pallas import tpu as pltpu
from jax.sharding import PartitionSpec as P

MESH = pl.DeviceIdType.MESH
F32 = jnp.float32
BF16 = jnp.bfloat16
norm_eps = 1e-06
masked_score = -1e30
HALVES = 2


def both(*conds):
    out = True
    for cond in conds:
        if isinstance(cond, bool):
            if not cond:
                return False
        else:
            out = cond if out is True else jnp.logical_and(out, cond)
    return out


def when(cond):
    if isinstance(cond, bool):
        return (lambda body: body()) if cond else (lambda body: None)
    return pl.when(cond)


def rows_at(index, rows):
    return pl.ds(pl.multiple_of(index * rows, rows), rows)


def lanes(index, width):
    return pl.ds(pl.multiple_of(index * width, width), width)


def dot(a, b, ca, cb):
    return lax.dot_general(a, b, (((ca,), (cb,)), ((), ())), preferred_element_type=F32)


def remote(src, dst, ssem, rsem, wide, narrow):
    return pltpu.make_async_remote_copy(
        src_ref=src, dst_ref=dst, send_sem=ssem, recv_sem=rsem, device_id=(wide, narrow), device_id_type=MESH
    )


def barrier(n, wide=0):
    w, z = lax.axis_index("wide"), lax.axis_index("narrow")
    bar = pltpu.get_barrier_semaphore()
    for step in range(1, n):
        pl.semaphore_signal(bar, inc=1, device_id=(w, lax.rem(z + step, n)), device_id_type=MESH)
    for step in range(1, wide):
        pl.semaphore_signal(bar, inc=1, device_id=(lax.rem(w + step, wide), z), device_id_type=MESH)
    pl.semaphore_wait(bar, n - 1 + max(wide - 1, 0))


class Line:
    def __init__(self, n, C, S):
        self.n, self.C, self.S = n, C, S
        self.pieces, self.rows = C * HALVES, S // HALVES
        self.w, self.z = lax.axis_index("wide"), lax.axis_index("narrow")

    def at(self, ref, chunk, p):
        start = chunk * self.S + (p % HALVES) * self.rows
        return ref.at[p // HALVES, pl.ds(pl.multiple_of(start, self.rows), self.rows)]


class Gather(Line):
    def __init__(self, n, C, S, full, ssem, rsem):
        super().__init__(n, C, S)
        self.full, self.ssem, self.rsem = full, ssem, rsem

    def copy(self, way, hop, p):
        chunk = self.z - hop if way == 0 else self.z + hop
        where = self.at(self.full, chunk, p)
        z_to = self.z + 1 if way == 0 else self.z - 1
        return remote(where, where, self.ssem.at[way, hop, p], self.rsem.at[way, hop, p], self.w, z_to)

    def arrival(self, way, hop, p):
        chunk = self.z - hop - 1 if way == 0 else self.z + hop + 1
        where = self.at(self.full, chunk, p)
        z_to = self.z + 1 if way == 0 else self.z - 1
        return remote(where, where, self.ssem.at[way, hop, p], self.rsem.at[way, hop, p], self.w, z_to)

    def has(self, way, hop):
        return self.z >= hop if way == 0 else self.z + hop <= self.n - 1

    def can_send(self, way, hop):
        edge = self.z < self.n - 1 if way == 0 else self.z > 0
        return both(self.has(way, hop), edge, hop < self.n - 1)

    def send(self, hop, p, ok=True):
        known = isinstance(hop, int)
        for way in (0, 1):
            if not (known and hop == 0):
                @when(both(ok, hop > 0, self.has(way, hop)))
                def _():
                    self.arrival(way, hop - 1, p).wait_recv()

            if not (known and hop >= self.n - 1):
                @when(both(ok, self.can_send(way, hop)))
                def _():
                    self.copy(way, hop, p).start()

    def drain(self):
        def step(t, carry):
            hop, p = t // self.pieces, t % self.pieces
            for way in (0, 1):
                @when(self.can_send(way, hop))
                def _():
                    self.copy(way, hop, p).wait_send()
            return carry

        lax.fori_loop(0, (self.n - 1) * self.pieces, step, 0)


class Scatter(Line):
    def __init__(self, n, C, S, partial, sbuf, rbuf, ssem, rsem):
        super().__init__(n, C, S)
        self.partial, self.sbuf, self.rbuf, self.ssem, self.rsem = partial, sbuf, rbuf, ssem, rsem

    def copy(self, way, d, p):
        z_to = self.z + 1 - 2 * way
        slot = jnp.where(both(way == 1, d == z_to), self.n, d)
        return remote(
            self.at(self.sbuf, d, p), self.at(self.rbuf, slot, p), self.ssem.at[d, p], self.rsem.at[way, d, p], self.w, z_to
        )

    def slot(self, way, d):
        return jnp.where(both(way == 1, d == self.z), self.n, d)

    def arrived(self, way, d, p):
        where = self.at(self.rbuf, self.slot(way, d), p)
        remote(where, where, self.ssem.at[d, p], self.rsem.at[way, d, p], self.w, self.z).wait_recv()
        return where[...].astype(F32)

    def originate(self, p):
        def step(i, carry):
            way = jnp.where(self.z == 0, 0, 1)
            d = jnp.where(self.z == 0, self.n - 1 - i, i)

            @when(jnp.logical_or(self.z == 0, self.z == self.n - 1))
            def _():
                if self.partial is not self.sbuf:
                    self.at(self.sbuf, d, p)[...] = self.at(self.partial, d, p)[...].astype(BF16)
                self.copy(way, d, p).start()

            return carry

        lax.fori_loop(0, self.n - 1, step, 0)

    def pass_on(self, order, p, ok=True):
        inner = both(ok, self.z > 0, self.z < self.n - 1)

        @when(inner)
        def _():
            def step(i, carry):
                way = jnp.where(self.z < self.n // 2, order, 1 - order)
                d = jnp.where(way == 0, self.n - 1 - i, i)

                @when(jnp.where(way == 0, d > self.z, d < self.z))
                def _():
                    value = self.arrived(way, d, p) + self.at(self.partial, d, p)[...].astype(F32)
                    self.at(self.sbuf, d, p)[...] = value.astype(BF16)
                    self.copy(way, d, p).start()

                return carry

            lax.fori_loop(0, self.n - 1, step, 0)

    def final(self, p, acc):
        acc[...] = self.at(self.partial, self.z, p)[...].astype(F32)
        for way, there in ((0, self.z > 0), (1, self.z < self.n - 1)):
            @when(there)
            def _():
                acc[...] += self.arrived(way, self.z, p)

    def drain(self, lo=0, hi=None):
        hi = self.pieces if hi is None else hi

        def step(t, carry):
            d, p = t // (hi - lo), lo + t % (hi - lo)

            @when(d != self.z)
            def _():
                self.copy(jnp.where(d > self.z, 0, 1), d, p).wait_send()

            return carry

        lax.fori_loop(0, self.n * (hi - lo), step, 0)


def rms_scale(values):
    return lax.rsqrt(jnp.mean(values * values, axis=-1, keepdims=True) + norm_eps)


def rms_back(grad_in, hat, scale_rows):
    return scale_rows * (grad_in - hat * jnp.mean(grad_in * hat, axis=-1, keepdims=True))


def rope(v, cos2, sin2):
    return v * cos2 + pltpu.roll(v, v.shape[-1] // 2, axis=1) * sin2


def chain(k, lo, hi, scat, gath, finish, n):
    def within(p):
        return both(p >= lo, p < hi)

    f = lo + k - 2

    @when(within(f))
    def _():
        finish(f)
        if gath is not None:
            gath.send(0, f)

    scat.pass_on(1, lo + k - 1, within(lo + k - 1))
    scat.pass_on(0, lo + k, within(lo + k))
    if gath is not None:
        for hop in range(n - 1, 0, -1):
            gath.send(hop, f - hop, within(f - hop))


def staggered(k, starts, scat, gath, finish, n):
    ages = [(k - start, p) for p, start in enumerate(starts)]
    for age, p in ages:
        if age == 2:
            finish(p)
            if gath is not None:
                gath.send(0, p)
    for age, p in ages:
        if age == 1:
            scat.pass_on(1, p)
    for age, p in ages:
        if age == 0:
            scat.pass_on(0, p)
    if gath is not None:
        for age, p in ages:
            if 3 <= age <= n + 1:
                gath.send(age - 2, p)


class Square:
    def __init__(self, stage, transit, recv, ssem, rsem):
        self.stage, self.transit, self.recv, self.ssem, self.rsem = stage, transit, recv, ssem, rsem
        w = lax.axis_index("wide")
        self.z = lax.axis_index("narrow")
        core, chip = w % 2, w // 2
        self.beside = 2 * (chip + 1 - 2 * (chip % 2)) + core
        self.below = 2 * (chip + 2 - 4 * (chip // 2)) + core
        self.far = 2 * (3 - chip) + core
        self.owners = (self.far, self.beside, self.below)

    def copy(self, m):
        N = self.transit.shape[1]
        h0, h1 = pl.ds(0, N // 2), pl.ds(N // 2, N // 2)
        block, half, there = ((0, h0, 0), (0, h1, 0), (1, h0, 1), (2, h1, 1), (2, h0, 2), (1, h1, 2))[m]
        to = (self.beside, self.below, self.beside, self.below, self.below, self.beside)[m]
        dst = self.transit.at[:, half] if there == 0 else self.recv.at[there - 1, :, half]
        return remote(self.stage.at[block, :, half], dst, self.ssem.at[m], self.rsem.at[m], to, self.z)

    def put(self, block):
        for m in ((0, 1), (2,), (3,))[block]:
            self.copy(m).start()

    def pass_on(self):
        N = self.transit.shape[1]
        for m, block, half in ((0, 2, pl.ds(0, N // 2)), (1, 1, pl.ds(N // 2, N // 2))):
            self.copy(m).wait_recv()
            value = self.stage[block, :, half].astype(F32) + self.transit[:, half].astype(F32)
            self.stage[block, :, half] = value.astype(BF16)
            self.copy(4 + m).start()

    def drain(self):
        for m in range(6):
            self.copy(m).wait_send()
        for m in range(2, 6):
            self.copy(m).wait_recv()


def row_of(ref):
    return ref[...].astype(F32).reshape(1, ref.shape[0])


def weight_block(A, B, sib_a, sib_b, cols):
    total = None
    for part in range(A.shape[0]):
        for term in (dot(A[part, :, cols], B[part], 0, 0), dot(sib_a(part), sib_b[part], 0, 0)):
            total = term if total is None else total + term
    return total


PLAN = dict(
    branch_starts=(0, 1, 4, 5), back_starts=(0, 1, 4, 5),
    after=dict(
        start=(('input', 0), ('input', 1), ('input', 2), ('input', 3), ('cot0', 0)),
        out0=(('input', 4), ('input', 5), ('cot0', 1), ('cot0', 2)),
        attend10=(('branch', 0), ('branch', 1), ('branch', 2), ('cot0', 3)),
        attend11=(('branch', 3),),
        out1=(('cot0', 4), ('cot1', 0)),
        act=(('branch', 4), ('branch', 5), ('branch', 6)),
        feed01=(('cot1', 1),),
        feed03=(('branch', 7),),
        feed05=(('branch', 8), ('cot1', 2)),
        feed06=(('branch', 9), ('branch', 10), ('cot1', 3), ('cot1', 4)),
        feed10=(('back', 0),),
        feed11=(('back', 1), ('back', 2)),
        feed14=(('back', 3),),
        work4=(('back', 4),),
        work6=(('back', 5), ('back', 6)),
        work9=(('back', 7), ('mlp', 0)),
        work11=(('back', 8),),
        work12=(('mlp', 1),),
        work13=(('back', 9), ('back', 10), ('mlp', 2), ('mlp', 3), ('mlp', 4)),
    ),
)


def middle_kernel(n, C, S, W, HD, docs, push, *refs):
    (lens_ref, attn_gain_ref, qg_ref, kg_ref, freq_ref, gain_ref, x_hbm, cot_hbm_in, wq_hbm, wk_hbm, wv_hbm,
     wout_hbm, wgate_hbm, wup_hbm, wdown_hbm) = refs[:15]
    (raws_hbm, prob_hbm, rots_hbm, tabs_hbm, mix_hbm, normed_hbm,
     middle_hbm, dmid_hbm, gaing_ref, dmix_hbm, db_hbm, mlp_hbm, out_hbm) = refs[15:28]
    rest = list(refs[28:])
    if push:
        sib_n2, sib_cot, sib_act, sib_dg, sib_du, recv_down, recv_gate, blk_up, own_down, own_gate, own_up = rest[:11]
        rest = rest[11:]
    else:
        n2_hbm, cot_hbm, act_hbm, dg_hbm, du_hbm = rest[:5]
        rest = rest[5:]
    (x_ref, cot_ref, middle_ref, dmid_ref, out_ref, dmix_ref, mixv, wout, wgate, wup, wdown, cotf, n2f, dbf, partial, sbuf, rbuf, sbufm,
     dact, act, dg, du, acc, wsem, g1s, g1r, cs, cr, s1s, s1r, g2s, g2r, s2s, s2r, g3s, g3r, sms, smr, osem, vsem) = rest[:40]
    rest = rest[40:]
    if push:
        (stage_d, stage_g, stage_u, transit_d, transit_g, stage32, cols_sib, b_sib, sib_ss, sib_rs,
         down_ss, down_rs, gate_ss, gate_rs, lsem, ssem32) = rest
    R = n * S
    D = x_ref.shape[2]
    FC = wgate.shape[1]
    TN = 512
    nt, nd = FC // TN, D // TN
    P_ = C * HALVES
    rows = S // HALVES
    w, z = lax.axis_index("wide"), lax.axis_index("narrow")
    QC, KC = mixv.shape[2], wk_hbm.shape[1]
    QH, KH = QC // HD, KC // HD
    G = QH // KH
    PC = QC + 2 * KC
    table_lanes = C * 2 * HD
    assert table_lanes % R == 0 and table_lanes + C * R <= FC and PC <= FC
    assert D % R == 0 and QC + KC <= D - QH * R
    prob_at = D // R - QH

    def tiles(count, body):
        def step(j, carry):
            body(j)
            return carry

        lax.fori_loop(0, count, step, 0)

    loads = [pltpu.make_async_copy(a, b, wsem.at[i]) for i, (a, b) in enumerate(
        ((x_hbm, x_ref), (cot_hbm_in, cot_ref), (wq_hbm, wgate.at[:, 0:QC]), (wk_hbm, wgate.at[:, QC:QC + KC]),
         (wv_hbm, wgate.at[:, QC + KC:PC]), (wout_hbm, wout), (wdown_hbm, wdown), (wup_hbm, wup), (wgate_hbm, wgate)))]
    for load in loads[:8]:
        load.start()
    gain, again, qgain, kgain, freq = [row_of(v) for v in (gain_ref, attn_gain_ref, qg_ref, kg_ref, freq_ref)]
    loads[0].wait()
    for part in range(C):
        x = x_ref[part].astype(F32)
        dbf[part, rows_at(z, S)] = (x * rms_scale(x) * again).astype(BF16)
    barrier(n, W if push else 0)
    g1 = Gather(n, C, S, dbf, g1s, g1r)
    gc = Gather(n, C, S, cotf, cs, cr)
    g2 = Gather(n, C, S, n2f, g2s, g2r)
    g3 = Gather(n, C, S, dbf, g3s, g3r)
    s1 = Scatter(n, C, S, partial, sbuf, rbuf, s1s, s1r)
    s2 = Scatter(n, C, S, partial, sbuf, rbuf, s2s, s2r)
    sm = Scatter(n, C, S, sbufm, sbufm, rbuf, sms, smr)
    for p in range(2):
        g1.send(0, p)
    loads[1].wait()
    for part in range(C):
        cotf[part, rows_at(z, S)] = cot_ref[part]
    for part in range(C):
        t = lax.broadcasted_iota(jnp.int32, (R, HD), 0)
        row = lax.broadcasted_iota(jnp.int32, (R, R), 0)
        col = lax.broadcasted_iota(jnp.int32, (R, R), 1)
        first = jnp.zeros((R, HD), jnp.int32)
        first_wide = jnp.zeros((R, R), jnp.int32)
        end = jnp.int32(0)
        for d in range(docs):
            end = end + lens_ref[part, d]
            first = jnp.where(t >= end, end, first)
            first_wide = jnp.where(row >= end, end, first_wide)
        angle = (t - first).astype(F32) * freq
        sign = jnp.where(lax.broadcasted_iota(jnp.int32, (R, HD), 1) < HD // 2, -1.0, 1.0)
        dact[:, lanes(2 * part, HD)] = jnp.cos(angle)
        dact[:, lanes(2 * part + 1, HD)] = jnp.sin(angle) * sign
        dact[:, lanes(table_lanes // R + part, R)] = jnp.where(both(col <= row, col >= first_wide), 0.0, masked_score)

    def input_step(k):
        for hop in range(n - 1, 0, -1):
            if 0 <= k + 1 - hop < P_:
                g1.send(hop, k + 1 - hop)
        if k + 2 < P_:
            g1.send(0, k + 2)

    def cot_step(part, k):
        if k == 0:
            for h in range(HALVES):
                gc.send(0, part * HALVES + h)
        for hop in range(n - 1, 0, -1):
            if 0 <= k - hop < HALVES:
                gc.send(hop, part * HALVES + k - hop)

    def mlp_step(k):
        if k == 0:
            for j in range(nd):
                sbufm[0, :, lanes(j, TN)] = dot(act[0], wdown[:, lanes(j, TN)], 1, 0).astype(BF16)
            for h in range(HALVES):
                sm.originate(h)
        else:
            staggered(k - 1, tuple(range(HALVES)), sm, None, mlp_done, n)

    def mlp_done(p):
        sm.final(p, acc)
        part, rr = mid_row(p)
        out_ref[part, rr] = middle_ref[part, rr] + acc[...]

    steps = dict(
        input=input_step, cot0=functools.partial(cot_step, 0), cot1=functools.partial(cot_step, 1), mlp=mlp_step,
        branch=lambda k: staggered(k, PLAN["branch_starts"], s1, g2, after_attention, n),
        back=lambda k: staggered(k, PLAN["back_starts"], s2, g3, after_feed, n))
    assert (n, C, HALVES, KH, nt, nd) == (4, 2, 2, 2, 3, 4)

    def run(place):
        for kind, k in PLAN["after"].get(place, ()):
            steps[kind](k)

    run("start")
    for load in loads[2:5]:
        load.wait()

    def project(part):
        lhs = dbf[part]
        partial[part, :, 0:QC + KC] = dot(lhs, wgate[:, 0:QC + KC], 1, 0)
        act[part, :, QC + KC:PC] = dot(lhs, wgate[:, QC + KC:PC], 1, 0).astype(BF16)

    def attend(part, k):
        cos2, sin2 = dact[:, lanes(2 * part, HD)], dact[:, lanes(2 * part + 1, HD)]

        def turned(index, head_gain):
            raw = partial[part, :, lanes(index, HD)]
            value = rope(raw * rms_scale(raw) * head_gain, cos2, sin2).astype(BF16)
            act[part, :, lanes(index, HD)] = value
            return value

        kr = turned(QH + k, kgain)
        for g in range(G):
            h = k * G + g
            qr = turned(h, qgain)
            s = dot(qr, kr, 1, 1) * HD ** (-0.5) + dact[:, lanes(table_lanes // R + part, R)]
            ex = jnp.exp(s - jnp.max(s, axis=-1, keepdims=True))
            prob = ex / jnp.sum(ex, axis=-1, keepdims=True)
            partial[part, :, lanes(prob_at + h, R)] = prob
            mix = dot(prob.astype(BF16), act[part, :, lanes(QH + KH + k, HD)], 1, 0)
            mixv[part, :, lanes(h, HD)] = mix.astype(BF16)

    def saves(part, lo=0, hi=6):
        return [pltpu.make_async_copy(a, b, vsem.at[i, part]) for i, (a, b) in list(enumerate((
            (partial.at[part, :, 0:QC + KC], raws_hbm.at[part]), (partial.at[part, :, prob_at * R:D], prob_hbm.at[part]),
            (act.at[part, :, 0:PC], rots_hbm.at[part]), (dact.at[:, lanes(part, 2 * HD)], tabs_hbm.at[part]),
            (mixv.at[part], mix_hbm.at[part]), (dbf.at[part], normed_hbm.at[part]))))[lo:hi]]

    def out_project(part):
        if part == 0:
            loads[5].wait()
        for save in saves(part, 0, 2):
            save.wait()

        def out_tile(j):
            partial[part, :, lanes(j, TN)] = dot(mixv[part], wout[:, lanes(j, TN)], 1, 0)

        tiles(nd, out_tile)
        for h in range(HALVES):
            s1.originate(part * HALVES + h)

    def mid_row(p):
        return p // HALVES, rows_at(p % HALVES, rows)

    def after_attention(p):
        s1.final(p, acc)
        part, rr = mid_row(p)
        middle = x_ref[part, rr].astype(F32) + acc[...]
        middle_ref[part, rr] = middle
        g2.at(n2f, z, p)[...] = (middle * rms_scale(middle) * gain).astype(BF16)

    def dact_tile(part, j):
        dact[:, lanes(j, TN)] = dot(cotf[part], wdown[rows_at(j, TN), :], 1, 1)

    project(0)
    run("project0")
    for k in range(KH):
        attend(0, k)
        if k == KH - 1:
            for save in saves(0):
                save.start()
        run("attend0%d" % k)
    out_project(0)
    run("out0")
    project(1)
    loads[8].start()
    run("project1")
    for k in range(KH):
        attend(1, k)
        if k == KH - 1:
            for save in saves(1):
                save.start()
        run("attend1%d" % k)
    out_project(1)
    run("out1")
    loads[6].wait()
    for part in range(C):
        for save in saves(part, 2, 6):
            save.wait()
    tiles(nt, lambda j: dact_tile(0, j))
    run("act")
    loads[7].wait()
    loads[8].wait()
    g1.drain()
    if push:
        core = w % 2
        mate = w + 1 - 2 * core

        def swap(index, src, dst, part):
            return remote(src.at[part], dst.at[part], sib_ss.at[index, part], sib_rs.at[index, part], mate, z)

    def after_feed(p):
        s2.final(p, acc)
        part, rr = mid_row(p)
        dn2 = acc[...]
        middle = middle_ref[part, rr]
        scale = rms_scale(middle)
        hat = middle * scale
        gaing_ref[...] += jnp.sum(dn2 * hat, axis=0, keepdims=True)
        dmid = cot_ref[part, rr].astype(F32) + rms_back(dn2 * gain, hat, scale)
        dmid_ref[part, rr] = dmid
        g3.at(dbf, z, p)[...] = dmid.astype(BF16)

    gaing_ref[...] = jnp.zeros_like(gaing_ref)

    def feed(part):
        def service(e, only=range(nt + nd - 1)):
            for which in range(C):
                for at in only:
                    if "feed%d%d" % (which, at) in PLAN["after"]:
                        @when(both(part == which, e == at))
                        def _():
                            run("feed%d%d" % (which, at))

        def gate_tile(j):
            @when(part > 0)
            def _():
                dact_tile(part, j)

            at = lanes(j, TN)
            gate = dot(n2f[part], wgate[:, at], 1, 0)
            up = dot(n2f[part], wup[:, at], 1, 0)
            sig = jax.nn.sigmoid(gate)
            silu = gate * sig
            d_act = dact[:, at]
            act[part, :, at] = (silu * up).astype(BF16)
            dg[part, :, at] = (d_act * up * sig * (1.0 + gate * (1.0 - sig))).astype(BF16)
            du[part, :, at] = (d_act * silu).astype(BF16)
            service(j)

        tiles(nt, gate_tile)
        if push:
            for index, (a, b) in enumerate(((n2f, sib_n2), (cotf, sib_cot), (act, sib_act), (dg, sib_dg), (du, sib_du))):
                swap(index, a, b, part).start()

        def back_tile(j):
            at = rows_at(j, TN)
            partial[part, :, lanes(j, TN)] = dot(dg[part], wgate[at, :], 1, 1) + dot(du[part], wup[at, :], 1, 1)
            service(nt + j)

        tiles(nd, back_tile)
        @when(part == 0)
        def _():
            s1.drain()

        for h in range(HALVES):
            s2.originate(part * HALVES + h)
        service(nt + nd - 1, (nt + nd - 1,))

    tiles(C, feed)

    def mlp_sums(part):
        for j in range(nd):
            sbufm[part, :, lanes(j, TN)] = dot(act[part], wdown[:, lanes(j, TN)], 1, 0).astype(BF16)

    def mix_back(part):
        dmix_ref[part] = dot(dbf[part], wout[...], 1, 1).astype(BF16)

    if push:
        width = D // W
        down = Square(stage_d, transit_d, recv_down, down_ss, down_rs)
        gate = Square(stage_g, transit_g, recv_gate, gate_ss, gate_rs)
        owners = down.owners

        def fetch(cols, b):
            copies = []
            if cols is not None:
                for q, owner in enumerate(owners + (w,)):
                    for part in range(C):
                        copies.append(pltpu.make_async_copy(
                            cols.at[part, :, lanes(owner, width)], cols_sib.at[q, part], lsem.at[0, q, part]))
            for part in range(C):
                copies.append(pltpu.make_async_copy(b.at[part], b_sib.at[part], lsem.at[1, 0, part]))
            for copy in copies:
                copy.start()
            for copy in copies:
                copy.wait()

        def block(A, B, q):
            return weight_block(A, B, lambda part: cols_sib[q, part], b_sib, lanes((owners + (w,))[q], width))

        def own_copy(dst, index):
            return pltpu.make_async_copy(stage32, dst, ssem32.at[index])

        def up_copy(q):
            return pltpu.make_async_copy(stage_u.at[q % 2], blk_up.at[q], osem.at[6 + q])

        def arrive(*pairs):
            for part in range(C):
                for index, dst in pairs:
                    swap(index, dst, dst, part).wait_recv()

        def down_block(q):
            if q == 0:
                arrive((1, sib_cot), (2, sib_act))
                fetch(sib_cot, sib_act)
            if q < 3:
                stage_d[q] = block(cotf, act, q).astype(BF16)
                down.put(q)
            else:
                stage32[...] = block(cotf, act, q)
                own_copy(own_down, 0).start()

        def gate_block(q):
            if q == 0:
                arrive((0, sib_n2), (3, sib_dg))
                fetch(sib_n2, sib_dg)
            if q < 3:
                stage_g[q] = block(n2f, dg, q).astype(BF16)
                gate.put(q)
            else:
                own_copy(own_down, 0).wait()
                stage32[...] = block(n2f, dg, q)
                own_copy(own_gate, 1).start()

        def up_block(q):
            if q == 0:
                arrive((4, sib_du))
                fetch(None, sib_du)
            if q < 3:
                if q == 2:
                    up_copy(0).wait()
                stage_u[q % 2] = block(n2f, du, q).astype(BF16)
                up_copy(q).start()
            else:
                own_copy(own_gate, 1).wait()
                stage32[...] = block(n2f, du, q)
                own_copy(own_up, 2).start()

        work = [[(down_block, q)] for q in range(4)] + [[(gate_block, q)] for q in range(3)] + [
            [(down.pass_on,), (gate_block, 3)], [(up_block, 0)], [(up_block, 1)], [(gate.pass_on,), (up_block, 2)], [(up_block, 3)]]
    else:
        outs = [pltpu.make_async_copy(a, b, osem.at[6 + i]) for i, (a, b) in enumerate(
            ((n2f, n2_hbm), (cotf, cot_hbm), (act, act_hbm), (dg, dg_hbm), (du, du_hbm)))]
        for out in outs:
            out.start()
        work = [[] for _ in range(12)]
    work += [[(mlp_sums, 1)], [(mix_back, 0)]]
    for place, pieces in enumerate(work):
        for piece in pieces:
            piece[0](*piece[1:])
        run("work%d" % place)
    ends = [pltpu.make_async_copy(a, b, osem.at[i]) for i, (a, b) in enumerate(
        ((sbufm, mlp_hbm), (dbf, db_hbm), (middle_ref, middle_hbm), (dmid_ref, dmid_hbm), (out_ref, out_hbm), (dmix_ref, dmix_hbm)))]
    for end in ends[:5]:
        end.start()
    for part in range(1, C):
        mix_back(part)
    ends[5].start()
    gc.drain()
    g2.drain()
    g3.drain()
    s2.drain()
    sm.drain(0, HALVES)
    for end in ends:
        end.wait()
    if push:
        for part in range(C):
            for index, (a, b) in enumerate(((n2f, sib_n2), (cotf, sib_cot), (act, sib_act), (dg, sib_dg), (du, sib_du))):
                swap(index, a, b, part).wait_send()
        for q in (1, 2):
            up_copy(q).wait()
        own_copy(own_up, 2).wait()
        down.drain()
        gate.drain()
    else:
        for out in outs:
            out.wait()


def last_kernel(n, C, S, W, HD, push, *refs):
    gain_ref, qg_ref, kg_ref, gmlp_ref = refs[:4]
    sources = refs[4:16]
    rest = list(refs[16:])
    if push:
        mix_hbm, db_hbm, normed_hbm, blk_up = rest[:4]
        rest = rest[4:]
    out_hbm, in_hbm, ga_ref, gm_ref, gq_ref, gk_ref = rest[:6]
    rest = rest[6:]
    if push:
        recv_up, recv_out, recv_qkv, own_out, own_qkv = rest[:5]
        rest = rest[5:]
    else:
        dproj_hbm = rest[0]
        rest = rest[1:]
    held = rest[:14]
    (sbufm, raws, rots, prob_ref, tabs, dmix_ref, wq, wk, wv, middle_ref, dmid_ref, x_ref) = held[:12]
    out_ref, in_ref = held[12:14]
    rest = rest[14:]
    (dproj, partial, sbuf, rbuf, rbufm, acc, gains, small, small_two,
     lsem, s3s, s3r, sms, smr, gs1, gr1, gs2, gr2, osem) = rest[:19]
    rest = rest[19:]
    if push:
        (mixv, dbv, normv, sib_mix, sib_db, sib_norm, sib_dproj, sib_ss, sib_rs) = rest[:9]
        squares = rest[9:]
    R, D = n * S, x_ref.shape[2]
    QC, KC = wq.shape[1], wk.shape[1]
    G, KH = QC // KC, KC // HD
    TN = 512
    nd = D // TN
    P_ = C * HALVES
    rows = S // HALVES
    w, z = lax.axis_index("wide"), lax.axis_index("narrow")
    loads = [pltpu.make_async_copy(a, b, lsem.at[i]) for i, (a, b) in enumerate(zip(sources, held[:12]))]
    for load in loads:
        load.start()
    if push:
        extra = [pltpu.make_async_copy(a, b, lsem.at[12 + i]) for i, (a, b) in enumerate(
            ((mix_hbm, mixv), (db_hbm, dbv), (normed_hbm, normv)))]
        for load in extra:
            load.start()
    barrier(n, W)
    sm = Scatter(n, C, S, sbufm, sbufm, rbufm, sms, smr)
    s3 = Scatter(n, C, S, partial, sbuf, rbuf, s3s, s3r)
    if push:
        core = w % 2
        mate = w + 1 - 2 * core
        width = D // W
        up_sums, out_sums, qkv_sums = [
            Square(squares[i], squares[i + 1], recv, squares[i + 2], squares[i + 3])
            for i, recv in ((0, recv_up), (4, recv_out), (8, recv_qkv))]
        stage_up, stage_out, stage_qkv = squares[0], squares[4], squares[8]
        blocks = [pltpu.make_async_copy(blk_up.at[q], stage_up.at[q], lsem.at[15 + q]) for q in range(3)]
        for q in range(3):
            blocks[q].start()

        def swap(index, src, dst, part):
            return remote(src.at[part], dst.at[part], sib_ss.at[index, part], sib_rs.at[index, part], mate, z)

    loads[0].wait()
    for p in range(HALVES, P_):
        sm.originate(p)
    if push:
        for q in range(3):
            blocks[q].wait()
            up_sums.put(q)
        for load in extra:
            load.wait()
        for part in range(C):
            for index, (a, b) in enumerate(((mixv, sib_mix), (dbv, sib_db), (normv, sib_norm))):
                swap(index, a, b, part).start()

    def piece_row(p):
        return p // HALVES, rows_at(p % HALVES, rows)

    def mlp_done(p):
        sm.final(p, acc)
        part, rr = piece_row(p)
        out_ref[0, rr] = middle_ref[part, rr] + acc[...]

    gain, qgain, kgain = [row_of(v) for v in (gain_ref, qg_ref, kg_ref)]

    def grad_done(p):
        s3.final(p, acc)
        part, rr = piece_row(p)
        dn = acc[...]
        x = x_ref[part, rr].astype(F32)
        scale = rms_scale(x)
        hat = x * scale
        gains[0:1, :] += jnp.sum(dn * hat, axis=0, keepdims=True)
        in_ref[part, rr] = dmid_ref[part, rr] + rms_back(dn * gain, hat, scale)

    gains[...] = jnp.zeros_like(gains)
    scale = HD ** (-0.5)
    for load in loads[1:]:
        load.wait()

    def unit(part, k):
        cos2, sin2 = tabs[part, :, 0:HD], tabs[part, :, HD:2 * HD]
        kr, vr = rots[part, :, lanes(QC // HD + k, HD)], rots[part, :, lanes(QC // HD + KH + k, HD)]

        def unturned(grad, raw, head_gain, at):
            d_n = grad * cos2 - pltpu.roll(grad, HD // 2, axis=1) * sin2
            r = rms_scale(raw)
            hat = raw * r
            gains[at:at + 1, :HD] += jnp.sum(d_n * hat, axis=0, keepdims=True)
            return rms_back(d_n * head_gain, hat, r).astype(BF16)

        dk, dv = None, None
        for g in range(G):
            h = k * G + g
            pr = prob_ref[part, :, lanes(h, R)]
            dm = dmix_ref[part, :, lanes(h, HD)]
            dp = dot(dm, vr, 1, 1)
            one = dot(pr.astype(BF16), dm, 0, 0)
            dv = one if dv is None else dv + one
            ds = (pr * (dp - jnp.sum(pr * dp, axis=-1, keepdims=True))).astype(BF16)
            one = dot(ds, rots[part, :, lanes(h, HD)], 0, 0)
            dk = one if dk is None else dk + one
            dq = dot(ds, kr, 1, 0) * scale
            dproj[part, :, lanes(h, HD)] = unturned(dq, raws[part, :, lanes(h, HD)], qgain, 1)
        dproj[part, :, lanes(QC // HD + k, HD)] = unturned(dk * scale, raws[part, :, lanes(QC // HD + k, HD)], kgain, 2)
        dproj[part, :, lanes(QC // HD + KH + k, HD)] = dv.astype(BF16)

    per_part = KH + 1

    def between(e):
        chain(e, HALVES, P_, sm, None, mlp_done, n)
        chain(e - per_part, 0, HALVES, s3, None, grad_done, n)
        if push:
            @when(e == per_part)
            def _():
                up_sums.pass_on()

    if push:
        def block(A, B, sib_a, sib_b, owner):
            cols = lanes(owner, width)
            return weight_block(A, B, lambda part: sib_a[part, :, cols], sib_b, cols)

        def arrive(*pairs):
            for part in range(C):
                for index, dst in pairs:
                    swap(index, dst, dst, part).wait_recv()

        def out_block(q):
            if q == 0:
                arrive((0, sib_mix), (1, sib_db))
            if q < 3:
                stage_out[q] = block(dbv, mixv, sib_db, sib_mix, out_sums.owners[q]).astype(BF16)
                out_sums.put(q)
            else:
                own_out[...] = block(dbv, mixv, sib_db, sib_mix, w)

        def qkv_block(q):
            if q == 0:
                arrive((2, sib_norm), (3, sib_dproj))
            if q < 3:
                stage_qkv[q] = block(normv, dproj, sib_norm, sib_dproj, qkv_sums.owners[q]).astype(BF16)
                qkv_sums.put(q)
            else:
                own_qkv[...] = block(normv, dproj, sib_norm, sib_dproj, w)

    def backward(part):
        def heads(k, carry):
            unit(part, k)
            between(part * per_part + k)
            return carry

        lax.fori_loop(0, KH, heads, 0)
        if push:
            swap(3, dproj, sib_dproj, part).start()

        def back_tile(j, carry):
            at = rows_at(j, TN)
            partial[part, :, lanes(j, TN)] = (
                dot(dproj[part, :, 0:QC], wq[at, :], 1, 1) + dot(dproj[part, :, QC:QC + KC], wk[at, :], 1, 1)
                + dot(dproj[part, :, QC + KC:QC + 2 * KC], wv[at, :], 1, 1))
            return carry

        lax.fori_loop(0, nd, back_tile, 0)
        for h in range(HALVES):
            s3.originate(part * HALVES + h)
        between(part * per_part + KH)
        if push:
            @when(part == 0)
            def _():
                for q in range(3):
                    out_block(q)

    def both_parts(part, carry):
        backward(part)
        return carry

    lax.fori_loop(0, C, both_parts, 0)
    done = C * per_part
    for e in range(done, max(HALVES + 2, per_part + HALVES + 2)):
        between(e)
    steps = HALVES + 2
    if push:
        work = [[(qkv_block, 0), (out_sums.pass_on,)], [(qkv_block, 1), (qkv_block, 2)], [(qkv_block, 3)],
                [(out_block, 3), (qkv_sums.pass_on,)]]
        assert len(work) == steps
    else:
        work = [[]] * steps
    for k in range(steps):
        chain(k, HALVES, P_, s3, None, grad_done, n)
        for piece in work[k]:
            piece[0](*piece[1:])
    if not push:
        out = pltpu.make_async_copy(dproj, dproj_hbm, lsem.at[16])
        out.start()
    ends = [pltpu.make_async_copy(a, b, osem.at[i]) for i, (a, b) in enumerate(((out_ref, out_hbm), (in_ref, in_hbm)))]
    for end in ends:
        end.start()
    L = 2 * D + 2 * HD
    small[w, :, 0:D] = gains[0:1, :]
    small[w, :, D:2 * D] = gmlp_ref[...]
    small[w, :, 2 * D:2 * D + HD] = gains[1:2, :HD]
    small[w, :, 2 * D + HD:L] = gains[2:3, :HD]

    def to_wide(s):
        return remote(small.at[w], small.at[w], gs1.at[s], gr1.at[s], lax.rem(w + s, W), z)

    def to_narrow(s):
        return remote(small_two.at[z], small_two.at[z], gs2.at[s], gr2.at[s], w, lax.rem(z + s, n))

    for s in range(1, W):
        to_wide(s).start()
    for s in range(1, W):
        to_wide(s).wait_recv()
    total = small[0]
    for s in range(1, W):
        total = total + small[s]
    small_two[z] = total
    for s in range(1, n):
        to_narrow(s).start()
    for s in range(1, n):
        to_narrow(s).wait_recv()
    total = small_two[0]
    for s in range(1, n):
        total = total + small_two[s]
    for ref, lo, hi in ((ga_ref, 0, D), (gm_ref, D, 2 * D), (gq_ref, 2 * D, 2 * D + HD), (gk_ref, 2 * D + HD, L)):
        ref[...] = total[:, lo:hi].reshape(hi - lo)
    for s in range(1, W):
        to_wide(s).wait_send()
    for s in range(1, n):
        to_narrow(s).wait_send()
    sm.drain(HALVES, P_)
    s3.drain()
    for end in ends:
        end.wait()
    if push:
        for part in range(C):
            for index, (a, b) in enumerate(((mixv, sib_mix), (dbv, sib_db), (normv, sib_norm), (dproj, sib_dproj))):
                swap(index, a, b, part).wait_send()
        for sums in (up_sums, out_sums, qkv_sums):
            sums.drain()
    else:
        out.wait()


def finish_kernel(*refs):
    own_down, recv_down, own_out, recv_out, own_gate, recv_gate, own_up, recv_up, own_qkv, recv_qkv = refs[:10]
    low, high = refs[10:12]
    passed = refs[12:17]
    down, out_g, gate, up, g_q, g_k, g_v, out_ref = refs[17:25]
    out_ref[0], out_ref[1] = low[0], high[0]

    def total(own, parts):
        value = own[...]
        for i in range(parts.shape[0]):
            value = value + parts[i].astype(F32)
        return value

    down[...] = total(own_down, recv_down).T
    out_g[...] = total(own_out, recv_out).T
    gate[...] = total(own_gate, recv_gate)
    up[...] = total(own_up, recv_up)
    qkv = total(own_qkv, recv_qkv)
    first, second = g_q.shape[1], g_q.shape[1] + g_k.shape[1]
    g_q[...], g_k[...], g_v[...] = qkv[:, :first], qkv[:, first:second], qkv[:, second:]
    for a, b in zip(passed, refs[25:]):
        b[...] = a[...]


def local(W, layer_input, document_lengths, attn_gain, w_query, w_key, w_value, query_gain, key_gain, w_out, mlp_gain,
          w_gate, w_up, w_down, output_cotangent):
    n = lax.axis_size("narrow")
    C, _, S, D = layer_input.shape
    R = n * S
    T = C * R
    HD = query_gain.shape[0]
    QC, KC = w_query.shape[1], w_key.shape[1]
    QH = QC // HD
    FC = w_gate.shape[1]
    docs = document_lengths.shape[2]
    P_ = C * HALVES
    grid = 4
    push = (W == 8 and (D // W) % 128 == 0 and FC % (128 * grid) == 0 and QC % (128 * grid) == 0
            and S % (8 * grid) == 0)
    assert C == 2
    width = D // W
    x_own, cot_own = layer_input[:, 0], output_cotangent[:, 0]
    sds = jax.ShapeDtypeStruct
    dma = pltpu.SemaphoreType.DMA
    gsem = lambda: dma((2, n - 1, P_))
    half = np.arange(HD) % (HD // 2)
    freq = jnp.asarray(np.power(np.float32(1000000.0), np.float32(-2.0) * half.astype(np.float32) / np.float32(HD)), F32)
    vm = pl.BlockSpec(memory_space=pltpu.VMEM)
    hbm = pl.BlockSpec(memory_space=pl.ANY)
    smem = pl.BlockSpec(memory_space=pltpu.SMEM)
    VM = pltpu.VMEM

    PC = QC + 2 * KC
    full, wide_rows = sds((C, R, D), BF16), sds((C, R, FC), BF16)
    kept = [sds((C, R, QC + KC), F32), sds((C, R, QH * R), F32), sds((C, R, PC), BF16), sds((C, R, 2 * HD), F32),
            sds((C, R, QC), BF16), full]
    outs = kept + [sds((C, S, D), F32), sds((C, S, D), F32), sds((1, D), F32), sds((C, R, QC), BF16), full, full, sds((1, S, D), F32)]
    specs = [hbm] * 8 + [vm] + [hbm] * 4
    line = lambda: [VM((C, R, D), BF16), VM((C, R + S, D), BF16)]
    scratch = (
        [VM((C, S, D), BF16), VM((C, S, D), BF16), VM((C, S, D), F32), VM((C, S, D), F32), VM((1, S, D), F32), VM((C, R, QC), BF16)]
        + [VM((C, R, QC), BF16), VM(w_out.shape, BF16), VM(w_gate.shape, BF16), VM(w_up.shape, BF16), VM(w_down.shape, BF16)]
        + [VM((C, R, D), BF16)] * 3 + [VM((C, R, D), F32)] + line()
        + [VM((C, R, D), BF16), VM((R, FC), F32)] + [VM((C, R, FC), BF16)] * 3 + [VM((S // HALVES, D), F32)]
        + [dma((9,)), gsem(), gsem(), gsem(), gsem(), dma((n, P_)), dma((2, n, P_)), gsem(), gsem(), dma((n, P_)), dma((2, n, P_)),
           gsem(), gsem(), dma((n, P_)), dma((2, n, P_)), dma((11,)), dma((6, C))]
    )
    if push:
        sums, own = sds((2, width, FC), BF16), sds((width, FC), F32)
        outs += [full, full, wide_rows, wide_rows, wide_rows, sums, sums, sds((3, width, FC), BF16), own, own, own]
        scratch += [VM((3, width, FC), BF16), VM((3, width, FC), BF16), VM((2, width, FC), BF16), VM((width, FC), BF16),
                    VM((width, FC), BF16), VM((width, FC), F32), VM((4, C, R, width), BF16), VM((C, R, FC), BF16),
                    dma((5, C)), dma((5, C)), dma((6,)), dma((6,)), dma((6,)), dma((6,)), dma((2, 4, C)), dma((3,))]
    else:
        outs += [full, full, wide_rows, wide_rows, wide_rows]
    res = pl.pallas_call(
        functools.partial(middle_kernel, n, C, S, W, HD, docs, push), name="middle", out_shape=outs,
        in_specs=[smem] + [vm] * 5 + [hbm] * 9, out_specs=specs + [hbm] * (len(outs) - len(specs)), scratch_shapes=scratch,
        compiler_params=pltpu.CompilerParams(collective_id=0, has_side_effects=True, vmem_limit_bytes=63 << 20),
    )(document_lengths[:, 0], attn_gain, query_gain, key_gain, freq, mlp_gain, x_own, cot_own, w_query, w_key, w_value, w_out, w_gate, w_up, w_down)
    raws, prob, rots, tabs, mix, normed_full = res[:6]
    res = res[6:]
    middle, d_middle, gmlp, d_mix, db_full, mlp_sums, out_low = res[:7]

    args = [attn_gain, query_gain, key_gain, gmlp, mlp_sums, raws, rots, prob, tabs, d_mix, w_query, w_key, w_value,
            middle, d_middle, x_own]
    in_specs = [vm] * 4 + [hbm] * 12
    held = [VM(v.shape, v.dtype) for v in args[4:]] + [VM((1, S, D), F32), VM((C, S, D), F32)]
    own_rows = sds((C, S, D), F32)
    outs = [sds((1, S, D), F32), own_rows, sds((D,), F32), sds((D,), F32), sds((HD,), F32), sds((HD,), F32)]
    specs = [hbm] * 2 + [vm] * 4
    L = 2 * D + 2 * HD
    scratch = (
        held + [VM((C, R, PC), BF16), VM((C, R, D), F32)]
        + line() + line()[1:] + [VM((S // HALVES, D), F32), VM((8, D), F32), VM((W, 1, L), F32), VM((n, 1, L), F32)]
        + [dma((18,)), dma((n, P_)), dma((2, n, P_)), dma((n, P_)), dma((2, n, P_)), dma((W,)), dma((W,)), dma((n,)), dma((n,)),
           dma((2,))]
    )
    if push:
        sib_n2, sib_cot, sib_act, sib_dg, sib_du, recv_down, recv_gate, blk_up, own_down, own_gate, own_up = res[7:]
        args += [mix, db_full, normed_full, blk_up]
        in_specs += [hbm] * 4
        outs += [sds((2, width, FC), BF16)] + [sds((2, width, QC), BF16), sds((2, width, PC), BF16),
                                                       sds((width, QC), F32), sds((width, PC), F32)]
        specs += [hbm] * 3 + [vm] * 2
        scratch += [VM((C, R, QC), BF16), VM((C, R, D), BF16), VM((C, R, D), BF16)]
        scratch += [VM((C, R, QC), BF16), VM((C, R, D), BF16), VM((C, R, D), BF16), VM((C, R, PC), BF16)]
        scratch += [dma((4, C)), dma((4, C))]
        for cols in (FC, QC, PC):
            scratch += [VM((3, width, cols), BF16), VM((width, cols), BF16), dma((6,)), dma((6,))]
    else:
        outs += [sds((C, R, PC), BF16)]
        specs += [hbm]
    last = pl.pallas_call(
        functools.partial(last_kernel, n, C, S, W, HD, push), name="last", out_shape=outs, in_specs=in_specs, out_specs=specs,
        scratch_shapes=scratch,
        compiler_params=pltpu.CompilerParams(collective_id=1, has_side_effects=True, vmem_limit_bytes=60 << 20),
    )(*args)
    out_high, in_own, g_attn, g_mlp, g_query, g_key = last[:6]
    if push:
        recv_up, recv_out, recv_qkv, own_out, own_qkv = last[6:]

        def by_rows(rows, cols, lead=None):
            if lead is None:
                return pl.BlockSpec((rows // grid, cols), lambda i: (i, 0))
            return pl.BlockSpec((lead, rows // grid, cols), lambda i: (0, i, 0))

        def by_cols(rows, cols, lead=None):
            if lead is None:
                return pl.BlockSpec((rows, cols // grid), lambda i: (0, i))
            return pl.BlockSpec((lead, rows, cols // grid), lambda i: (0, 0, i))

        def shard(parts):
            return pl.BlockSpec((parts, S // grid, D), lambda i: (0, i, 0))

        same = [shard(C)] + [pl.BlockSpec(v.shape, lambda i: (0,)) for v in last[2:6]]
        down, out_g, gate, up, g_q, g_k, g_v, out_own, in_own, g_attn, g_mlp, g_query, g_key = pl.pallas_call(
            finish_kernel, name="finish", grid=(grid,),
            out_shape=[sds((FC, width), F32), sds((QC, width), F32), sds((width, FC), F32), sds((width, FC), F32),
                       sds((width, QC), F32), sds((width, KC), F32), sds((width, KC), F32)]
            + [own_rows] + [sds(v.shape, v.dtype) for v in last[1:6]],
            in_specs=[by_cols(width, FC), by_cols(width, FC, 2), by_cols(width, QC), by_cols(width, QC, 2),
                      by_rows(width, FC), by_rows(width, FC, 2), by_rows(width, FC), by_rows(width, FC, 2),
                      by_rows(width, PC), by_rows(width, PC, 2), shard(1), shard(1)] + same,
            out_specs=[by_rows(FC, width), by_rows(QC, width), by_rows(width, FC), by_rows(width, FC), by_rows(width, QC),
                       by_rows(width, KC), by_rows(width, KC), shard(C)] + same,
            compiler_params=pltpu.CompilerParams(vmem_limit_bytes=62 << 20),
        )(own_down, recv_down, own_out, recv_out, own_gate, recv_gate, own_up, recv_up, own_qkv, recv_qkv, out_low, *last[:6])
        projections = (g_q, g_k, g_v)
    else:
        n2, cot, act, dg, du = [v.reshape(T, -1) for v in res[7:]]
        d_proj = last[6].reshape(T, PC)
        db, mixed, normed = db_full.reshape(T, D), mix.reshape(T, QC), normed_full.reshape(T, D)

        def scatter(a, b, dim):
            return lax.psum_scatter(dot(a, b, 0, 0).astype(BF16), "wide", scatter_dimension=dim, tiled=True).astype(F32)

        down, gate, up = scatter(act, cot, 1), scatter(n2, dg, 0), scatter(n2, du, 0)
        out_g, qkv = scatter(mixed, db, 1), scatter(normed, d_proj, 0)
        out_own = jnp.concatenate([out_low, out_high], axis=0)
        projections = (qkv[:, :QC], qkv[:, QC:QC + KC], qkv[:, QC + KC:])
    return (
        out_own[:, None], in_own[:, None], g_attn, *projections,
        g_query, g_key, out_g, g_mlp, gate, up, down,
    )


def solution(mesh):
    rows = P(None, "wide", "narrow", None)
    cols, tall = P(None, "narrow"), P("narrow", None)
    in_specs = (rows, P(None, "wide", None), P(), cols, cols, cols, P(), P(), tall, P(), cols, cols, tall, rows)
    both_ways, turned = P("wide", "narrow"), P("narrow", "wide")
    out_specs = (rows, rows, P(), both_ways, both_ways, both_ways, P(), P(), turned, P(), both_ways, both_ways, turned)
    body = functools.partial(local, mesh.shape["wide"])
    return jax.shard_map(body, mesh=mesh, in_specs=in_specs, out_specs=out_specs, check_vma=False)
```

```python
import functools

import jax
import jax.numpy as jnp
import numpy as np
from jax import lax
from jax.experimental import pallas as pl
from jax.experimental.pallas import tpu as pltpu
from jax.sharding import PartitionSpec as P

MESH = pl.DeviceIdType.MESH
F32 = jnp.float32
BF16 = jnp.bfloat16
norm_eps = 1e-06
masked_score = -1e30
HALVES = 2


def both(*conds):
    out = True
    for cond in conds:
        if isinstance(cond, bool):
            if not cond:
                return False
        else:
            out = cond if out is True else jnp.logical_and(out, cond)
    return out


def when(cond):
    if isinstance(cond, bool):
        return (lambda body: body()) if cond else (lambda body: None)
    return pl.when(cond)


def rows_at(index, rows):
    return pl.ds(pl.multiple_of(index * rows, rows), rows)


def lanes(index, width):
    return pl.ds(pl.multiple_of(index * width, width), width)


def dot(a, b, ca, cb):
    return lax.dot_general(a, b, (((ca,), (cb,)), ((), ())), preferred_element_type=F32)


def remote(src, dst, ssem, rsem, wide, narrow):
    return pltpu.make_async_remote_copy(
        src_ref=src, dst_ref=dst, send_sem=ssem, recv_sem=rsem, device_id=(wide, narrow), device_id_type=MESH
    )


def barrier(n, wide=0):
    w, z = lax.axis_index("wide"), lax.axis_index("narrow")
    bar = pltpu.get_barrier_semaphore()
    for step in range(1, n):
        pl.semaphore_signal(bar, inc=1, device_id=(w, lax.rem(z + step, n)), device_id_type=MESH)
    for step in range(1, wide):
        pl.semaphore_signal(bar, inc=1, device_id=(lax.rem(w + step, wide), z), device_id_type=MESH)
    pl.semaphore_wait(bar, n - 1 + max(wide - 1, 0))


class Line:
    def __init__(self, n, C, S):
        self.n, self.C, self.S = n, C, S
        self.pieces, self.rows = C * HALVES, S // HALVES
        self.w, self.z = lax.axis_index("wide"), lax.axis_index("narrow")

    def at(self, ref, chunk, p):
        start = chunk * self.S + (p % HALVES) * self.rows
        return ref.at[p // HALVES, pl.ds(pl.multiple_of(start, self.rows), self.rows)]


class Gather(Line):
    def __init__(self, n, C, S, full, ssem, rsem):
        super().__init__(n, C, S)
        self.full, self.ssem, self.rsem = full, ssem, rsem

    def copy(self, way, hop, p):
        chunk = self.z - hop if way == 0 else self.z + hop
        where = self.at(self.full, chunk, p)
        z_to = self.z + 1 if way == 0 else self.z - 1
        return remote(where, where, self.ssem.at[way, hop, p], self.rsem.at[way, hop, p], self.w, z_to)

    def arrival(self, way, hop, p):
        chunk = self.z - hop - 1 if way == 0 else self.z + hop + 1
        where = self.at(self.full, chunk, p)
        z_to = self.z + 1 if way == 0 else self.z - 1
        return remote(where, where, self.ssem.at[way, hop, p], self.rsem.at[way, hop, p], self.w, z_to)

    def has(self, way, hop):
        return self.z >= hop if way == 0 else self.z + hop <= self.n - 1

    def can_send(self, way, hop):
        edge = self.z < self.n - 1 if way == 0 else self.z > 0
        return both(self.has(way, hop), edge, hop < self.n - 1)

    def send(self, hop, p, ok=True):
        known = isinstance(hop, int)
        for way in (0, 1):
            if not (known and hop == 0):
                @when(both(ok, hop > 0, self.has(way, hop)))
                def _():
                    self.arrival(way, hop - 1, p).wait_recv()

            if not (known and hop >= self.n - 1):
                @when(both(ok, self.can_send(way, hop)))
                def _():
                    self.copy(way, hop, p).start()

    def drain(self):
        def step(t, carry):
            hop, p = t // self.pieces, t % self.pieces
            for way in (0, 1):
                @when(self.can_send(way, hop))
                def _():
                    self.copy(way, hop, p).wait_send()
            return carry

        lax.fori_loop(0, (self.n - 1) * self.pieces, step, 0)


class Scatter(Line):
    def __init__(self, n, C, S, partial, sbuf, rbuf, ssem, rsem):
        super().__init__(n, C, S)
        self.partial, self.sbuf, self.rbuf, self.ssem, self.rsem = partial, sbuf, rbuf, ssem, rsem

    def copy(self, way, d, p):
        z_to = self.z + 1 - 2 * way
        slot = jnp.where(both(way == 1, d == z_to), self.n, d)
        return remote(
            self.at(self.sbuf, d, p), self.at(self.rbuf, slot, p), self.ssem.at[d, p], self.rsem.at[way, d, p], self.w, z_to
        )

    def slot(self, way, d):
        return jnp.where(both(way == 1, d == self.z), self.n, d)

    def arrived(self, way, d, p):
        where = self.at(self.rbuf, self.slot(way, d), p)
        remote(where, where, self.ssem.at[d, p], self.rsem.at[way, d, p], self.w, self.z).wait_recv()
        return where[...].astype(F32)

    def originate(self, p):
        def step(i, carry):
            way = jnp.where(self.z == 0, 0, 1)
            d = jnp.where(self.z == 0, self.n - 1 - i, i)

            @when(jnp.logical_or(self.z == 0, self.z == self.n - 1))
            def _():
                if self.partial is not self.sbuf:
                    self.at(self.sbuf, d, p)[...] = self.at(self.partial, d, p)[...].astype(BF16)
                self.copy(way, d, p).start()

            return carry

        lax.fori_loop(0, self.n - 1, step, 0)

    def pass_on(self, order, p, ok=True):
        inner = both(ok, self.z > 0, self.z < self.n - 1)

        @when(inner)
        def _():
            def step(i, carry):
                way = jnp.where(self.z < self.n // 2, order, 1 - order)
                d = jnp.where(way == 0, self.n - 1 - i, i)

                @when(jnp.where(way == 0, d > self.z, d < self.z))
                def _():
                    value = self.arrived(way, d, p) + self.at(self.partial, d, p)[...].astype(F32)
                    self.at(self.sbuf, d, p)[...] = value.astype(BF16)
                    self.copy(way, d, p).start()

                return carry

            lax.fori_loop(0, self.n - 1, step, 0)

    def final(self, p, acc):
        acc[...] = self.at(self.partial, self.z, p)[...].astype(F32)
        for way, there in ((0, self.z > 0), (1, self.z < self.n - 1)):
            @when(there)
            def _():
                acc[...] += self.arrived(way, self.z, p)

    def drain(self, lo=0, hi=None):
        hi = self.pieces if hi is None else hi

        def step(t, carry):
            d, p = t // (hi - lo), lo + t % (hi - lo)

            @when(d != self.z)
            def _():
                self.copy(jnp.where(d > self.z, 0, 1), d, p).wait_send()

            return carry

        lax.fori_loop(0, self.n * (hi - lo), step, 0)


def rms_scale(values):
    return lax.rsqrt(jnp.mean(values * values, axis=-1, keepdims=True) + norm_eps)


def rms_back(grad_in, hat, scale_rows):
    return scale_rows * (grad_in - hat * jnp.mean(grad_in * hat, axis=-1, keepdims=True))


def rope(v, cos2, sin2):
    return v * cos2 + pltpu.roll(v, v.shape[-1] // 2, axis=1) * sin2


def chain(k, lo, hi, scat, gath, finish, n):
    def within(p):
        return both(p >= lo, p < hi)

    f = lo + k - 2

    @when(within(f))
    def _():
        finish(f)
        if gath is not None:
            gath.send(0, f)

    scat.pass_on(1, lo + k - 1, within(lo + k - 1))
    scat.pass_on(0, lo + k, within(lo + k))
    if gath is not None:
        for hop in range(n - 1, 0, -1):
            gath.send(hop, f - hop, within(f - hop))


def staggered(k, starts, scat, gath, finish, n):
    ages = [(k - start, p) for p, start in enumerate(starts)]
    for age, p in ages:
        if age == 2:
            finish(p)
            if gath is not None:
                gath.send(0, p)
    for age, p in ages:
        if age == 1:
            scat.pass_on(1, p)
    for age, p in ages:
        if age == 0:
            scat.pass_on(0, p)
    if gath is not None:
        for age, p in ages:
            if 3 <= age <= n + 1:
                gath.send(age - 2, p)


class Square:
    def __init__(self, stage, transit, recv, ssem, rsem):
        self.stage, self.transit, self.recv, self.ssem, self.rsem = stage, transit, recv, ssem, rsem
        w = lax.axis_index("wide")
        self.z = lax.axis_index("narrow")
        core, chip = w % 2, w // 2
        self.beside = 2 * (chip + 1 - 2 * (chip % 2)) + core
        self.below = 2 * (chip + 2 - 4 * (chip // 2)) + core
        self.far = 2 * (3 - chip) + core
        self.owners = (self.far, self.beside, self.below)

    def copy(self, m):
        N = self.transit.shape[1]
        h0, h1 = pl.ds(0, N // 2), pl.ds(N // 2, N // 2)
        block, half, there = ((0, h0, 0), (0, h1, 0), (1, h0, 1), (2, h1, 1), (2, h0, 2), (1, h1, 2))[m]
        to = (self.beside, self.below, self.beside, self.below, self.below, self.beside)[m]
        dst = self.transit.at[:, half] if there == 0 else self.recv.at[there - 1, :, half]
        return remote(self.stage.at[block, :, half], dst, self.ssem.at[m], self.rsem.at[m], to, self.z)

    def put(self, block):
        for m in ((0, 1), (2,), (3,))[block]:
            self.copy(m).start()

    def pass_on(self):
        N = self.transit.shape[1]
        for m, block, half in ((0, 2, pl.ds(0, N // 2)), (1, 1, pl.ds(N // 2, N // 2))):
            self.copy(m).wait_recv()
            value = self.stage[block, :, half].astype(F32) + self.transit[:, half].astype(F32)
            self.stage[block, :, half] = value.astype(BF16)
            self.copy(4 + m).start()

    def drain(self):
        for m in range(6):
            self.copy(m).wait_send()
        for m in range(2, 6):
            self.copy(m).wait_recv()


def row_of(ref):
    return ref[...].astype(F32).reshape(1, ref.shape[0])


def weight_block(A, B, sib_a, sib_b, cols):
    total = None
    for part in range(A.shape[0]):
        for term in (dot(A[part, :, cols], B[part], 0, 0), dot(sib_a(part), sib_b[part], 0, 0)):
            total = term if total is None else total + term
    return total


PLAN = dict(
    branch_starts=(0, 1, 4, 5), back_starts=(0, 1, 4, 5),
    after=dict(
        start=(('input', 0), ('input', 1), ('input', 2), ('input', 3), ('cot0', 0)),
        out0=(('input', 4), ('input', 5), ('cot0', 1), ('cot0', 2)),
        attend10=(('branch', 0), ('branch', 1), ('branch', 2), ('cot0', 3)),
        attend11=(('branch', 3),),
        out1=(('cot0', 4), ('cot1', 0)),
        act=(('branch', 4), ('branch', 5), ('branch', 6)),
        feed01=(('cot1', 1),),
        feed03=(('branch', 7),),
        feed05=(('branch', 8), ('cot1', 2)),
        feed06=(('branch', 9), ('branch', 10), ('cot1', 3), ('cot1', 4)),
        feed10=(('back', 0),),
        feed11=(('back', 1), ('back', 2)),
        feed14=(('back', 3),),
        work4=(('back', 4),),
        work6=(('back', 5), ('back', 6)),
        work9=(('back', 7), ('mlp', 0)),
        work11=(('back', 8),),
        work12=(('mlp', 1),),
        work13=(('back', 9), ('back', 10), ('mlp', 2), ('mlp', 3), ('mlp', 4)),
    ),
)


def middle_kernel(n, C, S, W, HD, docs, push, *refs):
    (lens_ref, attn_gain_ref, qg_ref, kg_ref, freq_ref, gain_ref, x_hbm, cot_hbm_in, wq_hbm, wk_hbm, wv_hbm,
     wout_hbm, wgate_hbm, wup_hbm, wdown_hbm) = refs[:15]
    (raws_hbm, prob_hbm, rots_hbm, tabs_hbm, mix_hbm, normed_hbm,
     middle_hbm, dmid_hbm, gaing_ref, dmix_hbm, db_hbm, mlp_hbm, out_hbm) = refs[15:28]
    rest = list(refs[28:])
    if push:
        sib_n2, sib_cot, sib_act, sib_dg, sib_du, recv_down, recv_gate, blk_up, own_down, own_gate, own_up = rest[:11]
        rest = rest[11:]
    else:
        n2_hbm, cot_hbm, act_hbm, dg_hbm, du_hbm = rest[:5]
        rest = rest[5:]
    (x_ref, cot_ref, middle_ref, dmid_ref, out_ref, dmix_ref, mixv, wout, wgate, wup, wdown, cotf, n2f, dbf, partial, sbuf, rbuf, sbufm,
     dact, act, dg, du, acc, wsem, g1s, g1r, cs, cr, s1s, s1r, g2s, g2r, s2s, s2r, g3s, g3r, sms, smr, osem, vsem) = rest[:40]
    rest = rest[40:]
    if push:
        (stage_d, stage_g, stage_u, transit_d, transit_g, stage32, cols_sib, b_sib, sib_ss, sib_rs,
         down_ss, down_rs, gate_ss, gate_rs, lsem, ssem32) = rest
    R = n * S
    D = x_ref.shape[2]
    FC = wgate.shape[1]
    TN = 512
    nt, nd = FC // TN, D // TN
    P_ = C * HALVES
    rows = S // HALVES
    w, z = lax.axis_index("wide"), lax.axis_index("narrow")
    QC, KC = mixv.shape[2], wk_hbm.shape[1]
    QH, KH = QC // HD, KC // HD
    G = QH // KH
    PC = QC + 2 * KC
    table_lanes = C * 2 * HD
    assert table_lanes % R == 0 and table_lanes + C * R <= FC and PC <= FC
    assert D % R == 0 and QC + KC <= D - QH * R
    prob_at = D // R - QH

    def tiles(count, body):
        def step(j, carry):
            body(j)
            return carry

        lax.fori_loop(0, count, step, 0)

    loads = [pltpu.make_async_copy(a, b, wsem.at[i]) for i, (a, b) in enumerate(
        ((x_hbm, x_ref), (cot_hbm_in, cot_ref), (wq_hbm, wgate.at[:, 0:QC]), (wk_hbm, wgate.at[:, QC:QC + KC]),
         (wv_hbm, wgate.at[:, QC + KC:PC]), (wout_hbm, wout), (wdown_hbm, wdown), (wup_hbm, wup), (wgate_hbm, wgate)))]
    for load in loads[:8]:
        load.start()
    gain, again, qgain, kgain, freq = [row_of(v) for v in (gain_ref, attn_gain_ref, qg_ref, kg_ref, freq_ref)]
    barrier(n, W if push else 0)
    loads[0].wait()
    for part in range(C):
        x = x_ref[part].astype(F32)
        dbf[part, rows_at(z, S)] = (x * rms_scale(x) * again).astype(BF16)
    g1 = Gather(n, C, S, dbf, g1s, g1r)
    gc = Gather(n, C, S, cotf, cs, cr)
    g2 = Gather(n, C, S, n2f, g2s, g2r)
    g3 = Gather(n, C, S, dbf, g3s, g3r)
    s1 = Scatter(n, C, S, partial, sbuf, rbuf, s1s, s1r)
    s2 = Scatter(n, C, S, partial, sbuf, rbuf, s2s, s2r)
    sm = Scatter(n, C, S, sbufm, sbufm, rbuf, sms, smr)
    for p in range(2):
        g1.send(0, p)
    loads[1].wait()
    for part in range(C):
        cotf[part, rows_at(z, S)] = cot_ref[part]
    for part in range(C):
        t = lax.broadcasted_iota(jnp.int32, (R, HD), 0)
        row = lax.broadcasted_iota(jnp.int32, (R, R), 0)
        col = lax.broadcasted_iota(jnp.int32, (R, R), 1)
        first = jnp.zeros((R, HD), jnp.int32)
        first_wide = jnp.zeros((R, R), jnp.int32)
        end = jnp.int32(0)
        for d in range(docs):
            end = end + lens_ref[part, d]
            first = jnp.where(t >= end, end, first)
            first_wide = jnp.where(row >= end, end, first_wide)
        angle = (t - first).astype(F32) * freq
        sign = jnp.where(lax.broadcasted_iota(jnp.int32, (R, HD), 1) < HD // 2, -1.0, 1.0)
        dact[:, lanes(2 * part, HD)] = jnp.cos(angle)
        dact[:, lanes(2 * part + 1, HD)] = jnp.sin(angle) * sign
        dact[:, lanes(table_lanes // R + part, R)] = jnp.where(both(col <= row, col >= first_wide), 0.0, masked_score)

    def input_step(k):
        for hop in range(n - 1, 0, -1):
            if 0 <= k + 1 - hop < P_:
                g1.send(hop, k + 1 - hop)
        if k + 2 < P_:
            g1.send(0, k + 2)

    def cot_step(part, k):
        if k == 0:
            for h in range(HALVES):
                gc.send(0, part * HALVES + h)
        for hop in range(n - 1, 0, -1):
            if 0 <= k - hop < HALVES:
                gc.send(hop, part * HALVES + k - hop)

    def mlp_step(k):
        if k == 0:
            for j in range(nd):
                sbufm[0, :, lanes(j, TN)] = dot(act[0], wdown[:, lanes(j, TN)], 1, 0).astype(BF16)
            for h in range(HALVES):
                sm.originate(h)
        else:
            staggered(k - 1, tuple(range(HALVES)), sm, None, mlp_done, n)

    def mlp_done(p):
        sm.final(p, acc)
        part, rr = mid_row(p)
        out_ref[part, rr] = middle_ref[part, rr] + acc[...]

    steps = dict(
        input=input_step, cot0=functools.partial(cot_step, 0), cot1=functools.partial(cot_step, 1), mlp=mlp_step,
        branch=lambda k: staggered(k, PLAN["branch_starts"], s1, g2, after_attention, n),
        back=lambda k: staggered(k, PLAN["back_starts"], s2, g3, after_feed, n))
    assert (n, C, HALVES, KH, nt, nd) == (4, 2, 2, 2, 3, 4)

    def run(place):
        for kind, k in PLAN["after"].get(place, ()):
            steps[kind](k)

    run("start")
    for load in loads[2:5]:
        load.wait()

    def project(part):
        lhs = dbf[part]
        partial[part, :, 0:QC + KC] = dot(lhs, wgate[:, 0:QC + KC], 1, 0)
        act[part, :, QC + KC:PC] = dot(lhs, wgate[:, QC + KC:PC], 1, 0).astype(BF16)

    def attend(part, k):
        cos2, sin2 = dact[:, lanes(2 * part, HD)], dact[:, lanes(2 * part + 1, HD)]

        def turned(index, head_gain):
            raw = partial[part, :, lanes(index, HD)]
            value = rope(raw * rms_scale(raw) * head_gain, cos2, sin2).astype(BF16)
            act[part, :, lanes(index, HD)] = value
            return value

        kr = turned(QH + k, kgain)
        for g in range(G):
            h = k * G + g
            qr = turned(h, qgain)
            s = dot(qr, kr, 1, 1) * HD ** (-0.5) + dact[:, lanes(table_lanes // R + part, R)]
            ex = jnp.exp(s - jnp.max(s, axis=-1, keepdims=True))
            prob = ex / jnp.sum(ex, axis=-1, keepdims=True)
            partial[part, :, lanes(prob_at + h, R)] = prob
            mix = dot(prob.astype(BF16), act[part, :, lanes(QH + KH + k, HD)], 1, 0)
            mixv[part, :, lanes(h, HD)] = mix.astype(BF16)

    def saves(part, lo=0, hi=6):
        return [pltpu.make_async_copy(a, b, vsem.at[i, part]) for i, (a, b) in list(enumerate((
            (partial.at[part, :, 0:QC + KC], raws_hbm.at[part]), (partial.at[part, :, prob_at * R:D], prob_hbm.at[part]),
            (act.at[part, :, 0:PC], rots_hbm.at[part]), (dact.at[:, lanes(part, 2 * HD)], tabs_hbm.at[part]),
            (mixv.at[part], mix_hbm.at[part]), (dbf.at[part], normed_hbm.at[part]))))[lo:hi]]

    def out_project(part):
        if part == 0:
            loads[5].wait()
        for save in saves(part, 0, 2):
            save.wait()

        def out_tile(j):
            partial[part, :, lanes(j, TN)] = dot(mixv[part], wout[:, lanes(j, TN)], 1, 0)

        tiles(nd, out_tile)
        for h in range(HALVES):
            s1.originate(part * HALVES + h)

    def mid_row(p):
        return p // HALVES, rows_at(p % HALVES, rows)

    def after_attention(p):
        s1.final(p, acc)
        part, rr = mid_row(p)
        middle = x_ref[part, rr].astype(F32) + acc[...]
        middle_ref[part, rr] = middle
        g2.at(n2f, z, p)[...] = (middle * rms_scale(middle) * gain).astype(BF16)

    def dact_tile(part, j):
        dact[:, lanes(j, TN)] = dot(cotf[part], wdown[rows_at(j, TN), :], 1, 1)

    project(0)
    run("project0")
    for k in range(KH):
        attend(0, k)
        if k == KH - 1:
            for save in saves(0):
                save.start()
        run("attend0%d" % k)
    out_project(0)
    run("out0")
    project(1)
    loads[8].start()
    run("project1")
    for k in range(KH):
        attend(1, k)
        if k == KH - 1:
            for save in saves(1):
                save.start()
        run("attend1%d" % k)
    out_project(1)
    run("out1")
    loads[6].wait()
    for part in range(C):
        for save in saves(part, 2, 6):
            save.wait()
    tiles(nt, lambda j: dact_tile(0, j))
    run("act")
    loads[7].wait()
    loads[8].wait()
    g1.drain()
    if push:
        core = w % 2
        mate = w + 1 - 2 * core

        def swap(index, src, dst, part):
            return remote(src.at[part], dst.at[part], sib_ss.at[index, part], sib_rs.at[index, part], mate, z)

    def after_feed(p):
        s2.final(p, acc)
        part, rr = mid_row(p)
        dn2 = acc[...]
        middle = middle_ref[part, rr]
        scale = rms_scale(middle)
        hat = middle * scale
        gaing_ref[...] += jnp.sum(dn2 * hat, axis=0, keepdims=True)
        dmid = cot_ref[part, rr].astype(F32) + rms_back(dn2 * gain, hat, scale)
        dmid_ref[part, rr] = dmid
        g3.at(dbf, z, p)[...] = dmid.astype(BF16)

    gaing_ref[...] = jnp.zeros_like(gaing_ref)

    def feed(part):
        def service(e, only=range(nt + nd - 1)):
            for which in range(C):
                for at in only:
                    if "feed%d%d" % (which, at) in PLAN["after"]:
                        @when(both(part == which, e == at))
                        def _():
                            run("feed%d%d" % (which, at))

        def gate_tile(j):
            @when(part > 0)
            def _():
                dact_tile(part, j)

            at = lanes(j, TN)
            gate = dot(n2f[part], wgate[:, at], 1, 0)
            up = dot(n2f[part], wup[:, at], 1, 0)
            sig = jax.nn.sigmoid(gate)
            silu = gate * sig
            d_act = dact[:, at]
            act[part, :, at] = (silu * up).astype(BF16)
            dg[part, :, at] = (d_act * up * sig * (1.0 + gate * (1.0 - sig))).astype(BF16)
            du[part, :, at] = (d_act * silu).astype(BF16)
            service(j)

        tiles(nt, gate_tile)
        if push:
            for index, (a, b) in enumerate(((n2f, sib_n2), (cotf, sib_cot), (act, sib_act), (dg, sib_dg), (du, sib_du))):
                swap(index, a, b, part).start()

        def back_tile(j):
            at = rows_at(j, TN)
            partial[part, :, lanes(j, TN)] = dot(dg[part], wgate[at, :], 1, 1) + dot(du[part], wup[at, :], 1, 1)
            service(nt + j)

        tiles(nd, back_tile)
        @when(part == 0)
        def _():
            s1.drain()

        for h in range(HALVES):
            s2.originate(part * HALVES + h)
        service(nt + nd - 1, (nt + nd - 1,))

    tiles(C, feed)

    def mlp_sums(part):
        for j in range(nd):
            sbufm[part, :, lanes(j, TN)] = dot(act[part], wdown[:, lanes(j, TN)], 1, 0).astype(BF16)

    def mix_back(part):
        dmix_ref[part] = dot(dbf[part], wout[...], 1, 1).astype(BF16)

    if push:
        width = D // W
        down = Square(stage_d, transit_d, recv_down, down_ss, down_rs)
        gate = Square(stage_g, transit_g, recv_gate, gate_ss, gate_rs)
        owners = down.owners

        def fetch(cols, b):
            copies = []
            if cols is not None:
                for q, owner in enumerate(owners + (w,)):
                    for part in range(C):
                        copies.append(pltpu.make_async_copy(
                            cols.at[part, :, lanes(owner, width)], cols_sib.at[q, part], lsem.at[0, q, part]))
            for part in range(C):
                copies.append(pltpu.make_async_copy(b.at[part], b_sib.at[part], lsem.at[1, 0, part]))
            for copy in copies:
                copy.start()
            for copy in copies:
                copy.wait()

        def block(A, B, q):
            return weight_block(A, B, lambda part: cols_sib[q, part], b_sib, lanes((owners + (w,))[q], width))

        def own_copy(dst, index):
            return pltpu.make_async_copy(stage32, dst, ssem32.at[index])

        def up_copy(q):
            return pltpu.make_async_copy(stage_u.at[q % 2], blk_up.at[q], osem.at[7 + q])

        def arrive(*pairs):
            for part in range(C):
                for index, dst in pairs:
                    swap(index, dst, dst, part).wait_recv()

        def down_block(q):
            if q == 0:
                arrive((1, sib_cot), (2, sib_act))
                fetch(sib_cot, sib_act)
            if q < 3:
                stage_d[q] = block(cotf, act, q).astype(BF16)
                down.put(q)
            else:
                stage32[...] = block(cotf, act, q)
                own_copy(own_down, 0).start()

        def gate_block(q):
            if q == 0:
                arrive((0, sib_n2), (3, sib_dg))
                fetch(sib_n2, sib_dg)
            if q < 3:
                stage_g[q] = block(n2f, dg, q).astype(BF16)
                gate.put(q)
            else:
                own_copy(own_down, 0).wait()
                stage32[...] = block(n2f, dg, q)
                own_copy(own_gate, 1).start()

        def up_block(q):
            if q == 0:
                arrive((4, sib_du))
                fetch(None, sib_du)
            if q < 3:
                if q == 2:
                    up_copy(0).wait()
                stage_u[q % 2] = block(n2f, du, q).astype(BF16)
                up_copy(q).start()
            else:
                own_copy(own_gate, 1).wait()
                stage32[...] = block(n2f, du, q)
                own_copy(own_up, 2).start()

        work = [[(down_block, q)] for q in range(4)] + [[(gate_block, q)] for q in range(3)] + [
            [(down.pass_on,), (gate_block, 3)], [(up_block, 0)], [(up_block, 1)], [(gate.pass_on,), (up_block, 2)], [(up_block, 3)]]
    else:
        outs = [pltpu.make_async_copy(a, b, osem.at[7 + i]) for i, (a, b) in enumerate(
            ((n2f, n2_hbm), (cotf, cot_hbm), (act, act_hbm), (dg, dg_hbm), (du, du_hbm)))]
        for out in outs:
            out.start()
        work = [[] for _ in range(12)]
    ends = [pltpu.make_async_copy(a, b, osem.at[i]) for i, (a, b) in enumerate(
        ((middle_ref, middle_hbm), (sbufm.at[1], mlp_hbm.at[0]), (dbf.at[0], db_hbm.at[0]), (dbf.at[1], db_hbm.at[1]),
         (dmid_ref, dmid_hbm), (out_ref, out_hbm), (dmix_ref, dmix_hbm)))]
    ends[0].start()

    def second_mlp_sums():
        mlp_sums(1)
        ends[1].start()

    def first_mix_back():
        mix_back(0)
        ends[2].start()

    work += [[(second_mlp_sums,)], [(first_mix_back,)]]
    for place, pieces in enumerate(work):
        for piece in pieces:
            piece[0](*piece[1:])
        run("work%d" % place)
    for end in ends[3:6]:
        end.start()
    for part in range(1, C):
        mix_back(part)
    ends[6].start()
    gc.drain()
    g2.drain()
    g3.drain()
    s2.drain()
    sm.drain(0, HALVES)
    for end in ends:
        end.wait()
    if push:
        for part in range(C):
            for index, (a, b) in enumerate(((n2f, sib_n2), (cotf, sib_cot), (act, sib_act), (dg, sib_dg), (du, sib_du))):
                swap(index, a, b, part).wait_send()
        for q in (1, 2):
            up_copy(q).wait()
        own_copy(own_up, 2).wait()
        down.drain()
        gate.drain()
    else:
        for out in outs:
            out.wait()


def last_kernel(n, C, S, W, HD, push, *refs):
    gain_ref, qg_ref, kg_ref, gmlp_ref = refs[:4]
    sources = refs[4:16]
    rest = list(refs[16:])
    if push:
        mix_hbm, db_hbm, normed_hbm, blk_up = rest[:4]
        rest = rest[4:]
    out_hbm, in_hbm, ga_ref, gm_ref, gq_ref, gk_ref = rest[:6]
    rest = rest[6:]
    if push:
        recv_up, recv_out, recv_qkv, own_out, own_qkv = rest[:5]
        rest = rest[5:]
    else:
        dproj_hbm = rest[0]
        rest = rest[1:]
    held = rest[:14]
    (sbufm, raws, rots, prob_ref, tabs, dmix_ref, wq, wk, wv, middle_ref, dmid_ref, x_ref) = held[:12]
    out_ref, in_ref = held[12:14]
    rest = rest[14:]
    (dproj, partial, sbuf, rbuf, rbufm, acc, gains, small, small_two,
     lsem, s3s, s3r, sms, smr, gs1, gr1, gs2, gr2, osem) = rest[:19]
    rest = rest[19:]
    if push:
        (mixv, dbv, normv, sib_mix, sib_db, sib_norm, sib_dproj, sib_ss, sib_rs) = rest[:9]
        squares = rest[9:]
    R, D = n * S, x_ref.shape[2]
    QC, KC = wq.shape[1], wk.shape[1]
    G, KH = QC // KC, KC // HD
    TN = 512
    nd = D // TN
    P_ = C * HALVES
    rows = S // HALVES
    w, z = lax.axis_index("wide"), lax.axis_index("narrow")
    targets = (sbufm.at[1:2],) + tuple(held[1:12])
    loads = [pltpu.make_async_copy(a, b, lsem.at[i]) for i, (a, b) in enumerate(zip(sources, targets))]
    loads[0].start()
    if push:
        stage_up = squares[0]
        blocks = [pltpu.make_async_copy(blk_up.at[q], stage_up.at[q], lsem.at[15 + q]) for q in range(3)]
        for q in range(3):
            blocks[q].start()
    for load in loads[1:6]:
        load.start()
    if push:
        extra = [pltpu.make_async_copy(a, b, lsem.at[12 + i]) for i, (a, b) in enumerate(
            ((mix_hbm, mixv), (db_hbm, dbv), (normed_hbm, normv)))]
        for load in extra:
            load.start()
    for load in loads[6:]:
        load.start()
    barrier(n, W)
    sm = Scatter(n, C, S, sbufm, sbufm, rbufm, sms, smr)
    s3 = Scatter(n, C, S, partial, sbuf, rbuf, s3s, s3r)
    if push:
        core = w % 2
        mate = w + 1 - 2 * core
        width = D // W
        up_sums, out_sums, qkv_sums = [
            Square(squares[i], squares[i + 1], recv, squares[i + 2], squares[i + 3])
            for i, recv in ((0, recv_up), (4, recv_out), (8, recv_qkv))]
        stage_out, stage_qkv = squares[4], squares[8]

        def swap(index, src, dst, part):
            return remote(src.at[part], dst.at[part], sib_ss.at[index, part], sib_rs.at[index, part], mate, z)

    loads[0].wait()
    for p in range(HALVES, P_):
        sm.originate(p)
    if push:
        for q in range(3):
            blocks[q].wait()
            up_sums.put(q)

    def rest_in():
        for load in loads[6:]:
            load.wait()
        if push:
            for load in extra:
                load.wait()
            for part in range(C):
                for index, (a, b) in enumerate(((mixv, sib_mix), (dbv, sib_db), (normv, sib_norm))):
                    swap(index, a, b, part).start()

    def piece_row(p):
        return p // HALVES, rows_at(p % HALVES, rows)

    def mlp_done(p):
        sm.final(p, acc)
        part, rr = piece_row(p)
        out_ref[0, rr] = middle_ref[part, rr] + acc[...]

    gain, qgain, kgain = [row_of(v) for v in (gain_ref, qg_ref, kg_ref)]

    def grad_done(p):
        s3.final(p, acc)
        part, rr = piece_row(p)
        dn = acc[...]
        x = x_ref[part, rr].astype(F32)
        scale = rms_scale(x)
        hat = x * scale
        gains[0:1, :] += jnp.sum(dn * hat, axis=0, keepdims=True)
        in_ref[part, rr] = dmid_ref[part, rr] + rms_back(dn * gain, hat, scale)

    gains[...] = jnp.zeros_like(gains)
    scale = HD ** (-0.5)
    for load in loads[1:6]:
        load.wait()

    def unit(part, k):
        cos2, sin2 = tabs[part, :, 0:HD], tabs[part, :, HD:2 * HD]
        kr, vr = rots[part, :, lanes(QC // HD + k, HD)], rots[part, :, lanes(QC // HD + KH + k, HD)]

        def unturned(grad, raw, head_gain, at):
            d_n = grad * cos2 - pltpu.roll(grad, HD // 2, axis=1) * sin2
            r = rms_scale(raw)
            hat = raw * r
            gains[at:at + 1, :HD] += jnp.sum(d_n * hat, axis=0, keepdims=True)
            return rms_back(d_n * head_gain, hat, r).astype(BF16)

        dk, dv = None, None
        for g in range(G):
            h = k * G + g
            pr = prob_ref[part, :, lanes(h, R)]
            dm = dmix_ref[part, :, lanes(h, HD)]
            dp = dot(dm, vr, 1, 1)
            one = dot(pr.astype(BF16), dm, 0, 0)
            dv = one if dv is None else dv + one
            ds = (pr * (dp - jnp.sum(pr * dp, axis=-1, keepdims=True))).astype(BF16)
            one = dot(ds, rots[part, :, lanes(h, HD)], 0, 0)
            dk = one if dk is None else dk + one
            dq = dot(ds, kr, 1, 0) * scale
            dproj[part, :, lanes(h, HD)] = unturned(dq, raws[part, :, lanes(h, HD)], qgain, 1)
        dproj[part, :, lanes(QC // HD + k, HD)] = unturned(dk * scale, raws[part, :, lanes(QC // HD + k, HD)], kgain, 2)
        dproj[part, :, lanes(QC // HD + KH + k, HD)] = dv.astype(BF16)

    if push:
        def block(A, B, sib_a, sib_b, owner):
            cols = lanes(owner, width)
            return weight_block(A, B, lambda part: sib_a[part, :, cols], sib_b, cols)

        def arrive(*pairs):
            for part in range(C):
                for index, dst in pairs:
                    swap(index, dst, dst, part).wait_recv()

        def out_block(q):
            if q == 0:
                arrive((0, sib_mix), (1, sib_db))
            if q < 3:
                stage_out[q] = block(dbv, mixv, sib_db, sib_mix, out_sums.owners[q]).astype(BF16)
                out_sums.put(q)
            else:
                own_out[...] = block(dbv, mixv, sib_db, sib_mix, w)

        def qkv_block(q):
            if q == 0:
                arrive((2, sib_norm), (3, sib_dproj))
            if q < 3:
                stage_qkv[q] = block(normv, dproj, sib_norm, sib_dproj, qkv_sums.owners[q]).astype(BF16)
                qkv_sums.put(q)
            else:
                own_qkv[...] = block(normv, dproj, sib_norm, sib_dproj, w)

    def grad_step(k):
        staggered(k, tuple(range(P_)), s3, None, grad_done, n)

    def mlp_step(k):
        chain(k, HALVES, P_, sm, None, mlp_done, n)

    assert (n, C, HALVES, KH) == (4, 2, 2, 2)

    def backward(part):
        def heads(k, carry):
            unit(part, k)

            @when(both(part == 0, k == 0))
            def _():
                rest_in()

            @when(both(part == 0, k == KH - 1))
            def _():
                mlp_step(0)

            if push:
                @when(both(part == 1, k == 0))
                def _():
                    up_sums.pass_on()

            return carry

        lax.fori_loop(0, KH, heads, 0)
        if push:
            swap(3, dproj, sib_dproj, part).start()

        def back_tile(j, carry):
            at = rows_at(j, TN)
            partial[part, :, lanes(j, TN)] = (
                dot(dproj[part, :, 0:QC], wq[at, :], 1, 1) + dot(dproj[part, :, QC:QC + KC], wk[at, :], 1, 1)
                + dot(dproj[part, :, QC + KC:QC + 2 * KC], wv[at, :], 1, 1))
            return carry

        lax.fori_loop(0, nd, back_tile, 0)
        for h in range(HALVES):
            s3.originate(part * HALVES + h)

        @when(part == 0)
        def _():
            if push:
                for q in range(3):
                    out_block(q)
            mlp_step(1)
            mlp_step(2)

        @when(part == 1)
        def _():
            grad_step(0)

    def both_parts(part, carry):
        backward(part)
        return carry

    lax.fori_loop(0, C, both_parts, 0)
    tail = [lambda: mlp_step(3), lambda: grad_step(1), lambda: grad_step(2), lambda: grad_step(3)]
    if push:
        tail = [lambda: qkv_block(0), lambda: qkv_block(1), tail[0], lambda: qkv_block(2), tail[1], out_sums.pass_on,
                lambda: out_block(3), lambda: qkv_block(3), tail[2], tail[3], qkv_sums.pass_on]
    for piece in tail + [lambda: grad_step(4), lambda: grad_step(5)]:
        piece()
    if not push:
        out = pltpu.make_async_copy(dproj, dproj_hbm, lsem.at[16])
        out.start()
    ends = [pltpu.make_async_copy(a, b, osem.at[i]) for i, (a, b) in enumerate(((out_ref, out_hbm), (in_ref, in_hbm)))]
    for end in ends:
        end.start()
    L = 2 * D + 2 * HD
    small[w, :, 0:D] = gains[0:1, :]
    small[w, :, D:2 * D] = gmlp_ref[...]
    small[w, :, 2 * D:2 * D + HD] = gains[1:2, :HD]
    small[w, :, 2 * D + HD:L] = gains[2:3, :HD]

    def to_wide(s):
        return remote(small.at[w], small.at[w], gs1.at[s], gr1.at[s], lax.rem(w + s, W), z)

    def to_narrow(s):
        return remote(small_two.at[z], small_two.at[z], gs2.at[s], gr2.at[s], w, lax.rem(z + s, n))

    for s in range(1, W):
        to_wide(s).start()
    for s in range(1, W):
        to_wide(s).wait_recv()
    total = small[0]
    for s in range(1, W):
        total = total + small[s]
    small_two[z] = total
    for s in range(1, n):
        to_narrow(s).start()
    for s in range(1, n):
        to_narrow(s).wait_recv()
    total = small_two[0]
    for s in range(1, n):
        total = total + small_two[s]
    for ref, lo, hi in ((ga_ref, 0, D), (gm_ref, D, 2 * D), (gq_ref, 2 * D, 2 * D + HD), (gk_ref, 2 * D + HD, L)):
        ref[...] = total[:, lo:hi].reshape(hi - lo)
    for s in range(1, W):
        to_wide(s).wait_send()
    for s in range(1, n):
        to_narrow(s).wait_send()
    sm.drain(HALVES, P_)
    s3.drain()
    for end in ends:
        end.wait()
    if push:
        for part in range(C):
            for index, (a, b) in enumerate(((mixv, sib_mix), (dbv, sib_db), (normv, sib_norm), (dproj, sib_dproj))):
                swap(index, a, b, part).wait_send()
        for sums in (up_sums, out_sums, qkv_sums):
            sums.drain()
    else:
        out.wait()


def finish_kernel(*refs):
    own_down, recv_down, own_out, recv_out, own_gate, recv_gate, own_up, recv_up, own_qkv, recv_qkv = refs[:10]
    low, high = refs[10:12]
    passed = refs[12:17]
    down, out_g, gate, up, g_q, g_k, g_v, out_ref = refs[17:25]
    out_ref[0], out_ref[1] = low[0], high[0]

    def total(own, parts):
        value = own[...]
        for i in range(parts.shape[0]):
            value = value + parts[i].astype(F32)
        return value

    down[...] = total(own_down, recv_down).T
    out_g[...] = total(own_out, recv_out).T
    gate[...] = total(own_gate, recv_gate)
    up[...] = total(own_up, recv_up)
    qkv = total(own_qkv, recv_qkv)
    first, second = g_q.shape[1], g_q.shape[1] + g_k.shape[1]
    g_q[...], g_k[...], g_v[...] = qkv[:, :first], qkv[:, first:second], qkv[:, second:]
    for a, b in zip(passed, refs[25:]):
        b[...] = a[...]


def local(W, layer_input, document_lengths, attn_gain, w_query, w_key, w_value, query_gain, key_gain, w_out, mlp_gain,
          w_gate, w_up, w_down, output_cotangent):
    n = lax.axis_size("narrow")
    C, _, S, D = layer_input.shape
    R = n * S
    T = C * R
    HD = query_gain.shape[0]
    QC, KC = w_query.shape[1], w_key.shape[1]
    QH = QC // HD
    FC = w_gate.shape[1]
    docs = document_lengths.shape[2]
    P_ = C * HALVES
    grid = 4
    push = (W == 8 and (D // W) % 128 == 0 and FC % (128 * grid) == 0 and QC % (128 * grid) == 0
            and S % (8 * grid) == 0)
    assert C == 2
    width = D // W
    x_own, cot_own = layer_input[:, 0], output_cotangent[:, 0]
    sds = jax.ShapeDtypeStruct
    dma = pltpu.SemaphoreType.DMA
    gsem = lambda: dma((2, n - 1, P_))
    half = np.arange(HD) % (HD // 2)
    freq = jnp.asarray(np.power(np.float32(1000000.0), np.float32(-2.0) * half.astype(np.float32) / np.float32(HD)), F32)
    vm = pl.BlockSpec(memory_space=pltpu.VMEM)
    hbm = pl.BlockSpec(memory_space=pl.ANY)
    smem = pl.BlockSpec(memory_space=pltpu.SMEM)
    VM = pltpu.VMEM

    PC = QC + 2 * KC
    full, wide_rows = sds((C, R, D), BF16), sds((C, R, FC), BF16)
    kept = [sds((C, R, QC + KC), F32), sds((C, R, QH * R), F32), sds((C, R, PC), BF16), sds((C, R, 2 * HD), F32),
            sds((C, R, QC), BF16), full]
    outs = kept + [sds((C, S, D), F32), sds((C, S, D), F32), sds((1, D), F32), sds((C, R, QC), BF16), full, sds((1, R, D), BF16), sds((1, S, D), F32)]
    specs = [hbm] * 8 + [vm] + [hbm] * 4
    line = lambda: [VM((C, R, D), BF16), VM((C, R + S, D), BF16)]
    scratch = (
        [VM((C, S, D), BF16), VM((C, S, D), BF16), VM((C, S, D), F32), VM((C, S, D), F32), VM((1, S, D), F32), VM((C, R, QC), BF16)]
        + [VM((C, R, QC), BF16), VM(w_out.shape, BF16), VM(w_gate.shape, BF16), VM(w_up.shape, BF16), VM(w_down.shape, BF16)]
        + [VM((C, R, D), BF16)] * 3 + [VM((C, R, D), F32)] + line()
        + [VM((C, R, D), BF16), VM((R, FC), F32)] + [VM((C, R, FC), BF16)] * 3 + [VM((S // HALVES, D), F32)]
        + [dma((9,)), gsem(), gsem(), gsem(), gsem(), dma((n, P_)), dma((2, n, P_)), gsem(), gsem(), dma((n, P_)), dma((2, n, P_)),
           gsem(), gsem(), dma((n, P_)), dma((2, n, P_)), dma((12,)), dma((6, C))]
    )
    if push:
        sums, own = sds((2, width, FC), BF16), sds((width, FC), F32)
        outs += [full, full, wide_rows, wide_rows, wide_rows, sums, sums, sds((3, width, FC), BF16), own, own, own]
        scratch += [VM((3, width, FC), BF16), VM((3, width, FC), BF16), VM((2, width, FC), BF16), VM((width, FC), BF16),
                    VM((width, FC), BF16), VM((width, FC), F32), VM((4, C, R, width), BF16), VM((C, R, FC), BF16),
                    dma((5, C)), dma((5, C)), dma((6,)), dma((6,)), dma((6,)), dma((6,)), dma((2, 4, C)), dma((3,))]
    else:
        outs += [full, full, wide_rows, wide_rows, wide_rows]
    res = pl.pallas_call(
        functools.partial(middle_kernel, n, C, S, W, HD, docs, push), name="middle", out_shape=outs,
        in_specs=[smem] + [vm] * 5 + [hbm] * 9, out_specs=specs + [hbm] * (len(outs) - len(specs)), scratch_shapes=scratch,
        compiler_params=pltpu.CompilerParams(collective_id=0, has_side_effects=True, vmem_limit_bytes=63 << 20),
    )(document_lengths[:, 0], attn_gain, query_gain, key_gain, freq, mlp_gain, x_own, cot_own, w_query, w_key, w_value, w_out, w_gate, w_up, w_down)
    raws, prob, rots, tabs, mix, normed_full = res[:6]
    res = res[6:]
    middle, d_middle, gmlp, d_mix, db_full, mlp_sums, out_low = res[:7]

    args = [attn_gain, query_gain, key_gain, gmlp, mlp_sums, raws, rots, prob, tabs, d_mix, w_query, w_key, w_value,
            middle, d_middle, x_own]
    in_specs = [vm] * 4 + [hbm] * 12
    held = [VM((C, R, D), BF16)] + [VM(v.shape, v.dtype) for v in args[5:]] + [VM((1, S, D), F32), VM((C, S, D), F32)]
    own_rows = sds((C, S, D), F32)
    outs = [sds((1, S, D), F32), own_rows, sds((D,), F32), sds((D,), F32), sds((HD,), F32), sds((HD,), F32)]
    specs = [hbm] * 2 + [vm] * 4
    L = 2 * D + 2 * HD
    scratch = (
        held + [VM((C, R, PC), BF16), VM((C, R, D), F32)]
        + line() + line()[1:] + [VM((S // HALVES, D), F32), VM((8, D), F32), VM((W, 1, L), F32), VM((n, 1, L), F32)]
        + [dma((18,)), dma((n, P_)), dma((2, n, P_)), dma((n, P_)), dma((2, n, P_)), dma((W,)), dma((W,)), dma((n,)), dma((n,)),
           dma((2,))]
    )
    if push:
        sib_n2, sib_cot, sib_act, sib_dg, sib_du, recv_down, recv_gate, blk_up, own_down, own_gate, own_up = res[7:]
        args += [mix, db_full, normed_full, blk_up]
        in_specs += [hbm] * 4
        outs += [sds((2, width, FC), BF16)] + [sds((2, width, QC), BF16), sds((2, width, PC), BF16),
                                                       sds((width, QC), F32), sds((width, PC), F32)]
        specs += [hbm] * 3 + [vm] * 2
        scratch += [VM((C, R, QC), BF16), VM((C, R, D), BF16), VM((C, R, D), BF16)]
        scratch += [VM((C, R, QC), BF16), VM((C, R, D), BF16), VM((C, R, D), BF16), VM((C, R, PC), BF16)]
        scratch += [dma((4, C)), dma((4, C))]
        for cols in (FC, QC, PC):
            scratch += [VM((3, width, cols), BF16), VM((width, cols), BF16), dma((6,)), dma((6,))]
    else:
        outs += [sds((C, R, PC), BF16)]
        specs += [hbm]
    last = pl.pallas_call(
        functools.partial(last_kernel, n, C, S, W, HD, push), name="last", out_shape=outs, in_specs=in_specs, out_specs=specs,
        scratch_shapes=scratch,
        compiler_params=pltpu.CompilerParams(collective_id=1, has_side_effects=True, vmem_limit_bytes=60 << 20),
    )(*args)
    out_high, in_own, g_attn, g_mlp, g_query, g_key = last[:6]
    if push:
        recv_up, recv_out, recv_qkv, own_out, own_qkv = last[6:]

        def by_rows(rows, cols, lead=None):
            if lead is None:
                return pl.BlockSpec((rows // grid, cols), lambda i: (i, 0))
            return pl.BlockSpec((lead, rows // grid, cols), lambda i: (0, i, 0))

        def by_cols(rows, cols, lead=None):
            if lead is None:
                return pl.BlockSpec((rows, cols // grid), lambda i: (0, i))
            return pl.BlockSpec((lead, rows, cols // grid), lambda i: (0, 0, i))

        def shard(parts):
            return pl.BlockSpec((parts, S // grid, D), lambda i: (0, i, 0))

        same = [shard(C)] + [pl.BlockSpec(v.shape, lambda i: (0,)) for v in last[2:6]]
        down, out_g, gate, up, g_q, g_k, g_v, out_own, in_own, g_attn, g_mlp, g_query, g_key = pl.pallas_call(
            finish_kernel, name="finish", grid=(grid,),
            out_shape=[sds((FC, width), F32), sds((QC, width), F32), sds((width, FC), F32), sds((width, FC), F32),
                       sds((width, QC), F32), sds((width, KC), F32), sds((width, KC), F32)]
            + [own_rows] + [sds(v.shape, v.dtype) for v in last[1:6]],
            in_specs=[by_cols(width, FC), by_cols(width, FC, 2), by_cols(width, QC), by_cols(width, QC, 2),
                      by_rows(width, FC), by_rows(width, FC, 2), by_rows(width, FC), by_rows(width, FC, 2),
                      by_rows(width, PC), by_rows(width, PC, 2), shard(1), shard(1)] + same,
            out_specs=[by_rows(FC, width), by_rows(QC, width), by_rows(width, FC), by_rows(width, FC), by_rows(width, QC),
                       by_rows(width, KC), by_rows(width, KC), shard(C)] + same,
            compiler_params=pltpu.CompilerParams(vmem_limit_bytes=62 << 20),
        )(own_down, recv_down, own_out, recv_out, own_gate, recv_gate, own_up, recv_up, own_qkv, recv_qkv, out_low, *last[:6])
        projections = (g_q, g_k, g_v)
    else:
        n2, cot, act, dg, du = [v.reshape(T, -1) for v in res[7:]]
        d_proj = last[6].reshape(T, PC)
        db, mixed, normed = db_full.reshape(T, D), mix.reshape(T, QC), normed_full.reshape(T, D)

        def scatter(a, b, dim):
            return lax.psum_scatter(dot(a, b, 0, 0).astype(BF16), "wide", scatter_dimension=dim, tiled=True).astype(F32)

        down, gate, up = scatter(act, cot, 1), scatter(n2, dg, 0), scatter(n2, du, 0)
        out_g, qkv = scatter(mixed, db, 1), scatter(normed, d_proj, 0)
        out_own = jnp.concatenate([out_low, out_high], axis=0)
        projections = (qkv[:, :QC], qkv[:, QC:QC + KC], qkv[:, QC + KC:])
    return (
        out_own[:, None], in_own[:, None], g_attn, *projections,
        g_query, g_key, out_g, g_mlp, gate, up, down,
    )


def solution(mesh):
    rows = P(None, "wide", "narrow", None)
    cols, tall = P(None, "narrow"), P("narrow", None)
    in_specs = (rows, P(None, "wide", None), P(), cols, cols, cols, P(), P(), tall, P(), cols, cols, tall, rows)
    both_ways, turned = P("wide", "narrow"), P("narrow", "wide")
    out_specs = (rows, rows, P(), both_ways, both_ways, both_ways, P(), P(), turned, P(), both_ways, both_ways, turned)
    body = functools.partial(local, mesh.shape["wide"])
    return jax.shard_map(body, mesh=mesh, in_specs=in_specs, out_specs=out_specs, check_vma=False)
```

```python
import functools

import jax
import jax.numpy as jnp
import numpy as np
from jax import lax
from jax.experimental import pallas as pl
from jax.experimental.pallas import tpu as pltpu
from jax.sharding import PartitionSpec as P

MESH = pl.DeviceIdType.MESH
F32 = jnp.float32
BF16 = jnp.bfloat16
norm_eps = 1e-06
masked_score = -1e30
HALVES = 2


def both(*conds):
    out = True
    for cond in conds:
        if isinstance(cond, bool):
            if not cond:
                return False
        else:
            out = cond if out is True else jnp.logical_and(out, cond)
    return out


def when(cond):
    if isinstance(cond, bool):
        return (lambda body: body()) if cond else (lambda body: None)
    return pl.when(cond)


def rows_at(index, rows):
    return pl.ds(pl.multiple_of(index * rows, rows), rows)


def lanes(index, width):
    return pl.ds(pl.multiple_of(index * width, width), width)


def dot(a, b, ca, cb):
    return lax.dot_general(a, b, (((ca,), (cb,)), ((), ())), preferred_element_type=F32)


def remote(src, dst, ssem, rsem, wide, narrow):
    return pltpu.make_async_remote_copy(
        src_ref=src, dst_ref=dst, send_sem=ssem, recv_sem=rsem, device_id=(wide, narrow), device_id_type=MESH
    )


def barrier(n, wide=0):
    w, z = lax.axis_index("wide"), lax.axis_index("narrow")
    bar = pltpu.get_barrier_semaphore()
    for step in range(1, n):
        pl.semaphore_signal(bar, inc=1, device_id=(w, lax.rem(z + step, n)), device_id_type=MESH)
    for step in range(1, wide):
        pl.semaphore_signal(bar, inc=1, device_id=(lax.rem(w + step, wide), z), device_id_type=MESH)
    pl.semaphore_wait(bar, n - 1 + max(wide - 1, 0))


class Line:
    def __init__(self, n, C, S):
        self.n, self.C, self.S = n, C, S
        self.pieces, self.rows = C * HALVES, S // HALVES
        self.w, self.z = lax.axis_index("wide"), lax.axis_index("narrow")

    def at(self, ref, chunk, p):
        start = chunk * self.S + (p % HALVES) * self.rows
        return ref.at[p // HALVES, pl.ds(pl.multiple_of(start, self.rows), self.rows)]


class Gather(Line):
    def __init__(self, n, C, S, full, ssem, rsem):
        super().__init__(n, C, S)
        self.full, self.ssem, self.rsem = full, ssem, rsem

    def copy(self, way, hop, p):
        chunk = self.z - hop if way == 0 else self.z + hop
        where = self.at(self.full, chunk, p)
        z_to = self.z + 1 if way == 0 else self.z - 1
        return remote(where, where, self.ssem.at[way, hop, p], self.rsem.at[way, hop, p], self.w, z_to)

    def arrival(self, way, hop, p):
        chunk = self.z - hop - 1 if way == 0 else self.z + hop + 1
        where = self.at(self.full, chunk, p)
        z_to = self.z + 1 if way == 0 else self.z - 1
        return remote(where, where, self.ssem.at[way, hop, p], self.rsem.at[way, hop, p], self.w, z_to)

    def has(self, way, hop):
        return self.z >= hop if way == 0 else self.z + hop <= self.n - 1

    def can_send(self, way, hop):
        edge = self.z < self.n - 1 if way == 0 else self.z > 0
        return both(self.has(way, hop), edge, hop < self.n - 1)

    def send(self, hop, p, ok=True):
        known = isinstance(hop, int)
        for way in (0, 1):
            if not (known and hop == 0):
                @when(both(ok, hop > 0, self.has(way, hop)))
                def _():
                    self.arrival(way, hop - 1, p).wait_recv()

            if not (known and hop >= self.n - 1):
                @when(both(ok, self.can_send(way, hop)))
                def _():
                    self.copy(way, hop, p).start()

    def drain(self):
        def step(t, carry):
            hop, p = t // self.pieces, t % self.pieces
            for way in (0, 1):
                @when(self.can_send(way, hop))
                def _():
                    self.copy(way, hop, p).wait_send()
            return carry

        lax.fori_loop(0, (self.n - 1) * self.pieces, step, 0)


class Scatter(Line):
    def __init__(self, n, C, S, partial, sbuf, rbuf, ssem, rsem):
        super().__init__(n, C, S)
        self.partial, self.sbuf, self.rbuf, self.ssem, self.rsem = partial, sbuf, rbuf, ssem, rsem

    def copy(self, way, d, p):
        z_to = self.z + 1 - 2 * way
        slot = jnp.where(both(way == 1, d == z_to), self.n, d)
        return remote(
            self.at(self.sbuf, d, p), self.at(self.rbuf, slot, p), self.ssem.at[d, p], self.rsem.at[way, d, p], self.w, z_to
        )

    def slot(self, way, d):
        return jnp.where(both(way == 1, d == self.z), self.n, d)

    def arrived(self, way, d, p):
        where = self.at(self.rbuf, self.slot(way, d), p)
        remote(where, where, self.ssem.at[d, p], self.rsem.at[way, d, p], self.w, self.z).wait_recv()
        return where[...].astype(F32)

    def originate(self, p):
        def step(i, carry):
            way = jnp.where(self.z == 0, 0, 1)
            d = jnp.where(self.z == 0, self.n - 1 - i, i)

            @when(jnp.logical_or(self.z == 0, self.z == self.n - 1))
            def _():
                if self.partial is not self.sbuf:
                    self.at(self.sbuf, d, p)[...] = self.at(self.partial, d, p)[...].astype(BF16)
                self.copy(way, d, p).start()

            return carry

        lax.fori_loop(0, self.n - 1, step, 0)

    def pass_on(self, order, p, ok=True):
        inner = both(ok, self.z > 0, self.z < self.n - 1)

        @when(inner)
        def _():
            def step(i, carry):
                way = jnp.where(self.z < self.n // 2, order, 1 - order)
                d = jnp.where(way == 0, self.n - 1 - i, i)

                @when(jnp.where(way == 0, d > self.z, d < self.z))
                def _():
                    value = self.arrived(way, d, p) + self.at(self.partial, d, p)[...].astype(F32)
                    self.at(self.sbuf, d, p)[...] = value.astype(BF16)
                    self.copy(way, d, p).start()

                return carry

            lax.fori_loop(0, self.n - 1, step, 0)

    def final(self, p, acc):
        acc[...] = self.at(self.partial, self.z, p)[...].astype(F32)
        for way, there in ((0, self.z > 0), (1, self.z < self.n - 1)):
            @when(there)
            def _():
                acc[...] += self.arrived(way, self.z, p)

    def drain(self, lo=0, hi=None):
        hi = self.pieces if hi is None else hi

        def step(t, carry):
            d, p = t // (hi - lo), lo + t % (hi - lo)

            @when(d != self.z)
            def _():
                self.copy(jnp.where(d > self.z, 0, 1), d, p).wait_send()

            return carry

        lax.fori_loop(0, self.n * (hi - lo), step, 0)


def rms_scale(values):
    return lax.rsqrt(jnp.mean(values * values, axis=-1, keepdims=True) + norm_eps)


def rms_back(grad_in, hat, scale_rows):
    return scale_rows * (grad_in - hat * jnp.mean(grad_in * hat, axis=-1, keepdims=True))


def rope(v, cos2, sin2):
    return v * cos2 + pltpu.roll(v, v.shape[-1] // 2, axis=1) * sin2


def chain(k, lo, hi, scat, gath, finish, n):
    def within(p):
        return both(p >= lo, p < hi)

    f = lo + k - 2

    @when(within(f))
    def _():
        finish(f)
        if gath is not None:
            gath.send(0, f)

    scat.pass_on(1, lo + k - 1, within(lo + k - 1))
    scat.pass_on(0, lo + k, within(lo + k))
    if gath is not None:
        for hop in range(n - 1, 0, -1):
            gath.send(hop, f - hop, within(f - hop))


def staggered(k, starts, scat, gath, finish, n):
    ages = [(k - start, p) for p, start in enumerate(starts)]
    for age, p in ages:
        if age == 2:
            finish(p)
            if gath is not None:
                gath.send(0, p)
    for age, p in ages:
        if age == 1:
            scat.pass_on(1, p)
    for age, p in ages:
        if age == 0:
            scat.pass_on(0, p)
    if gath is not None:
        for age, p in ages:
            if 3 <= age <= n + 1:
                gath.send(age - 2, p)


class Square:
    def __init__(self, stage, transit, recv, ssem, rsem):
        self.stage, self.transit, self.recv, self.ssem, self.rsem = stage, transit, recv, ssem, rsem
        w = lax.axis_index("wide")
        self.z = lax.axis_index("narrow")
        core, chip = w % 2, w // 2
        self.beside = 2 * (chip + 1 - 2 * (chip % 2)) + core
        self.below = 2 * (chip + 2 - 4 * (chip // 2)) + core
        self.far = 2 * (3 - chip) + core
        self.owners = (self.far, self.beside, self.below)

    def copy(self, m):
        N = self.transit.shape[1]
        h0, h1 = pl.ds(0, N // 2), pl.ds(N // 2, N // 2)
        block, half, there = ((0, h0, 0), (0, h1, 0), (1, h0, 1), (2, h1, 1), (2, h0, 2), (1, h1, 2))[m]
        to = (self.beside, self.below, self.beside, self.below, self.below, self.beside)[m]
        dst = self.transit.at[:, half] if there == 0 else self.recv.at[there - 1, :, half]
        return remote(self.stage.at[block, :, half], dst, self.ssem.at[m], self.rsem.at[m], to, self.z)

    def put(self, block):
        for m in ((0, 1), (2,), (3,))[block]:
            self.copy(m).start()

    def pass_on(self):
        N = self.transit.shape[1]
        for m, block, half in ((0, 2, pl.ds(0, N // 2)), (1, 1, pl.ds(N // 2, N // 2))):
            self.copy(m).wait_recv()
            value = self.stage[block, :, half].astype(F32) + self.transit[:, half].astype(F32)
            self.stage[block, :, half] = value.astype(BF16)
            self.copy(4 + m).start()

    def drain(self):
        for m in range(6):
            self.copy(m).wait_send()
        for m in range(2, 6):
            self.copy(m).wait_recv()


def row_of(ref):
    return ref[...].astype(F32).reshape(1, ref.shape[0])


def weight_block(A, B, sib_a, sib_b, cols):
    total = None
    for part in range(A.shape[0]):
        for term in (dot(A[part, :, cols], B[part], 0, 0), dot(sib_a(part), sib_b[part], 0, 0)):
            total = term if total is None else total + term
    return total


PLAN = dict(
    branch_starts=(0, 1, 5, 6), back_starts=(0, 1, 5, 6),
    after=dict(
        start=(('input', 0), ('input', 1), ('input', 2), ('input', 3), ('cot0', 0)),
        attend01=(('input', 4),),
        out0=(('input', 5), ('cot0', 1), ('cot0', 2), ('cot1', 0)),
        project1=(('branch', 0),),
        attend10=(('branch', 1), ('branch', 2)),
        attend11=(('branch', 3), ('cot1', 1)),
        out1=(('cot0', 3), ('cot0', 4)),
        act=(('branch', 4), ('branch', 5), ('branch', 6), ('branch', 7)),
        feed00=(('cot1', 2),),
        feed03=(('branch', 8),),
        feed04=(('cot1', 3),),
        feed06=(('branch', 9), ('branch', 10), ('branch', 11), ('cot1', 4)),
        feed10=(('back', 0),),
        feed11=(('back', 1), ('back', 2)),
        feed14=(('back', 3),),
        work1=(('back', 4),),
        work3=(('back', 5), ('back', 6), ('back', 7)),
        work5=(('back', 8), ('mlp', 0)),
        work7=(('back', 9),),
        work10=(('back', 10), ('mlp', 1)),
        work11=(('mlp', 2), ('mlp', 3)),
        work12=(('back', 11),),
        work13=(('mlp', 4),),
    ),
)


def middle_kernel(n, C, S, W, HD, docs, push, *refs):
    (lens_ref, attn_gain_ref, qg_ref, kg_ref, freq_ref, gain_ref, x_hbm, cot_hbm_in, wq_hbm, wk_hbm, wv_hbm,
     wout_hbm, wgate_hbm, wup_hbm, wdown_hbm) = refs[:15]
    (raws_hbm, prob_hbm, rots_hbm, tabs_hbm, mix_hbm, normed_hbm,
     middle_hbm, dmid_hbm, gaing_ref, dmix_hbm, db_hbm, mlp_hbm, out_hbm) = refs[15:28]
    rest = list(refs[28:])
    if push:
        sib_n2, sib_cot, sib_act, sib_dg, sib_du, recv_down, recv_gate, blk_up, own_down, own_gate, own_up = rest[:11]
        rest = rest[11:]
    else:
        n2_hbm, cot_hbm, act_hbm, dg_hbm, du_hbm = rest[:5]
        rest = rest[5:]
    (x_ref, cot_ref, middle_ref, dmid_ref, out_ref, dmix_ref, mixv, wout, wgate, wup, wdown, cotf, n2f, dbf, partial, sbuf, rbuf, sbufm,
     dact, act, dg, du, acc, wsem, g1s, g1r, cs, cr, s1s, s1r, g2s, g2r, s2s, s2r, g3s, g3r, sms, smr, osem, vsem) = rest[:40]
    rest = rest[40:]
    if push:
        (stage_d, stage_g, stage_u, transit_d, transit_g, stage_own, cols_sib, b_sib, sib_ss, sib_rs,
         down_ss, down_rs, gate_ss, gate_rs, lsem, own_sem) = rest
    R = n * S
    D = x_ref.shape[2]
    FC = wgate.shape[1]
    TN = 512
    nt, nd = FC // TN, D // TN
    P_ = C * HALVES
    rows = S // HALVES
    w, z = lax.axis_index("wide"), lax.axis_index("narrow")
    QC, KC = mixv.shape[2], wk_hbm.shape[1]
    QH, KH = QC // HD, KC // HD
    G = QH // KH
    PC = QC + 2 * KC
    table_lanes = C * 2 * HD
    assert table_lanes % R == 0 and table_lanes + C * R <= FC and PC <= FC
    assert D % R == 0 and QC + KC <= D - QH * R
    prob_at = D // R - QH

    def tiles(count, body):
        def step(j, carry):
            body(j)
            return carry

        lax.fori_loop(0, count, step, 0)

    loads = [pltpu.make_async_copy(a, b, wsem.at[i]) for i, (a, b) in enumerate(
        ((x_hbm, x_ref), (cot_hbm_in, cot_ref), (wq_hbm, wgate.at[:, 0:QC]), (wk_hbm, wgate.at[:, QC:QC + KC]),
         (wv_hbm, wgate.at[:, QC + KC:PC]), (wout_hbm, wout), (wdown_hbm, wdown), (wup_hbm, wup), (wgate_hbm, wgate)))]
    for load in loads[:8]:
        load.start()
    gain, again, qgain, kgain, freq = [row_of(v) for v in (gain_ref, attn_gain_ref, qg_ref, kg_ref, freq_ref)]
    barrier(n, W if push else 0)
    loads[0].wait()
    for part in range(C):
        x = x_ref[part].astype(F32)
        dbf[part, rows_at(z, S)] = (x * rms_scale(x) * again).astype(BF16)
    g1 = Gather(n, C, S, dbf, g1s, g1r)
    gc = Gather(n, C, S, cotf, cs, cr)
    g2 = Gather(n, C, S, n2f, g2s, g2r)
    g3 = Gather(n, C, S, dbf, g3s, g3r)
    s1 = Scatter(n, C, S, partial, sbuf, rbuf, s1s, s1r)
    s2 = Scatter(n, C, S, partial, sbuf, rbuf, s2s, s2r)
    sm = Scatter(n, C, S, sbufm, sbufm, rbuf, sms, smr)
    for p in range(2):
        g1.send(0, p)
    loads[1].wait()
    for part in range(C):
        cotf[part, rows_at(z, S)] = cot_ref[part]
    for part in range(C):
        t = lax.broadcasted_iota(jnp.int32, (R, HD), 0)
        row = lax.broadcasted_iota(jnp.int32, (R, R), 0)
        col = lax.broadcasted_iota(jnp.int32, (R, R), 1)
        first = jnp.zeros((R, HD), jnp.int32)
        first_wide = jnp.zeros((R, R), jnp.int32)
        end = jnp.int32(0)
        for d in range(docs):
            end = end + lens_ref[part, d]
            first = jnp.where(t >= end, end, first)
            first_wide = jnp.where(row >= end, end, first_wide)
        angle = (t - first).astype(F32) * freq
        sign = jnp.where(lax.broadcasted_iota(jnp.int32, (R, HD), 1) < HD // 2, -1.0, 1.0)
        dact[:, lanes(2 * part, HD)] = jnp.cos(angle)
        dact[:, lanes(2 * part + 1, HD)] = jnp.sin(angle) * sign
        dact[:, lanes(table_lanes // R + part, R)] = jnp.where(both(col <= row, col >= first_wide), 0.0, masked_score)

    def input_step(k):
        for hop in range(n - 1, 0, -1):
            if 0 <= k + 1 - hop < P_:
                g1.send(hop, k + 1 - hop)
        if k + 2 < P_:
            g1.send(0, k + 2)

    def cot_step(part, k):
        if k == 0:
            for h in range(HALVES):
                gc.send(0, part * HALVES + h)
        for hop in range(n - 1, 0, -1):
            if 0 <= k - hop < HALVES:
                gc.send(hop, part * HALVES + k - hop)

    def mlp_step(k):
        if k == 0:
            for j in range(nd):
                sbufm[0, :, lanes(j, TN)] = dot(act[0], wdown[:, lanes(j, TN)], 1, 0).astype(BF16)
            for h in range(HALVES):
                sm.originate(h)
        else:
            staggered(k - 1, tuple(range(HALVES)), sm, None, mlp_done, n)

    def mlp_done(p):
        sm.final(p, acc)
        part, rr = mid_row(p)
        out_ref[part, rr] = middle_ref[part, rr] + acc[...]

    steps = dict(
        input=input_step, cot0=functools.partial(cot_step, 0), cot1=functools.partial(cot_step, 1), mlp=mlp_step,
        branch=lambda k: staggered(k, PLAN["branch_starts"], s1, g2, after_attention, n),
        back=lambda k: staggered(k, PLAN["back_starts"], s2, g3, after_feed, n))
    assert (n, C, HALVES, KH, nt, nd) == (4, 2, 2, 2, 3, 4)

    def run(place):
        for kind, k in PLAN["after"].get(place, ()):
            steps[kind](k)

    run("start")
    for load in loads[2:5]:
        load.wait()

    def project(part):
        lhs = dbf[part]
        partial[part, :, 0:QC + KC] = dot(lhs, wgate[:, 0:QC + KC], 1, 0)
        act[part, :, QC + KC:PC] = dot(lhs, wgate[:, QC + KC:PC], 1, 0).astype(BF16)

    def attend(part, k):
        cos2, sin2 = dact[:, lanes(2 * part, HD)], dact[:, lanes(2 * part + 1, HD)]

        def turned(index, head_gain):
            raw = partial[part, :, lanes(index, HD)]
            value = rope(raw * rms_scale(raw) * head_gain, cos2, sin2).astype(BF16)
            act[part, :, lanes(index, HD)] = value
            return value

        kr = turned(QH + k, kgain)
        for g in range(G):
            h = k * G + g
            qr = turned(h, qgain)
            s = dot(qr, kr, 1, 1) * HD ** (-0.5) + dact[:, lanes(table_lanes // R + part, R)]
            ex = jnp.exp(s - jnp.max(s, axis=-1, keepdims=True))
            prob = ex / jnp.sum(ex, axis=-1, keepdims=True)
            partial[part, :, lanes(prob_at + h, R)] = prob
            mix = dot(prob.astype(BF16), act[part, :, lanes(QH + KH + k, HD)], 1, 0)
            mixv[part, :, lanes(h, HD)] = mix.astype(BF16)

    def saves(part, lo=0, hi=6):
        return [pltpu.make_async_copy(a, b, vsem.at[i, part]) for i, (a, b) in list(enumerate((
            (partial.at[part, :, 0:QC + KC], raws_hbm.at[part]), (partial.at[part, :, prob_at * R:D], prob_hbm.at[part]),
            (act.at[part, :, 0:PC], rots_hbm.at[part]), (dact.at[:, lanes(part, 2 * HD)], tabs_hbm.at[part]),
            (mixv.at[part], mix_hbm.at[part]), (dbf.at[part], normed_hbm.at[part]))))[lo:hi]]

    def out_project(part):
        if part == 0:
            loads[5].wait()
        for save in saves(part, 0, 2):
            save.wait()

        def out_tile(j):
            partial[part, :, lanes(j, TN)] = dot(mixv[part], wout[:, lanes(j, TN)], 1, 0)

        tiles(nd, out_tile)
        for h in range(HALVES):
            s1.originate(part * HALVES + h)

    def mid_row(p):
        return p // HALVES, rows_at(p % HALVES, rows)

    def after_attention(p):
        s1.final(p, acc)
        part, rr = mid_row(p)
        middle = x_ref[part, rr].astype(F32) + acc[...]
        middle_ref[part, rr] = middle
        g2.at(n2f, z, p)[...] = (middle * rms_scale(middle) * gain).astype(BF16)

    def dact_tile(part, j):
        dact[:, lanes(j, TN)] = dot(cotf[part], wdown[rows_at(j, TN), :], 1, 1)

    project(0)
    run("project0")
    for k in range(KH):
        attend(0, k)
        if k == KH - 1:
            for save in saves(0):
                save.start()
        run("attend0%d" % k)
    out_project(0)
    run("out0")
    project(1)
    loads[8].start()
    run("project1")
    for k in range(KH):
        attend(1, k)
        if k == KH - 1:
            for save in saves(1):
                save.start()
        run("attend1%d" % k)
    out_project(1)
    run("out1")
    loads[6].wait()
    for part in range(C):
        for save in saves(part, 2, 6):
            save.wait()
    tiles(nt, lambda j: dact_tile(0, j))
    run("act")
    loads[7].wait()
    loads[8].wait()
    g1.drain()
    if push:
        core = w % 2
        mate = w + 1 - 2 * core

        def swap(index, src, dst, part):
            return remote(src.at[part], dst.at[part], sib_ss.at[index, part], sib_rs.at[index, part], mate, z)

    def after_feed(p):
        s2.final(p, acc)
        part, rr = mid_row(p)
        dn2 = acc[...]
        middle = middle_ref[part, rr]
        scale = rms_scale(middle)
        hat = middle * scale
        gaing_ref[...] += jnp.sum(dn2 * hat, axis=0, keepdims=True)
        dmid = cot_ref[part, rr].astype(F32) + rms_back(dn2 * gain, hat, scale)
        dmid_ref[part, rr] = dmid
        g3.at(dbf, z, p)[...] = dmid.astype(BF16)

    gaing_ref[...] = jnp.zeros_like(gaing_ref)

    def feed(part):
        def service(e, only=range(nt + nd - 1)):
            for which in range(C):
                for at in only:
                    if "feed%d%d" % (which, at) in PLAN["after"]:
                        @when(both(part == which, e == at))
                        def _():
                            run("feed%d%d" % (which, at))

        def gate_tile(j):
            @when(part > 0)
            def _():
                dact_tile(part, j)

            at = lanes(j, TN)
            gate = dot(n2f[part], wgate[:, at], 1, 0)
            up = dot(n2f[part], wup[:, at], 1, 0)
            sig = jax.nn.sigmoid(gate)
            silu = gate * sig
            d_act = dact[:, at]
            act[part, :, at] = (silu * up).astype(BF16)
            dg[part, :, at] = (d_act * up * sig * (1.0 + gate * (1.0 - sig))).astype(BF16)
            du[part, :, at] = (d_act * silu).astype(BF16)
            service(j)

        tiles(nt, gate_tile)
        if push:
            for index, (a, b) in enumerate(((n2f, sib_n2), (cotf, sib_cot), (act, sib_act), (dg, sib_dg), (du, sib_du))):
                swap(index, a, b, part).start()

        def back_tile(j):
            at = rows_at(j, TN)
            partial[part, :, lanes(j, TN)] = dot(dg[part], wgate[at, :], 1, 1) + dot(du[part], wup[at, :], 1, 1)
            service(nt + j)

        tiles(nd, back_tile)
        @when(part == 0)
        def _():
            s1.drain()

        for h in range(HALVES):
            s2.originate(part * HALVES + h)
        service(nt + nd - 1, (nt + nd - 1,))

    tiles(C, feed)

    def mlp_sums(part):
        for j in range(nd):
            sbufm[part, :, lanes(j, TN)] = dot(act[part], wdown[:, lanes(j, TN)], 1, 0).astype(BF16)

    def mix_back():
        dmix_ref[0] = dot(dbf[0], wout[...], 1, 1).astype(BF16)

    if push:
        width = D // W
        down = Square(stage_d, transit_d, recv_down, down_ss, down_rs)
        gate = Square(stage_g, transit_g, recv_gate, gate_ss, gate_rs)
        owners = down.owners

        def fetch(cols, b):
            copies = []
            if cols is not None:
                for q, owner in enumerate(owners + (w,)):
                    for part in range(C):
                        copies.append(pltpu.make_async_copy(
                            cols.at[part, :, lanes(owner, width)], cols_sib.at[q, part], lsem.at[0, q, part]))
            for part in range(C):
                copies.append(pltpu.make_async_copy(b.at[part], b_sib.at[part], lsem.at[1, 0, part]))
            for copy in copies:
                copy.start()
            for copy in copies:
                copy.wait()

        def block(A, B, q):
            return weight_block(A, B, lambda part: cols_sib[q, part], b_sib, lanes((owners + (w,))[q], width))

        def own_copy(dst, index):
            return pltpu.make_async_copy(stage_own, dst, own_sem.at[index])

        def up_copy(q):
            return pltpu.make_async_copy(stage_u.at[q % 2], blk_up.at[q], osem.at[7 + q])

        def arrive(*pairs):
            for part in range(C):
                for index, dst in pairs:
                    swap(index, dst, dst, part).wait_recv()

        def down_block(q):
            if q == 0:
                arrive((1, sib_cot), (2, sib_act))
                fetch(sib_cot, sib_act)
            if q < 3:
                stage_d[q] = block(cotf, act, q).astype(BF16)
                down.put(q)
            else:
                stage_own[...] = block(cotf, act, q).astype(BF16)
                own_copy(own_down, 0).start()

        def gate_block(q):
            if q == 0:
                arrive((0, sib_n2), (3, sib_dg))
                fetch(sib_n2, sib_dg)
            if q < 3:
                stage_g[q] = block(n2f, dg, q).astype(BF16)
                gate.put(q)
            else:
                own_copy(own_down, 0).wait()
                stage_own[...] = block(n2f, dg, q).astype(BF16)
                own_copy(own_gate, 1).start()

        def up_block(q):
            if q == 0:
                arrive((4, sib_du))
                fetch(None, sib_du)
            if q < 3:
                if q == 2:
                    up_copy(0).wait()
                stage_u[q % 2] = block(n2f, du, q).astype(BF16)
                up_copy(q).start()
            else:
                own_copy(own_gate, 1).wait()
                stage_own[...] = block(n2f, du, q).astype(BF16)
                own_copy(own_up, 2).start()

        work = [[(down_block, q)] for q in range(4)] + [[(gate_block, q)] for q in range(3)] + [
            [(down.pass_on,), (gate_block, 3)], [(up_block, 0)], [(up_block, 1)], [(gate.pass_on,), (up_block, 2)], [(up_block, 3)]]
    else:
        outs = [pltpu.make_async_copy(a, b, osem.at[7 + i]) for i, (a, b) in enumerate(
            ((n2f, n2_hbm), (cotf, cot_hbm), (act, act_hbm), (dg, dg_hbm), (du, du_hbm)))]
        for out in outs:
            out.start()
        work = [[] for _ in range(12)]
    ends = [pltpu.make_async_copy(a, b, osem.at[i]) for i, (a, b) in enumerate(
        ((middle_ref, middle_hbm), (sbufm.at[1], mlp_hbm.at[0]), (dbf.at[0], db_hbm.at[0]), (dbf.at[1], db_hbm.at[1]),
         (dmid_ref, dmid_hbm), (out_ref, out_hbm), (dmix_ref, dmix_hbm)))]
    ends[0].start()

    def second_mlp_sums():
        mlp_sums(1)
        ends[1].start()

    def first_mix_back():
        mix_back()
        ends[2].start()
        ends[6].start()

    work += [[(second_mlp_sums,)], [(first_mix_back,)]]
    for place, pieces in enumerate(work):
        for piece in pieces:
            piece[0](*piece[1:])
        run("work%d" % place)
    for end in ends[3:6]:
        end.start()
    gc.drain()
    g2.drain()
    g3.drain()
    s2.drain()
    sm.drain(0, HALVES)
    for end in ends:
        end.wait()
    if push:
        for part in range(C):
            for index, (a, b) in enumerate(((n2f, sib_n2), (cotf, sib_cot), (act, sib_act), (dg, sib_dg), (du, sib_du))):
                swap(index, a, b, part).wait_send()
        for q in (1, 2):
            up_copy(q).wait()
        own_copy(own_up, 2).wait()
        down.drain()
        gate.drain()
    else:
        for out in outs:
            out.wait()


def last_kernel(n, C, S, W, HD, push, *refs):
    gain_ref, qg_ref, kg_ref, gmlp_ref = refs[:4]
    sources = refs[4:18]
    rest = list(refs[18:])
    if push:
        mix_hbm, normed_hbm, blk_up = rest[:3]
        rest = rest[3:]
    out_hbm, in_hbm, ga_ref, gm_ref, gq_ref, gk_ref = rest[:6]
    rest = rest[6:]
    if push:
        recv_up, recv_out, recv_qkv, own_out_hbm, own_qkv_hbm = rest[:5]
        rest = rest[5:]
    else:
        dproj_hbm = rest[0]
        rest = rest[1:]
    held = rest[:16]
    (sbufm, raws, rots, prob_ref, tabs, dmix_ref, wq, wk, wv, middle_ref, dmid_ref, x_ref, dbv, wout) = held[:14]
    out_ref, in_ref = held[14:16]
    rest = rest[16:]
    (dproj, partial, sbuf, rbuf, rbufm, acc, gains, small, small_two,
     lsem, s3s, s3r, sms, smr, gs1, gr1, gs2, gr2, osem) = rest[:19]
    rest = rest[19:]
    if push:
        (mixv, normv, sib_mix, sib_db, sib_norm, sib_dproj, sib_ss, sib_rs, own_out, own_qkv) = rest[:10]
        squares = rest[10:]
    R, D = n * S, x_ref.shape[2]
    QC, KC = wq.shape[1], wk.shape[1]
    G, KH = QC // KC, KC // HD
    TN = 512
    nd = D // TN
    P_ = C * HALVES
    rows = S // HALVES
    w, z = lax.axis_index("wide"), lax.axis_index("narrow")
    targets = (sbufm.at[1:2],) + tuple(held[1:5]) + (dmix_ref.at[0:1],) + tuple(held[6:14])
    loads = [pltpu.make_async_copy(a, b, lsem.at[i]) for i, (a, b) in enumerate(zip(sources, targets))]
    loads[0].start()
    if push:
        stage_up = squares[0]
        blocks = [pltpu.make_async_copy(blk_up.at[q], stage_up.at[q], lsem.at[16 + q]) for q in range(3)]
        for q in range(3):
            blocks[q].start()
    for load in loads[1:6]:
        load.start()
    if push:
        extra = [pltpu.make_async_copy(a, b, lsem.at[14 + i]) for i, (a, b) in enumerate(
            ((mix_hbm, mixv), (normed_hbm, normv)))]
        for load in extra:
            load.start()
    for load in loads[6:]:
        load.start()
    barrier(n, W)
    sm = Scatter(n, C, S, sbufm, sbufm, rbufm, sms, smr)
    s3 = Scatter(n, C, S, partial, sbuf, rbuf, s3s, s3r)
    if push:
        core = w % 2
        mate = w + 1 - 2 * core
        width = D // W
        up_sums, out_sums, qkv_sums = [
            Square(squares[i], squares[i + 1], recv, squares[i + 2], squares[i + 3])
            for i, recv in ((0, recv_up), (4, recv_out), (8, recv_qkv))]
        stage_out, stage_qkv = squares[4], squares[8]

        def swap(index, src, dst, part):
            return remote(src.at[part], dst.at[part], sib_ss.at[index, part], sib_rs.at[index, part], mate, z)

    loads[0].wait()
    for p in range(HALVES, P_):
        sm.originate(p)
    if push:
        for q in range(3):
            blocks[q].wait()
            up_sums.put(q)

    def rest_in():
        for load in loads[6:]:
            load.wait()
        if push:
            for load in extra:
                load.wait()
            for part in range(C):
                for index, (a, b) in enumerate(((mixv, sib_mix), (dbv, sib_db), (normv, sib_norm))):
                    swap(index, a, b, part).start()

    def piece_row(p):
        return p // HALVES, rows_at(p % HALVES, rows)

    def mlp_done(p):
        sm.final(p, acc)
        part, rr = piece_row(p)
        out_ref[0, rr] = middle_ref[part, rr] + acc[...]

    gain, qgain, kgain = [row_of(v) for v in (gain_ref, qg_ref, kg_ref)]

    def grad_done(p):
        s3.final(p, acc)
        part, rr = piece_row(p)
        dn = acc[...]
        x = x_ref[part, rr].astype(F32)
        scale = rms_scale(x)
        hat = x * scale
        gains[0:1, :] += jnp.sum(dn * hat, axis=0, keepdims=True)
        in_ref[part, rr] = dmid_ref[part, rr] + rms_back(dn * gain, hat, scale)

    gains[...] = jnp.zeros_like(gains)
    scale = HD ** (-0.5)
    for load in loads[1:6]:
        load.wait()

    def unit(part, k):
        cos2, sin2 = tabs[part, :, 0:HD], tabs[part, :, HD:2 * HD]
        kr, vr = rots[part, :, lanes(QC // HD + k, HD)], rots[part, :, lanes(QC // HD + KH + k, HD)]

        def unturned(grad, raw, head_gain, at):
            d_n = grad * cos2 - pltpu.roll(grad, HD // 2, axis=1) * sin2
            r = rms_scale(raw)
            hat = raw * r
            gains[at:at + 1, :HD] += jnp.sum(d_n * hat, axis=0, keepdims=True)
            return rms_back(d_n * head_gain, hat, r).astype(BF16)

        dk, dv = None, None
        for g in range(G):
            h = k * G + g
            pr = prob_ref[part, :, lanes(h, R)]
            dm = dmix_ref[part, :, lanes(h, HD)]
            dp = dot(dm, vr, 1, 1)
            one = dot(pr.astype(BF16), dm, 0, 0)
            dv = one if dv is None else dv + one
            ds = (pr * (dp - jnp.sum(pr * dp, axis=-1, keepdims=True))).astype(BF16)
            one = dot(ds, rots[part, :, lanes(h, HD)], 0, 0)
            dk = one if dk is None else dk + one
            dq = dot(ds, kr, 1, 0) * scale
            dproj[part, :, lanes(h, HD)] = unturned(dq, raws[part, :, lanes(h, HD)], qgain, 1)
        dproj[part, :, lanes(QC // HD + k, HD)] = unturned(dk * scale, raws[part, :, lanes(QC // HD + k, HD)], kgain, 2)
        dproj[part, :, lanes(QC // HD + KH + k, HD)] = dv.astype(BF16)

    if push:
        def block(A, B, sib_a, sib_b, owner):
            cols = lanes(owner, width)
            return weight_block(A, B, lambda part: sib_a[part, :, cols], sib_b, cols)

        own_copies = [pltpu.make_async_copy(a, b, osem.at[2 + i]) for i, (a, b) in enumerate(
            ((own_out, own_out_hbm), (own_qkv, own_qkv_hbm)))]

        def arrive(*pairs):
            for part in range(C):
                for index, dst in pairs:
                    swap(index, dst, dst, part).wait_recv()

        def out_block(q):
            if q == 0:
                arrive((0, sib_mix), (1, sib_db))
            if q < 3:
                stage_out[q] = block(dbv, mixv, sib_db, sib_mix, out_sums.owners[q]).astype(BF16)
                out_sums.put(q)
            else:
                own_out[...] = block(dbv, mixv, sib_db, sib_mix, w).astype(BF16)
                own_copies[0].start()

        def qkv_block(q):
            if q == 0:
                arrive((2, sib_norm), (3, sib_dproj))
            if q < 3:
                stage_qkv[q] = block(normv, dproj, sib_norm, sib_dproj, qkv_sums.owners[q]).astype(BF16)
                qkv_sums.put(q)
            else:
                own_qkv[...] = block(normv, dproj, sib_norm, sib_dproj, w).astype(BF16)
                own_copies[1].start()

    def grad_step(k):
        staggered(k, tuple(range(P_)), s3, None, grad_done, n)

    def mlp_step(k):
        chain(k, HALVES, P_, sm, None, mlp_done, n)

    assert (n, C, HALVES, KH) == (4, 2, 2, 2)

    def backward(part):
        @when(part == 1)
        def _():
            dmix_ref[1] = dot(dbv[1], wout[...], 1, 1).astype(BF16)

        def heads(k, carry):
            unit(part, k)

            @when(both(part == 0, k == 0))
            def _():
                rest_in()

            @when(both(part == 0, k == KH - 1))
            def _():
                mlp_step(0)

            if push:
                @when(both(part == 1, k == 0))
                def _():
                    up_sums.pass_on()

            return carry

        lax.fori_loop(0, KH, heads, 0)
        if push:
            swap(3, dproj, sib_dproj, part).start()

        def back_tile(j, carry):
            at = rows_at(j, TN)
            partial[part, :, lanes(j, TN)] = (
                dot(dproj[part, :, 0:QC], wq[at, :], 1, 1) + dot(dproj[part, :, QC:QC + KC], wk[at, :], 1, 1)
                + dot(dproj[part, :, QC + KC:QC + 2 * KC], wv[at, :], 1, 1))
            return carry

        lax.fori_loop(0, nd, back_tile, 0)
        for h in range(HALVES):
            s3.originate(part * HALVES + h)

        @when(part == 0)
        def _():
            if push:
                for q in range(3):
                    out_block(q)
            mlp_step(1)
            mlp_step(2)

        @when(part == 1)
        def _():
            grad_step(0)

    def both_parts(part, carry):
        backward(part)
        return carry

    lax.fori_loop(0, C, both_parts, 0)
    tail = [lambda: mlp_step(3), lambda: grad_step(1), lambda: grad_step(2), lambda: grad_step(3)]
    if push:
        tail = [lambda: qkv_block(0), lambda: qkv_block(1), tail[0], lambda: qkv_block(2), tail[1], out_sums.pass_on,
                lambda: out_block(3), lambda: qkv_block(3), tail[2], tail[3], qkv_sums.pass_on]
    for piece in tail + [lambda: grad_step(4), lambda: grad_step(5)]:
        piece()
    if not push:
        out = pltpu.make_async_copy(dproj, dproj_hbm, lsem.at[14])
        out.start()
    ends = [pltpu.make_async_copy(a, b, osem.at[i]) for i, (a, b) in enumerate(((out_ref, out_hbm), (in_ref, in_hbm)))]
    for end in ends:
        end.start()
    L = 2 * D + 2 * HD
    small[w, :, 0:D] = gains[0:1, :]
    small[w, :, D:2 * D] = gmlp_ref[...]
    small[w, :, 2 * D:2 * D + HD] = gains[1:2, :HD]
    small[w, :, 2 * D + HD:L] = gains[2:3, :HD]

    def to_wide(s):
        return remote(small.at[w], small.at[w], gs1.at[s], gr1.at[s], lax.rem(w + s, W), z)

    def to_narrow(s):
        return remote(small_two.at[z], small_two.at[z], gs2.at[s], gr2.at[s], w, lax.rem(z + s, n))

    for s in range(1, W):
        to_wide(s).start()
    for s in range(1, W):
        to_wide(s).wait_recv()
    total = small[0]
    for s in range(1, W):
        total = total + small[s]
    small_two[z] = total
    for s in range(1, n):
        to_narrow(s).start()
    for s in range(1, n):
        to_narrow(s).wait_recv()
    total = small_two[0]
    for s in range(1, n):
        total = total + small_two[s]
    for ref, lo, hi in ((ga_ref, 0, D), (gm_ref, D, 2 * D), (gq_ref, 2 * D, 2 * D + HD), (gk_ref, 2 * D + HD, L)):
        ref[...] = total[:, lo:hi].reshape(hi - lo)
    for s in range(1, W):
        to_wide(s).wait_send()
    for s in range(1, n):
        to_narrow(s).wait_send()
    sm.drain(HALVES, P_)
    s3.drain()
    for end in ends:
        end.wait()
    if push:
        for part in range(C):
            for index, (a, b) in enumerate(((mixv, sib_mix), (dbv, sib_db), (normv, sib_norm), (dproj, sib_dproj))):
                swap(index, a, b, part).wait_send()
        for sums in (up_sums, out_sums, qkv_sums):
            sums.drain()
        for copy in own_copies:
            copy.wait()
    else:
        out.wait()


def finish_kernel(*refs):
    own_down, recv_down, own_out, recv_out, own_gate, recv_gate, own_up, recv_up, own_qkv, recv_qkv = refs[:10]
    low, high = refs[10:12]
    passed = refs[12:17]
    down, out_g, gate, up, g_q, g_k, g_v, out_ref = refs[17:25]
    out_ref[0], out_ref[1] = low[0], high[0]

    def total(own, parts):
        value = own[...].astype(F32)
        for i in range(parts.shape[0]):
            value = value + parts[i].astype(F32)
        return value

    down[...] = total(own_down, recv_down).T
    out_g[...] = total(own_out, recv_out).T
    gate[...] = total(own_gate, recv_gate)
    up[...] = total(own_up, recv_up)
    qkv = total(own_qkv, recv_qkv)
    first, second = g_q.shape[1], g_q.shape[1] + g_k.shape[1]
    g_q[...], g_k[...], g_v[...] = qkv[:, :first], qkv[:, first:second], qkv[:, second:]
    for a, b in zip(passed, refs[25:]):
        b[...] = a[...]


def local(W, layer_input, document_lengths, attn_gain, w_query, w_key, w_value, query_gain, key_gain, w_out, mlp_gain,
          w_gate, w_up, w_down, output_cotangent):
    n = lax.axis_size("narrow")
    C, _, S, D = layer_input.shape
    R = n * S
    T = C * R
    HD = query_gain.shape[0]
    QC, KC = w_query.shape[1], w_key.shape[1]
    QH = QC // HD
    FC = w_gate.shape[1]
    docs = document_lengths.shape[2]
    P_ = C * HALVES
    grid = 4
    push = (W == 8 and (D // W) % 128 == 0 and FC % (128 * grid) == 0 and QC % (128 * grid) == 0
            and S % (8 * grid) == 0)
    assert C == 2
    width = D // W
    x_own, cot_own = layer_input[:, 0], output_cotangent[:, 0]
    sds = jax.ShapeDtypeStruct
    dma = pltpu.SemaphoreType.DMA
    gsem = lambda: dma((2, n - 1, P_))
    half = np.arange(HD) % (HD // 2)
    freq = jnp.asarray(np.power(np.float32(1000000.0), np.float32(-2.0) * half.astype(np.float32) / np.float32(HD)), F32)
    vm = pl.BlockSpec(memory_space=pltpu.VMEM)
    hbm = pl.BlockSpec(memory_space=pl.ANY)
    smem = pl.BlockSpec(memory_space=pltpu.SMEM)
    VM = pltpu.VMEM

    PC = QC + 2 * KC
    full, wide_rows = sds((C, R, D), BF16), sds((C, R, FC), BF16)
    kept = [sds((C, R, QC + KC), F32), sds((C, R, QH * R), F32), sds((C, R, PC), BF16), sds((C, R, 2 * HD), F32),
            sds((C, R, QC), BF16), full]
    outs = kept + [sds((C, S, D), F32), sds((C, S, D), F32), sds((1, D), F32), sds((1, R, QC), BF16), full, sds((1, R, D), BF16), sds((1, S, D), F32)]
    specs = [hbm] * 8 + [vm] + [hbm] * 4
    line = lambda: [VM((C, R, D), BF16), VM((C, R + S, D), BF16)]
    scratch = (
        [VM((C, S, D), BF16), VM((C, S, D), BF16), VM((C, S, D), F32), VM((C, S, D), F32), VM((1, S, D), F32), VM((1, R, QC), BF16)]
        + [VM((C, R, QC), BF16), VM(w_out.shape, BF16), VM(w_gate.shape, BF16), VM(w_up.shape, BF16), VM(w_down.shape, BF16)]
        + [VM((C, R, D), BF16)] * 3 + [VM((C, R, D), F32)] + line()
        + [VM((C, R, D), BF16), VM((R, FC), F32)] + [VM((C, R, FC), BF16)] * 3 + [VM((S // HALVES, D), F32)]
        + [dma((9,)), gsem(), gsem(), gsem(), gsem(), dma((n, P_)), dma((2, n, P_)), gsem(), gsem(), dma((n, P_)), dma((2, n, P_)),
           gsem(), gsem(), dma((n, P_)), dma((2, n, P_)), dma((12,)), dma((6, C))]
    )
    if push:
        sums, own = sds((2, width, FC), BF16), sds((width, FC), BF16)
        outs += [full, full, wide_rows, wide_rows, wide_rows, sums, sums, sds((3, width, FC), BF16), own, own, own]
        scratch += [VM((3, width, FC), BF16), VM((3, width, FC), BF16), VM((2, width, FC), BF16), VM((width, FC), BF16),
                    VM((width, FC), BF16), VM((width, FC), BF16), VM((4, C, R, width), BF16), VM((C, R, FC), BF16),
                    dma((5, C)), dma((5, C)), dma((6,)), dma((6,)), dma((6,)), dma((6,)), dma((2, 4, C)), dma((3,))]
    else:
        outs += [full, full, wide_rows, wide_rows, wide_rows]
    res = pl.pallas_call(
        functools.partial(middle_kernel, n, C, S, W, HD, docs, push), name="middle", out_shape=outs,
        in_specs=[smem] + [vm] * 5 + [hbm] * 9, out_specs=specs + [hbm] * (len(outs) - len(specs)), scratch_shapes=scratch,
        compiler_params=pltpu.CompilerParams(collective_id=0, has_side_effects=True, vmem_limit_bytes=63 << 20),
    )(document_lengths[:, 0], attn_gain, query_gain, key_gain, freq, mlp_gain, x_own, cot_own, w_query, w_key, w_value, w_out, w_gate, w_up, w_down)
    raws, prob, rots, tabs, mix, normed_full = res[:6]
    res = res[6:]
    middle, d_middle, gmlp, d_mix, db_full, mlp_sums, out_low = res[:7]

    args = [attn_gain, query_gain, key_gain, gmlp, mlp_sums, raws, rots, prob, tabs, d_mix, w_query, w_key, w_value,
            middle, d_middle, x_own, db_full, w_out]
    in_specs = [vm] * 4 + [hbm] * 14
    held = [VM((C, R, D), BF16)] + [VM(v.shape, v.dtype) for v in args[5:9]] + [VM((C, R, QC), BF16)]
    held += [VM(v.shape, v.dtype) for v in args[10:]] + [VM((1, S, D), F32), VM((C, S, D), F32)]
    own_rows = sds((C, S, D), F32)
    outs = [sds((1, S, D), F32), own_rows, sds((D,), F32), sds((D,), F32), sds((HD,), F32), sds((HD,), F32)]
    specs = [hbm] * 2 + [vm] * 4
    L = 2 * D + 2 * HD
    scratch = (
        held + [VM((C, R, PC), BF16), VM((C, R, D), F32)]
        + line() + line()[1:] + [VM((S // HALVES, D), F32), VM((8, D), F32), VM((W, 1, L), F32), VM((n, 1, L), F32)]
        + [dma((19,)), dma((n, P_)), dma((2, n, P_)), dma((n, P_)), dma((2, n, P_)), dma((W,)), dma((W,)), dma((n,)), dma((n,)),
           dma((4,))]
    )
    if push:
        sib_n2, sib_cot, sib_act, sib_dg, sib_du, recv_down, recv_gate, blk_up, own_down, own_gate, own_up = res[7:]
        args += [mix, normed_full, blk_up]
        in_specs += [hbm] * 3
        outs += [sds((2, width, FC), BF16)] + [sds((2, width, QC), BF16), sds((2, width, PC), BF16),
                                                       sds((width, QC), BF16), sds((width, PC), BF16)]
        specs += [hbm] * 5
        scratch += [VM((C, R, QC), BF16), VM((C, R, D), BF16)]
        scratch += [VM((C, R, QC), BF16), VM((C, R, D), BF16), VM((C, R, D), BF16), VM((C, R, PC), BF16)]
        scratch += [dma((4, C)), dma((4, C)), VM((width, QC), BF16), VM((width, PC), BF16)]
        for cols in (FC, QC, PC):
            scratch += [VM((3, width, cols), BF16), VM((width, cols), BF16), dma((6,)), dma((6,))]
    else:
        outs += [sds((C, R, PC), BF16)]
        specs += [hbm]
    last = pl.pallas_call(
        functools.partial(last_kernel, n, C, S, W, HD, push), name="last", out_shape=outs, in_specs=in_specs, out_specs=specs,
        scratch_shapes=scratch,
        compiler_params=pltpu.CompilerParams(collective_id=1, has_side_effects=True, vmem_limit_bytes=60 << 20),
    )(*args)
    out_high, in_own, g_attn, g_mlp, g_query, g_key = last[:6]
    if push:
        recv_up, recv_out, recv_qkv, own_out, own_qkv = last[6:]

        def by_rows(rows, cols, lead=None):
            if lead is None:
                return pl.BlockSpec((rows // grid, cols), lambda i: (i, 0))
            return pl.BlockSpec((lead, rows // grid, cols), lambda i: (0, i, 0))

        def by_cols(rows, cols, lead=None):
            if lead is None:
                return pl.BlockSpec((rows, cols // grid), lambda i: (0, i))
            return pl.BlockSpec((lead, rows, cols // grid), lambda i: (0, 0, i))

        def shard(parts):
            return pl.BlockSpec((parts, S // grid, D), lambda i: (0, i, 0))

        same = [shard(C)] + [pl.BlockSpec(v.shape, lambda i: (0,)) for v in last[2:6]]
        down, out_g, gate, up, g_q, g_k, g_v, out_own, in_own, g_attn, g_mlp, g_query, g_key = pl.pallas_call(
            finish_kernel, name="finish", grid=(grid,),
            out_shape=[sds((FC, width), F32), sds((QC, width), F32), sds((width, FC), F32), sds((width, FC), F32),
                       sds((width, QC), F32), sds((width, KC), F32), sds((width, KC), F32)]
            + [own_rows] + [sds(v.shape, v.dtype) for v in last[1:6]],
            in_specs=[by_cols(width, FC), by_cols(width, FC, 2), by_cols(width, QC), by_cols(width, QC, 2),
                      by_rows(width, FC), by_rows(width, FC, 2), by_rows(width, FC), by_rows(width, FC, 2),
                      by_rows(width, PC), by_rows(width, PC, 2), shard(1), shard(1)] + same,
            out_specs=[by_rows(FC, width), by_rows(QC, width), by_rows(width, FC), by_rows(width, FC), by_rows(width, QC),
                       by_rows(width, KC), by_rows(width, KC), shard(C)] + same,
            compiler_params=pltpu.CompilerParams(vmem_limit_bytes=62 << 20),
        )(own_down, recv_down, own_out, recv_out, own_gate, recv_gate, own_up, recv_up, own_qkv, recv_qkv, out_low, *last[:6])
        projections = (g_q, g_k, g_v)
    else:
        n2, cot, act, dg, du = [v.reshape(T, -1) for v in res[7:]]
        d_proj = last[6].reshape(T, PC)
        db, mixed, normed = db_full.reshape(T, D), mix.reshape(T, QC), normed_full.reshape(T, D)

        def scatter(a, b, dim):
            return lax.psum_scatter(dot(a, b, 0, 0).astype(BF16), "wide", scatter_dimension=dim, tiled=True).astype(F32)

        down, gate, up = scatter(act, cot, 1), scatter(n2, dg, 0), scatter(n2, du, 0)
        out_g, qkv = scatter(mixed, db, 1), scatter(normed, d_proj, 0)
        out_own = jnp.concatenate([out_low, out_high], axis=0)
        projections = (qkv[:, :QC], qkv[:, QC:QC + KC], qkv[:, QC + KC:])
    return (
        out_own[:, None], in_own[:, None], g_attn, *projections,
        g_query, g_key, out_g, g_mlp, gate, up, down,
    )


def solution(mesh):
    rows = P(None, "wide", "narrow", None)
    cols, tall = P(None, "narrow"), P("narrow", None)
    in_specs = (rows, P(None, "wide", None), P(), cols, cols, cols, P(), P(), tall, P(), cols, cols, tall, rows)
    both_ways, turned = P("wide", "narrow"), P("narrow", "wide")
    out_specs = (rows, rows, P(), both_ways, both_ways, both_ways, P(), P(), turned, P(), both_ways, both_ways, turned)
    body = functools.partial(local, mesh.shape["wide"])
    return jax.shard_map(body, mesh=mesh, in_specs=in_specs, out_specs=out_specs, check_vma=False)
```

```python
import functools

import jax
import jax.numpy as jnp
import numpy as np
from jax import lax
from jax.experimental import pallas as pl
from jax.experimental.pallas import tpu as pltpu
from jax.sharding import PartitionSpec as P

MESH = pl.DeviceIdType.MESH
F32 = jnp.float32
BF16 = jnp.bfloat16
norm_eps = 1e-06
masked_score = -1e30
HALVES = 2


def both(*conds):
    out = True
    for cond in conds:
        if isinstance(cond, bool):
            if not cond:
                return False
        else:
            out = cond if out is True else jnp.logical_and(out, cond)
    return out


def when(cond):
    if isinstance(cond, bool):
        return (lambda body: body()) if cond else (lambda body: None)
    return pl.when(cond)


def rows_at(index, rows):
    return pl.ds(pl.multiple_of(index * rows, rows), rows)


def lanes(index, width):
    return pl.ds(pl.multiple_of(index * width, width), width)


def dot(a, b, ca, cb):
    return lax.dot_general(a, b, (((ca,), (cb,)), ((), ())), preferred_element_type=F32)


def remote(src, dst, ssem, rsem, wide, narrow):
    return pltpu.make_async_remote_copy(
        src_ref=src, dst_ref=dst, send_sem=ssem, recv_sem=rsem, device_id=(wide, narrow), device_id_type=MESH
    )


def barrier(n, wide=0):
    w, z = lax.axis_index("wide"), lax.axis_index("narrow")
    bar = pltpu.get_barrier_semaphore()
    for step in range(1, n):
        pl.semaphore_signal(bar, inc=1, device_id=(w, lax.rem(z + step, n)), device_id_type=MESH)
    for step in range(1, wide):
        pl.semaphore_signal(bar, inc=1, device_id=(lax.rem(w + step, wide), z), device_id_type=MESH)
    pl.semaphore_wait(bar, n - 1 + max(wide - 1, 0))


class Line:
    def __init__(self, n, C, S):
        self.n, self.C, self.S = n, C, S
        self.pieces, self.rows = C * HALVES, S // HALVES
        self.w, self.z = lax.axis_index("wide"), lax.axis_index("narrow")

    def at(self, ref, chunk, p):
        start = chunk * self.S + (p % HALVES) * self.rows
        return ref.at[p // HALVES, pl.ds(pl.multiple_of(start, self.rows), self.rows)]


class Gather(Line):
    def __init__(self, n, C, S, full, ssem, rsem):
        super().__init__(n, C, S)
        self.full, self.ssem, self.rsem = full, ssem, rsem

    def copy(self, way, hop, p):
        chunk = self.z - hop if way == 0 else self.z + hop
        where = self.at(self.full, chunk, p)
        z_to = self.z + 1 if way == 0 else self.z - 1
        return remote(where, where, self.ssem.at[way, hop, p], self.rsem.at[way, hop, p], self.w, z_to)

    def arrival(self, way, hop, p):
        chunk = self.z - hop - 1 if way == 0 else self.z + hop + 1
        where = self.at(self.full, chunk, p)
        z_to = self.z + 1 if way == 0 else self.z - 1
        return remote(where, where, self.ssem.at[way, hop, p], self.rsem.at[way, hop, p], self.w, z_to)

    def has(self, way, hop):
        return self.z >= hop if way == 0 else self.z + hop <= self.n - 1

    def can_send(self, way, hop):
        edge = self.z < self.n - 1 if way == 0 else self.z > 0
        return both(self.has(way, hop), edge, hop < self.n - 1)

    def send(self, hop, p, ok=True):
        known = isinstance(hop, int)
        for way in (0, 1):
            if not (known and hop == 0):
                @when(both(ok, hop > 0, self.has(way, hop)))
                def _():
                    self.arrival(way, hop - 1, p).wait_recv()

            if not (known and hop >= self.n - 1):
                @when(both(ok, self.can_send(way, hop)))
                def _():
                    self.copy(way, hop, p).start()

    def drain(self):
        def step(t, carry):
            hop, p = t // self.pieces, t % self.pieces
            for way in (0, 1):
                @when(self.can_send(way, hop))
                def _():
                    self.copy(way, hop, p).wait_send()
            return carry

        lax.fori_loop(0, (self.n - 1) * self.pieces, step, 0)


class Scatter(Line):
    def __init__(self, n, C, S, partial, sbuf, rbuf, ssem, rsem):
        super().__init__(n, C, S)
        self.partial, self.sbuf, self.rbuf, self.ssem, self.rsem = partial, sbuf, rbuf, ssem, rsem

    def copy(self, way, d, p):
        z_to = self.z + 1 - 2 * way
        slot = jnp.where(both(way == 1, d == z_to), self.n, d)
        return remote(
            self.at(self.sbuf, d, p), self.at(self.rbuf, slot, p), self.ssem.at[d, p], self.rsem.at[way, d, p], self.w, z_to
        )

    def slot(self, way, d):
        return jnp.where(both(way == 1, d == self.z), self.n, d)

    def arrived(self, way, d, p):
        where = self.at(self.rbuf, self.slot(way, d), p)
        remote(where, where, self.ssem.at[d, p], self.rsem.at[way, d, p], self.w, self.z).wait_recv()
        return where[...].astype(F32)

    def originate(self, p):
        def step(i, carry):
            way = jnp.where(self.z == 0, 0, 1)
            d = jnp.where(self.z == 0, self.n - 1 - i, i)

            @when(jnp.logical_or(self.z == 0, self.z == self.n - 1))
            def _():
                if self.partial is not self.sbuf:
                    self.at(self.sbuf, d, p)[...] = self.at(self.partial, d, p)[...].astype(BF16)
                self.copy(way, d, p).start()

            return carry

        lax.fori_loop(0, self.n - 1, step, 0)

    def pass_on(self, order, p, ok=True):
        inner = both(ok, self.z > 0, self.z < self.n - 1)

        @when(inner)
        def _():
            def step(i, carry):
                way = jnp.where(self.z < self.n // 2, order, 1 - order)
                d = jnp.where(way == 0, self.n - 1 - i, i)

                @when(jnp.where(way == 0, d > self.z, d < self.z))
                def _():
                    value = self.arrived(way, d, p) + self.at(self.partial, d, p)[...].astype(F32)
                    self.at(self.sbuf, d, p)[...] = value.astype(BF16)
                    self.copy(way, d, p).start()

                return carry

            lax.fori_loop(0, self.n - 1, step, 0)

    def final(self, p, acc):
        acc[...] = self.at(self.partial, self.z, p)[...].astype(F32)
        for way, there in ((0, self.z > 0), (1, self.z < self.n - 1)):
            @when(there)
            def _():
                acc[...] += self.arrived(way, self.z, p)

    def drain(self, lo=0, hi=None):
        hi = self.pieces if hi is None else hi

        def step(t, carry):
            d, p = t // (hi - lo), lo + t % (hi - lo)

            @when(d != self.z)
            def _():
                self.copy(jnp.where(d > self.z, 0, 1), d, p).wait_send()

            return carry

        lax.fori_loop(0, self.n * (hi - lo), step, 0)


def rms_scale(values):
    return lax.rsqrt(jnp.mean(values * values, axis=-1, keepdims=True) + norm_eps)


def rms_back(grad_in, hat, scale_rows):
    return scale_rows * (grad_in - hat * jnp.mean(grad_in * hat, axis=-1, keepdims=True))


def rope(v, cos2, sin2):
    return v * cos2 + pltpu.roll(v, v.shape[-1] // 2, axis=1) * sin2


def chain(k, lo, hi, scat, gath, finish, n):
    def within(p):
        return both(p >= lo, p < hi)

    f = lo + k - 2

    @when(within(f))
    def _():
        finish(f)
        if gath is not None:
            gath.send(0, f)

    scat.pass_on(1, lo + k - 1, within(lo + k - 1))
    scat.pass_on(0, lo + k, within(lo + k))
    if gath is not None:
        for hop in range(n - 1, 0, -1):
            gath.send(hop, f - hop, within(f - hop))


def staggered(k, starts, scat, gath, finish, n):
    ages = [(k - start, p) for p, start in enumerate(starts)]
    for age, p in ages:
        if age == 2:
            finish(p)
            if gath is not None:
                gath.send(0, p)
    for age, p in ages:
        if age == 1:
            scat.pass_on(1, p)
    for age, p in ages:
        if age == 0:
            scat.pass_on(0, p)
    if gath is not None:
        for age, p in ages:
            if 3 <= age <= n + 1:
                gath.send(age - 2, p)


class Square:
    def __init__(self, stage, transit, recv, ssem, rsem):
        self.stage, self.transit, self.recv, self.ssem, self.rsem = stage, transit, recv, ssem, rsem
        w = lax.axis_index("wide")
        self.z = lax.axis_index("narrow")
        core, chip = w % 2, w // 2
        self.beside = 2 * (chip + 1 - 2 * (chip % 2)) + core
        self.below = 2 * (chip + 2 - 4 * (chip // 2)) + core
        self.far = 2 * (3 - chip) + core
        self.owners = (self.far, self.beside, self.below)

    def copy(self, m):
        N = self.transit.shape[1]
        h0, h1 = pl.ds(0, N // 2), pl.ds(N // 2, N // 2)
        block, half, there = ((0, h0, 0), (0, h1, 0), (1, h0, 1), (2, h1, 1), (2, h0, 2), (1, h1, 2))[m]
        to = (self.beside, self.below, self.beside, self.below, self.below, self.beside)[m]
        dst = self.transit.at[:, half] if there == 0 else self.recv.at[there - 1, :, half]
        return remote(self.stage.at[block, :, half], dst, self.ssem.at[m], self.rsem.at[m], to, self.z)

    def put(self, block):
        for m in ((0, 1), (2,), (3,))[block]:
            self.copy(m).start()

    def pass_on(self):
        N = self.transit.shape[1]
        for m, block, half in ((0, 2, pl.ds(0, N // 2)), (1, 1, pl.ds(N // 2, N // 2))):
            self.copy(m).wait_recv()
            value = self.stage[block, :, half].astype(F32) + self.transit[:, half].astype(F32)
            self.stage[block, :, half] = value.astype(BF16)
            self.copy(4 + m).start()

    def drain(self):
        for m in range(6):
            self.copy(m).wait_send()
        for m in range(2, 6):
            self.copy(m).wait_recv()


def row_of(ref):
    return ref[...].astype(F32).reshape(1, ref.shape[0])


def weight_block(A, B, sib_a, sib_b, cols):
    total = None
    for part in range(A.shape[0]):
        for term in (dot(A[part, :, cols], B[part], 0, 0), dot(sib_a(part), sib_b[part], 0, 0)):
            total = term if total is None else total + term
    return total


PLAN = dict(
    branch_starts=(0, 1, 5, 6), back_starts=(0, 1, 5, 6),
    after=dict(
        start=(('input', 0), ('input', 1), ('input', 2), ('input', 3), ('cot0', 0)),
        attend01=(('input', 4),),
        out0=(('input', 5), ('cot0', 1), ('cot0', 2), ('cot1', 0)),
        project1=(('branch', 0),),
        attend10=(('branch', 1), ('branch', 2)),
        attend11=(('branch', 3), ('cot1', 1)),
        out1=(('cot0', 3), ('cot0', 4)),
        act=(('branch', 4), ('branch', 5), ('branch', 6), ('branch', 7)),
        feed00=(('cot1', 2),),
        feed03=(('branch', 8),),
        feed04=(('cot1', 3),),
        feed06=(('branch', 9), ('branch', 10), ('branch', 11), ('cot1', 4)),
        feed10=(('back', 0),),
        feed11=(('back', 1), ('back', 2)),
        feed14=(('back', 3),),
        work1=(('back', 4),),
        work3=(('back', 5), ('back', 6), ('back', 7)),
        work5=(('back', 8), ('mlp', 0)),
        work7=(('back', 9),),
        work10=(('back', 10), ('mlp', 1)),
        work11=(('mlp', 2), ('mlp', 3)),
        work12=(('back', 11),),
        work13=(('mlp', 4),),
    ),
)


def middle_kernel(n, C, S, W, HD, docs, push, *refs):
    (lens_ref, attn_gain_ref, qg_ref, kg_ref, freq_ref, gain_ref, x_hbm, cot_hbm_in, wq_hbm, wk_hbm, wv_hbm,
     wout_hbm, wgate_hbm, wup_hbm, wdown_hbm) = refs[:15]
    (raws_hbm, prob_hbm, rots_hbm, tabs_hbm, mix_hbm, normed_hbm,
     middle_hbm, dmid_hbm, gaing_ref, dmix_hbm, db_hbm, mlp_hbm, out_hbm) = refs[15:28]
    rest = list(refs[28:])
    if push:
        sib_n2, sib_cot, sib_act, sib_dg, sib_du, recv_down, recv_gate, blk_up, own_down, own_gate, own_up = rest[:11]
        rest = rest[11:]
    else:
        n2_hbm, cot_hbm, act_hbm, dg_hbm, du_hbm = rest[:5]
        rest = rest[5:]
    (x_ref, cot_ref, middle_ref, dmid_ref, out_ref, dmix_ref, mixv, wout, wgate, wup, wdown, cotf, n2f, dbf, partial, sbuf, rbuf, sbufm,
     dact, act, dg, du, acc, wsem, g1s, g1r, cs, cr, s1s, s1r, g2s, g2r, s2s, s2r, g3s, g3r, sms, smr, osem, vsem) = rest[:40]
    rest = rest[40:]
    if push:
        (stage_d, stage_g, stage_u, transit_d, transit_g, stage_own, cols_sib, b_sib, sib_ss, sib_rs,
         down_ss, down_rs, gate_ss, gate_rs, lsem, own_sem) = rest
    R = n * S
    D = x_ref.shape[2]
    FC = wgate.shape[1]
    TN = 512
    nt, nd = FC // TN, D // TN
    P_ = C * HALVES
    rows = S // HALVES
    w, z = lax.axis_index("wide"), lax.axis_index("narrow")
    QC, KC = mixv.shape[2], wk_hbm.shape[1]
    QH, KH = QC // HD, KC // HD
    G = QH // KH
    PC = QC + 2 * KC
    table_lanes = C * 2 * HD
    assert table_lanes % R == 0 and table_lanes + C * R <= FC and PC <= FC
    assert D % R == 0 and QC + KC <= D - QH * R
    prob_at = D // R - QH

    def tiles(count, body):
        def step(j, carry):
            body(j)
            return carry

        lax.fori_loop(0, count, step, 0)

    loads = [pltpu.make_async_copy(a, b, wsem.at[i]) for i, (a, b) in enumerate(
        ((x_hbm, x_ref), (cot_hbm_in, cot_ref), (wq_hbm, wgate.at[:, 0:QC]), (wk_hbm, wgate.at[:, QC:QC + KC]),
         (wv_hbm, wgate.at[:, QC + KC:PC]), (wout_hbm, wout), (wdown_hbm, wdown), (wup_hbm, wup), (wgate_hbm, wgate)))]
    for load in loads[:8]:
        load.start()
    gain, again, qgain, kgain, freq = [row_of(v) for v in (gain_ref, attn_gain_ref, qg_ref, kg_ref, freq_ref)]
    barrier(n, W if push else 0)
    loads[0].wait()
    for part in range(C):
        x = x_ref[part].astype(F32)
        dbf[part, rows_at(z, S)] = (x * rms_scale(x) * again).astype(BF16)
    g1 = Gather(n, C, S, dbf, g1s, g1r)
    gc = Gather(n, C, S, cotf, cs, cr)
    g2 = Gather(n, C, S, n2f, g2s, g2r)
    g3 = Gather(n, C, S, dbf, g3s, g3r)
    s1 = Scatter(n, C, S, partial, sbuf, rbuf, s1s, s1r)
    s2 = Scatter(n, C, S, partial, sbuf, rbuf, s2s, s2r)
    sm = Scatter(n, C, S, sbufm, sbufm, rbuf, sms, smr)
    for p in range(2):
        g1.send(0, p)
    loads[1].wait()
    for part in range(C):
        cotf[part, rows_at(z, S)] = cot_ref[part]
    for part in range(C):
        t = lax.broadcasted_iota(jnp.int32, (R, HD), 0)
        row = lax.broadcasted_iota(jnp.int32, (R, R), 0)
        col = lax.broadcasted_iota(jnp.int32, (R, R), 1)
        first = jnp.zeros((R, HD), jnp.int32)
        first_wide = jnp.zeros((R, R), jnp.int32)
        end = jnp.int32(0)
        for d in range(docs):
            end = end + lens_ref[part, d]
            first = jnp.where(t >= end, end, first)
            first_wide = jnp.where(row >= end, end, first_wide)
        angle = (t - first).astype(F32) * freq
        sign = jnp.where(lax.broadcasted_iota(jnp.int32, (R, HD), 1) < HD // 2, -1.0, 1.0)
        dact[:, lanes(2 * part, HD)] = jnp.cos(angle)
        dact[:, lanes(2 * part + 1, HD)] = jnp.sin(angle) * sign
        dact[:, lanes(table_lanes // R + part, R)] = jnp.where(both(col <= row, col >= first_wide), 0.0, masked_score)

    def input_step(k):
        for hop in range(n - 1, 0, -1):
            if 0 <= k + 1 - hop < P_:
                g1.send(hop, k + 1 - hop)
        if k + 2 < P_:
            g1.send(0, k + 2)

    def cot_step(part, k):
        if k == 0:
            for h in range(HALVES):
                gc.send(0, part * HALVES + h)
        for hop in range(n - 1, 0, -1):
            if 0 <= k - hop < HALVES:
                gc.send(hop, part * HALVES + k - hop)

    def mlp_step(k):
        if k == 0:
            for j in range(nd):
                sbufm[0, :, lanes(j, TN)] = dot(act[0], wdown[:, lanes(j, TN)], 1, 0).astype(BF16)
            for h in range(HALVES):
                sm.originate(h)
        else:
            staggered(k - 1, tuple(range(HALVES)), sm, None, mlp_done, n)

    def mlp_done(p):
        sm.final(p, acc)
        part, rr = mid_row(p)
        out_ref[part, rr] = middle_ref[part, rr] + acc[...]

    steps = dict(
        input=input_step, cot0=functools.partial(cot_step, 0), cot1=functools.partial(cot_step, 1), mlp=mlp_step,
        branch=lambda k: staggered(k, PLAN["branch_starts"], s1, g2, after_attention, n),
        back=lambda k: staggered(k, PLAN["back_starts"], s2, g3, after_feed, n))
    assert (n, C, HALVES, KH, nt, nd) == (4, 2, 2, 2, 3, 4)

    def run(place):
        for kind, k in PLAN["after"].get(place, ()):
            steps[kind](k)

    run("start")
    for load in loads[2:5]:
        load.wait()

    def project(part):
        lhs = dbf[part]
        partial[part, :, 0:QC + KC] = dot(lhs, wgate[:, 0:QC + KC], 1, 0)
        act[part, :, QC + KC:PC] = dot(lhs, wgate[:, QC + KC:PC], 1, 0).astype(BF16)

    def attend(part, k):
        cos2, sin2 = dact[:, lanes(2 * part, HD)], dact[:, lanes(2 * part + 1, HD)]

        def turned(index, head_gain):
            raw = partial[part, :, lanes(index, HD)]
            value = rope(raw * rms_scale(raw) * head_gain, cos2, sin2).astype(BF16)
            act[part, :, lanes(index, HD)] = value
            return value

        kr = turned(QH + k, kgain)
        for g in range(G):
            h = k * G + g
            qr = turned(h, qgain)
            s = dot(qr, kr, 1, 1) * HD ** (-0.5) + dact[:, lanes(table_lanes // R + part, R)]
            ex = jnp.exp(s - jnp.max(s, axis=-1, keepdims=True))
            prob = ex / jnp.sum(ex, axis=-1, keepdims=True)
            partial[part, :, lanes(prob_at + h, R)] = prob
            mix = dot(prob.astype(BF16), act[part, :, lanes(QH + KH + k, HD)], 1, 0)
            mixv[part, :, lanes(h, HD)] = mix.astype(BF16)

    def saves(part, lo=0, hi=6):
        return [pltpu.make_async_copy(a, b, vsem.at[i, part]) for i, (a, b) in list(enumerate((
            (partial.at[part, :, 0:QC + KC], raws_hbm.at[part]), (partial.at[part, :, prob_at * R:D], prob_hbm.at[part]),
            (act.at[part, :, 0:PC], rots_hbm.at[part]), (dact.at[:, lanes(part, 2 * HD)], tabs_hbm.at[part]),
            (mixv.at[part], mix_hbm.at[part]), (dbf.at[part], normed_hbm.at[part]))))[lo:hi]]

    def out_project(part):
        if part == 0:
            loads[5].wait()
        for save in saves(part, 0, 2):
            save.wait()

        def out_tile(j):
            partial[part, :, lanes(j, TN)] = dot(mixv[part], wout[:, lanes(j, TN)], 1, 0)

        tiles(nd, out_tile)
        for h in range(HALVES):
            s1.originate(part * HALVES + h)

    def mid_row(p):
        return p // HALVES, rows_at(p % HALVES, rows)

    def after_attention(p):
        s1.final(p, acc)
        part, rr = mid_row(p)
        middle = x_ref[part, rr].astype(F32) + acc[...]
        middle_ref[part, rr] = middle
        g2.at(n2f, z, p)[...] = (middle * rms_scale(middle) * gain).astype(BF16)

    def dact_tile(part, j):
        dact[:, lanes(j, TN)] = dot(cotf[part], wdown[rows_at(j, TN), :], 1, 1)

    project(0)
    run("project0")
    for k in range(KH):
        attend(0, k)
        if k == KH - 1:
            for save in saves(0):
                save.start()
        run("attend0%d" % k)
    out_project(0)
    run("out0")
    project(1)
    loads[8].start()
    run("project1")
    for k in range(KH):
        attend(1, k)
        if k == KH - 1:
            for save in saves(1):
                save.start()
        run("attend1%d" % k)
    out_project(1)
    run("out1")
    loads[6].wait()
    for part in range(C):
        for save in saves(part, 2, 6):
            save.wait()
    tiles(nt, lambda j: dact_tile(0, j))
    run("act")
    loads[7].wait()
    loads[8].wait()
    g1.drain()
    if push:
        core = w % 2
        mate = w + 1 - 2 * core

        def swap(index, src, dst, part):
            return remote(src.at[part], dst.at[part], sib_ss.at[index, part], sib_rs.at[index, part], mate, z)

    def after_feed(p):
        s2.final(p, acc)
        part, rr = mid_row(p)
        dn2 = acc[...]
        middle = middle_ref[part, rr]
        scale = rms_scale(middle)
        hat = middle * scale
        gaing_ref[...] += jnp.sum(dn2 * hat, axis=0, keepdims=True)
        dmid = cot_ref[part, rr].astype(F32) + rms_back(dn2 * gain, hat, scale)
        dmid_ref[part, rr] = dmid
        g3.at(dbf, z, p)[...] = dmid.astype(BF16)

    gaing_ref[...] = jnp.zeros_like(gaing_ref)

    def feed(part):
        def service(e, only=range(nt + nd - 1)):
            for which in range(C):
                for at in only:
                    if "feed%d%d" % (which, at) in PLAN["after"]:
                        @when(both(part == which, e == at))
                        def _():
                            run("feed%d%d" % (which, at))

        def gate_tile(j):
            @when(part > 0)
            def _():
                dact_tile(part, j)

            at = lanes(j, TN)
            gate = dot(n2f[part], wgate[:, at], 1, 0)
            up = dot(n2f[part], wup[:, at], 1, 0)
            sig = jax.nn.sigmoid(gate)
            silu = gate * sig
            d_act = dact[:, at]
            act[part, :, at] = (silu * up).astype(BF16)
            dg[part, :, at] = (d_act * up * sig * (1.0 + gate * (1.0 - sig))).astype(BF16)
            du[part, :, at] = (d_act * silu).astype(BF16)
            service(j)

        tiles(nt, gate_tile)
        if push:
            for index, (a, b) in enumerate(((n2f, sib_n2), (cotf, sib_cot), (act, sib_act), (dg, sib_dg), (du, sib_du))):
                swap(index, a, b, part).start()

        def back_tile(j):
            at = rows_at(j, TN)
            partial[part, :, lanes(j, TN)] = dot(dg[part], wgate[at, :], 1, 1) + dot(du[part], wup[at, :], 1, 1)
            service(nt + j)

        tiles(nd, back_tile)
        @when(part == 0)
        def _():
            s1.drain()

        for h in range(HALVES):
            s2.originate(part * HALVES + h)
        service(nt + nd - 1, (nt + nd - 1,))

    tiles(C, feed)

    def mlp_sums(part):
        for j in range(nd):
            sbufm[part, :, lanes(j, TN)] = dot(act[part], wdown[:, lanes(j, TN)], 1, 0).astype(BF16)

    def mix_back():
        dmix_ref[0] = dot(dbf[0], wout[...], 1, 1).astype(BF16)

    if push:
        width = D // W
        down = Square(stage_d, transit_d, recv_down, down_ss, down_rs)
        gate = Square(stage_g, transit_g, recv_gate, gate_ss, gate_rs)
        owners = down.owners

        def fetch(cols, b):
            copies = []
            if cols is not None:
                for q, owner in enumerate(owners + (w,)):
                    for part in range(C):
                        copies.append(pltpu.make_async_copy(
                            cols.at[part, :, lanes(owner, width)], cols_sib.at[q, part], lsem.at[0, q, part]))
            for part in range(C):
                copies.append(pltpu.make_async_copy(b.at[part], b_sib.at[part], lsem.at[1, 0, part]))
            for copy in copies:
                copy.start()
            for copy in copies:
                copy.wait()

        def block(A, B, q):
            return weight_block(A, B, lambda part: cols_sib[q, part], b_sib, lanes((owners + (w,))[q], width))

        def own_copy(dst, index):
            return pltpu.make_async_copy(stage_own, dst, own_sem.at[index])

        def up_copy(q):
            return pltpu.make_async_copy(stage_u.at[q % 2], blk_up.at[q], osem.at[7 + q])

        def arrive(*pairs):
            for part in range(C):
                for index, dst in pairs:
                    swap(index, dst, dst, part).wait_recv()

        def down_block(q):
            if q == 0:
                arrive((1, sib_cot), (2, sib_act))
                fetch(sib_cot, sib_act)
            if q < 3:
                stage_d[q] = block(cotf, act, q).astype(BF16)
                down.put(q)
            else:
                stage_own[...] = block(cotf, act, q).astype(BF16)
                own_copy(own_down, 0).start()

        def gate_block(q):
            if q == 0:
                arrive((0, sib_n2), (3, sib_dg))
                fetch(sib_n2, sib_dg)
            if q < 3:
                stage_g[q] = block(n2f, dg, q).astype(BF16)
                gate.put(q)
            else:
                own_copy(own_down, 0).wait()
                stage_own[...] = block(n2f, dg, q).astype(BF16)
                own_copy(own_gate, 1).start()

        def up_block(q):
            if q == 0:
                arrive((4, sib_du))
                fetch(None, sib_du)
            if q < 3:
                if q == 2:
                    up_copy(0).wait()
                stage_u[q % 2] = block(n2f, du, q).astype(BF16)
                up_copy(q).start()
            else:
                own_copy(own_gate, 1).wait()
                stage_own[...] = block(n2f, du, q).astype(BF16)
                own_copy(own_up, 2).start()

        work = [[(down_block, q)] for q in range(4)] + [[(gate_block, q)] for q in range(3)] + [
            [(down.pass_on,), (gate_block, 3)], [(up_block, 0)], [(up_block, 1)], [(gate.pass_on,), (up_block, 2)], [(up_block, 3)]]
    else:
        outs = [pltpu.make_async_copy(a, b, osem.at[7 + i]) for i, (a, b) in enumerate(
            ((n2f, n2_hbm), (cotf, cot_hbm), (act, act_hbm), (dg, dg_hbm), (du, du_hbm)))]
        for out in outs:
            out.start()
        work = [[] for _ in range(12)]
    ends = [pltpu.make_async_copy(a, b, osem.at[i]) for i, (a, b) in enumerate(
        ((middle_ref, middle_hbm), (sbufm.at[1], mlp_hbm.at[0]), (dbf.at[0], db_hbm.at[0]), (dbf.at[1], db_hbm.at[1]),
         (dmid_ref, dmid_hbm), (out_ref, out_hbm), (dmix_ref, dmix_hbm)))]
    ends[0].start()

    def second_mlp_sums():
        mlp_sums(1)
        ends[1].start()

    def first_mix_back():
        mix_back()
        ends[2].start()
        ends[6].start()

    work += [[(second_mlp_sums,)], [(first_mix_back,)]]
    for place, pieces in enumerate(work):
        for piece in pieces:
            piece[0](*piece[1:])
        run("work%d" % place)
    for end in ends[3:6]:
        end.start()
    gc.drain()
    g2.drain()
    g3.drain()
    s2.drain()
    sm.drain(0, HALVES)
    for end in ends:
        end.wait()
    if push:
        for part in range(C):
            for index, (a, b) in enumerate(((n2f, sib_n2), (cotf, sib_cot), (act, sib_act), (dg, sib_dg), (du, sib_du))):
                swap(index, a, b, part).wait_send()
        for q in (1, 2):
            up_copy(q).wait()
        own_copy(own_up, 2).wait()
        down.drain()
        gate.drain()
    else:
        for out in outs:
            out.wait()


def last_kernel(n, C, S, W, HD, push, *refs):
    gain_ref, qg_ref, kg_ref, gmlp_ref = refs[:4]
    sources = refs[4:18]
    rest = list(refs[18:])
    if push:
        mix_hbm, normed_hbm, blk_up = rest[:3]
        rest = rest[3:]
    out_hbm, in_hbm, ga_ref, gm_ref, gq_ref, gk_ref = rest[:6]
    rest = rest[6:]
    if push:
        recv_up, recv_out, recv_qkv, own_out_hbm, own_qkv_hbm = rest[:5]
        rest = rest[5:]
    else:
        dproj_hbm = rest[0]
        rest = rest[1:]
    held = rest[:16]
    (sbufm, raws, rots, prob_ref, tabs, dmix_ref, wq, wk, wv, middle_ref, dmid_ref, x_ref, dbv, wout) = held[:14]
    out_ref, in_ref = held[14:16]
    rest = rest[16:]
    (dproj, partial, sbuf, rbuf, rbufm, acc, gains, small, small_two, others, others_two,
     lsem, s3s, s3r, sms, smr, gs1, gr1, gs2, gr2, osem) = rest[:21]
    rest = rest[21:]
    if push:
        (mixv, normv, sib_mix, sib_db, sib_norm, sib_dproj, sib_ss, sib_rs, own_out, own_qkv) = rest[:10]
        squares = rest[10:]
    R, D = n * S, x_ref.shape[2]
    QC, KC = wq.shape[1], wk.shape[1]
    G, KH = QC // KC, KC // HD
    TN = 512
    nd = D // TN
    P_ = C * HALVES
    rows = S // HALVES
    w, z = lax.axis_index("wide"), lax.axis_index("narrow")
    targets = (sbufm.at[1:2],) + tuple(held[1:5]) + (dmix_ref.at[0:1],) + tuple(held[6:14])
    loads = [pltpu.make_async_copy(a, b, lsem.at[i]) for i, (a, b) in enumerate(zip(sources, targets))]
    loads[0].start()
    if push:
        stage_up = squares[0]
        blocks = [pltpu.make_async_copy(blk_up.at[q], stage_up.at[q], lsem.at[16 + q]) for q in range(3)]
        for q in range(3):
            blocks[q].start()
    for load in loads[1:6]:
        load.start()
    if push:
        extra = [pltpu.make_async_copy(a, b, lsem.at[14 + i]) for i, (a, b) in enumerate(
            ((mix_hbm, mixv), (normed_hbm, normv)))]
        for load in extra:
            load.start()
    for load in loads[6:]:
        load.start()
    barrier(n, W)
    sm = Scatter(n, C, S, sbufm, sbufm, rbufm, sms, smr)
    s3 = Scatter(n, C, S, partial, sbuf, rbuf, s3s, s3r)
    if push:
        core = w % 2
        mate = w + 1 - 2 * core
        width = D // W
        up_sums, out_sums, qkv_sums = [
            Square(squares[i], squares[i + 1], recv, squares[i + 2], squares[i + 3])
            for i, recv in ((0, recv_up), (4, recv_out), (8, recv_qkv))]
        stage_out, stage_qkv = squares[4], squares[8]

        def swap(index, src, dst, part):
            return remote(src.at[part], dst.at[part], sib_ss.at[index, part], sib_rs.at[index, part], mate, z)

    loads[0].wait()
    for p in range(HALVES, P_):
        sm.originate(p)
    if push:
        for q in range(3):
            blocks[q].wait()
            up_sums.put(q)

    def rest_in():
        for load in loads[6:]:
            load.wait()
        if push:
            for load in extra:
                load.wait()
            for part in range(C):
                for index, (a, b) in enumerate(((mixv, sib_mix), (dbv, sib_db), (normv, sib_norm))):
                    swap(index, a, b, part).start()

    def piece_row(p):
        return p // HALVES, rows_at(p % HALVES, rows)

    def mlp_done(p):
        sm.final(p, acc)
        part, rr = piece_row(p)
        out_ref[0, rr] = middle_ref[part, rr] + acc[...]

    gain, qgain, kgain = [row_of(v) for v in (gain_ref, qg_ref, kg_ref)]

    def grad_done(p):
        s3.final(p, acc)
        part, rr = piece_row(p)
        dn = acc[...]
        x = x_ref[part, rr].astype(F32)
        scale = rms_scale(x)
        hat = x * scale
        gains[0:1, :] += jnp.sum(dn * hat, axis=0, keepdims=True)
        in_ref[part, rr] = dmid_ref[part, rr] + rms_back(dn * gain, hat, scale)

    gains[...] = jnp.zeros_like(gains)
    scale = HD ** (-0.5)
    for load in loads[1:6]:
        load.wait()

    def unit(part, k):
        cos2, sin2 = tabs[part, :, 0:HD], tabs[part, :, HD:2 * HD]
        kr, vr = rots[part, :, lanes(QC // HD + k, HD)], rots[part, :, lanes(QC // HD + KH + k, HD)]

        def unturned(grad, raw, head_gain, at):
            d_n = grad * cos2 - pltpu.roll(grad, HD // 2, axis=1) * sin2
            r = rms_scale(raw)
            hat = raw * r
            gains[at:at + 1, :HD] += jnp.sum(d_n * hat, axis=0, keepdims=True)
            return rms_back(d_n * head_gain, hat, r).astype(BF16)

        dk, dv = None, None
        for g in range(G):
            h = k * G + g
            pr = prob_ref[part, :, lanes(h, R)]
            dm = dmix_ref[part, :, lanes(h, HD)]
            dp = dot(dm, vr, 1, 1)
            one = dot(pr.astype(BF16), dm, 0, 0)
            dv = one if dv is None else dv + one
            ds = (pr * (dp - jnp.sum(pr * dp, axis=-1, keepdims=True))).astype(BF16)
            one = dot(ds, rots[part, :, lanes(h, HD)], 0, 0)
            dk = one if dk is None else dk + one
            dq = dot(ds, kr, 1, 0) * scale
            dproj[part, :, lanes(h, HD)] = unturned(dq, raws[part, :, lanes(h, HD)], qgain, 1)
        dproj[part, :, lanes(QC // HD + k, HD)] = unturned(dk * scale, raws[part, :, lanes(QC // HD + k, HD)], kgain, 2)
        dproj[part, :, lanes(QC // HD + KH + k, HD)] = dv.astype(BF16)

    if push:
        def block(A, B, sib_a, sib_b, owner):
            cols = lanes(owner, width)
            return weight_block(A, B, lambda part: sib_a[part, :, cols], sib_b, cols)

        own_copies = [pltpu.make_async_copy(a, b, osem.at[2 + i]) for i, (a, b) in enumerate(
            ((own_out, own_out_hbm), (own_qkv, own_qkv_hbm)))]

        def arrive(*pairs):
            for part in range(C):
                for index, dst in pairs:
                    swap(index, dst, dst, part).wait_recv()

        def out_block(q):
            if q == 0:
                arrive((0, sib_mix), (1, sib_db))
            if q < 3:
                stage_out[q] = block(dbv, mixv, sib_db, sib_mix, out_sums.owners[q]).astype(BF16)
                out_sums.put(q)
            else:
                own_out[...] = block(dbv, mixv, sib_db, sib_mix, w).astype(BF16)
                own_copies[0].start()

        def qkv_block(q):
            if q == 0:
                arrive((2, sib_norm), (3, sib_dproj))
            if q < 3:
                stage_qkv[q] = block(normv, dproj, sib_norm, sib_dproj, qkv_sums.owners[q]).astype(BF16)
                qkv_sums.put(q)
            else:
                own_qkv[...] = block(normv, dproj, sib_norm, sib_dproj, w).astype(BF16)
                own_copies[1].start()

    def to_wide(ref, index, s):
        return remote(ref.at[w], ref.at[w], gs1.at[index, s], gr1.at[index, s], lax.rem(w + s, W), z)

    def to_narrow(ref, index, s):
        return remote(ref.at[z], ref.at[z], gs2.at[index, s], gr2.at[index, s], w, lax.rem(z + s, n))

    def send_wide(ref, index):
        for s in range(1, W):
            to_wide(ref, index, s).start()

    def send_narrow(ref, two, index):
        for s in range(1, W):
            to_wide(ref, index, s).wait_recv()
        total = ref[0]
        for s in range(1, W):
            total = total + ref[s]
        two[z] = total
        for s in range(1, n):
            to_narrow(two, index, s).start()

    def summed(two, index):
        for s in range(1, n):
            to_narrow(two, index, s).wait_recv()
        total = two[0]
        for s in range(1, n):
            total = total + two[s]
        return total

    def exchange(ref, two, index, value):
        ref[w] = value
        send_wide(ref, index)
        send_narrow(ref, two, index)
        return summed(two, index)

    def early_gains(stage):
        if stage == 0:
            others[w, :, 0:D] = gmlp_ref[...]
            others[w, :, D:D + HD] = gains[1:2, :HD]
            others[w, :, D + HD:D + 2 * HD] = gains[2:3, :HD]
            send_wide(others, 1)
            return None
        return summed(others_two, 1)

    def grad_step(k):
        staggered(k, tuple(range(P_)), s3, None, grad_done, n)

    def mlp_step(k):
        chain(k, HALVES, P_, sm, None, mlp_done, n)

    assert (n, C, HALVES, KH) == (4, 2, 2, 2)

    def backward(part):
        @when(part == 1)
        def _():
            dmix_ref[1] = dot(dbv[1], wout[...], 1, 1).astype(BF16)

        def heads(k, carry):
            unit(part, k)

            @when(both(part == 0, k == 0))
            def _():
                rest_in()

            @when(both(part == 0, k == KH - 1))
            def _():
                mlp_step(0)

            if push:
                @when(both(part == 1, k == 0))
                def _():
                    up_sums.pass_on()

            return carry

        lax.fori_loop(0, KH, heads, 0)
        if push:
            swap(3, dproj, sib_dproj, part).start()

        def back_tile(j, carry):
            at = rows_at(j, TN)
            partial[part, :, lanes(j, TN)] = (
                dot(dproj[part, :, 0:QC], wq[at, :], 1, 1) + dot(dproj[part, :, QC:QC + KC], wk[at, :], 1, 1)
                + dot(dproj[part, :, QC + KC:QC + 2 * KC], wv[at, :], 1, 1))
            return carry

        lax.fori_loop(0, nd, back_tile, 0)
        for h in range(HALVES):
            s3.originate(part * HALVES + h)

        @when(part == 0)
        def _():
            if push:
                for q in range(3):
                    out_block(q)
            mlp_step(1)
            mlp_step(2)

        @when(part == 1)
        def _():
            grad_step(0)

    def both_parts(part, carry):
        backward(part)
        return carry

    lax.fori_loop(0, C, both_parts, 0)
    tail = [lambda: mlp_step(3), lambda: grad_step(1), lambda: grad_step(2), lambda: grad_step(3)]
    if push:
        tail = [lambda: qkv_block(0), lambda: qkv_block(1), tail[0], lambda: qkv_block(2), tail[1], out_sums.pass_on,
                lambda: out_block(3), lambda: qkv_block(3), tail[2], tail[3], qkv_sums.pass_on]
    early_gains(0)
    for piece in tail + [lambda: send_narrow(others, others_two, 1), lambda: grad_step(4), lambda: grad_step(5)]:
        piece()
    if not push:
        out = pltpu.make_async_copy(dproj, dproj_hbm, lsem.at[14])
        out.start()
    ends = [pltpu.make_async_copy(a, b, osem.at[i]) for i, (a, b) in enumerate(((out_ref, out_hbm), (in_ref, in_hbm)))]
    for end in ends:
        end.start()
    finish_others = early_gains(1)
    attn = exchange(small, small_two, 0, gains[0:1, :])
    for ref, lo, hi in ((gm_ref, 0, D), (gq_ref, D, D + HD), (gk_ref, D + HD, D + 2 * HD)):
        ref[...] = finish_others[:, lo:hi].reshape(hi - lo)
    ga_ref[...] = attn.reshape(D)
    for index, (first, second) in enumerate(((small, small_two), (others, others_two))):
        for s in range(1, W):
            to_wide(first, index, s).wait_send()
        for s in range(1, n):
            to_narrow(second, index, s).wait_send()
    sm.drain(HALVES, P_)
    s3.drain()
    for end in ends:
        end.wait()
    if push:
        for part in range(C):
            for index, (a, b) in enumerate(((mixv, sib_mix), (dbv, sib_db), (normv, sib_norm), (dproj, sib_dproj))):
                swap(index, a, b, part).wait_send()
        for sums in (up_sums, out_sums, qkv_sums):
            sums.drain()
        for copy in own_copies:
            copy.wait()
    else:
        out.wait()


def finish_kernel(*refs):
    own_down, recv_down, own_out, recv_out, own_gate, recv_gate, own_up, recv_up, own_qkv, recv_qkv = refs[:10]
    low, high = refs[10:12]
    passed = refs[12:17]
    down, out_g, gate, up, g_q, g_k, g_v, out_ref = refs[17:25]
    out_ref[0], out_ref[1] = low[0], high[0]

    def total(own, parts):
        value = own[...].astype(F32)
        for i in range(parts.shape[0]):
            value = value + parts[i].astype(F32)
        return value

    down[...] = total(own_down, recv_down).T
    out_g[...] = total(own_out, recv_out).T
    gate[...] = total(own_gate, recv_gate)
    up[...] = total(own_up, recv_up)
    qkv = total(own_qkv, recv_qkv)
    first, second = g_q.shape[1], g_q.shape[1] + g_k.shape[1]
    g_q[...], g_k[...], g_v[...] = qkv[:, :first], qkv[:, first:second], qkv[:, second:]
    for a, b in zip(passed, refs[25:]):
        b[...] = a[...]


def local(W, layer_input, document_lengths, attn_gain, w_query, w_key, w_value, query_gain, key_gain, w_out, mlp_gain,
          w_gate, w_up, w_down, output_cotangent):
    n = lax.axis_size("narrow")
    C, _, S, D = layer_input.shape
    R = n * S
    T = C * R
    HD = query_gain.shape[0]
    QC, KC = w_query.shape[1], w_key.shape[1]
    QH = QC // HD
    FC = w_gate.shape[1]
    docs = document_lengths.shape[2]
    P_ = C * HALVES
    grid = 2
    push = (W == 8 and (D // W) % 128 == 0 and FC % (128 * grid) == 0 and QC % (128 * grid) == 0
            and S % (8 * grid) == 0)
    assert C == 2
    width = D // W
    x_own, cot_own = layer_input[:, 0], output_cotangent[:, 0]
    sds = jax.ShapeDtypeStruct
    dma = pltpu.SemaphoreType.DMA
    gsem = lambda: dma((2, n - 1, P_))
    half = np.arange(HD) % (HD // 2)
    freq = jnp.asarray(np.power(np.float32(1000000.0), np.float32(-2.0) * half.astype(np.float32) / np.float32(HD)), F32)
    vm = pl.BlockSpec(memory_space=pltpu.VMEM)
    hbm = pl.BlockSpec(memory_space=pl.ANY)
    smem = pl.BlockSpec(memory_space=pltpu.SMEM)
    VM = pltpu.VMEM

    PC = QC + 2 * KC
    full, wide_rows = sds((C, R, D), BF16), sds((C, R, FC), BF16)
    kept = [sds((C, R, QC + KC), F32), sds((C, R, QH * R), F32), sds((C, R, PC), BF16), sds((C, R, 2 * HD), F32),
            sds((C, R, QC), BF16), full]
    outs = kept + [sds((C, S, D), F32), sds((C, S, D), F32), sds((1, D), F32), sds((1, R, QC), BF16), full, sds((1, R, D), BF16), sds((1, S, D), F32)]
    specs = [hbm] * 8 + [vm] + [hbm] * 4
    line = lambda: [VM((C, R, D), BF16), VM((C, R + S, D), BF16)]
    scratch = (
        [VM((C, S, D), BF16), VM((C, S, D), BF16), VM((C, S, D), F32), VM((C, S, D), F32), VM((1, S, D), F32), VM((1, R, QC), BF16)]
        + [VM((C, R, QC), BF16), VM(w_out.shape, BF16), VM(w_gate.shape, BF16), VM(w_up.shape, BF16), VM(w_down.shape, BF16)]
        + [VM((C, R, D), BF16)] * 3 + [VM((C, R, D), F32)] + line()
        + [VM((C, R, D), BF16), VM((R, FC), F32)] + [VM((C, R, FC), BF16)] * 3 + [VM((S // HALVES, D), F32)]
        + [dma((9,)), gsem(), gsem(), gsem(), gsem(), dma((n, P_)), dma((2, n, P_)), gsem(), gsem(), dma((n, P_)), dma((2, n, P_)),
           gsem(), gsem(), dma((n, P_)), dma((2, n, P_)), dma((12,)), dma((6, C))]
    )
    if push:
        sums, own = sds((2, width, FC), BF16), sds((width, FC), BF16)
        outs += [full, full, wide_rows, wide_rows, wide_rows, sums, sums, sds((3, width, FC), BF16), own, own, own]
        scratch += [VM((3, width, FC), BF16), VM((3, width, FC), BF16), VM((2, width, FC), BF16), VM((width, FC), BF16),
                    VM((width, FC), BF16), VM((width, FC), BF16), VM((4, C, R, width), BF16), VM((C, R, FC), BF16),
                    dma((5, C)), dma((5, C)), dma((6,)), dma((6,)), dma((6,)), dma((6,)), dma((2, 4, C)), dma((3,))]
    else:
        outs += [full, full, wide_rows, wide_rows, wide_rows]
    res = pl.pallas_call(
        functools.partial(middle_kernel, n, C, S, W, HD, docs, push), name="middle", out_shape=outs,
        in_specs=[smem] + [vm] * 5 + [hbm] * 9, out_specs=specs + [hbm] * (len(outs) - len(specs)), scratch_shapes=scratch,
        compiler_params=pltpu.CompilerParams(collective_id=0, has_side_effects=True, vmem_limit_bytes=63 << 20),
    )(document_lengths[:, 0], attn_gain, query_gain, key_gain, freq, mlp_gain, x_own, cot_own, w_query, w_key, w_value, w_out, w_gate, w_up, w_down)
    raws, prob, rots, tabs, mix, normed_full = res[:6]
    res = res[6:]
    middle, d_middle, gmlp, d_mix, db_full, mlp_sums, out_low = res[:7]

    args = [attn_gain, query_gain, key_gain, gmlp, mlp_sums, raws, rots, prob, tabs, d_mix, w_query, w_key, w_value,
            middle, d_middle, x_own, db_full, w_out]
    in_specs = [vm] * 4 + [hbm] * 14
    held = [VM((C, R, D), BF16)] + [VM(v.shape, v.dtype) for v in args[5:9]] + [VM((C, R, QC), BF16)]
    held += [VM(v.shape, v.dtype) for v in args[10:]] + [VM((1, S, D), F32), VM((C, S, D), F32)]
    own_rows = sds((C, S, D), F32)
    outs = [sds((1, S, D), F32), own_rows, sds((D,), F32), sds((D,), F32), sds((HD,), F32), sds((HD,), F32)]
    specs = [hbm] * 2 + [vm] * 4
    L = D + 2 * HD
    scratch = (
        held + [VM((C, R, PC), BF16), VM((C, R, D), F32)]
        + line() + line()[1:] + [VM((S // HALVES, D), F32), VM((8, D), F32), VM((W, 1, D), F32), VM((n, 1, D), F32), VM((W, 1, L), F32), VM((n, 1, L), F32)]
        + [dma((19,)), dma((n, P_)), dma((2, n, P_)), dma((n, P_)), dma((2, n, P_)), dma((2, W)), dma((2, W)), dma((2, n)), dma((2, n)),
           dma((4,))]
    )
    if push:
        sib_n2, sib_cot, sib_act, sib_dg, sib_du, recv_down, recv_gate, blk_up, own_down, own_gate, own_up = res[7:]
        args += [mix, normed_full, blk_up]
        in_specs += [hbm] * 3
        outs += [sds((2, width, FC), BF16)] + [sds((2, width, QC), BF16), sds((2, width, PC), BF16),
                                                       sds((width, QC), BF16), sds((width, PC), BF16)]
        specs += [hbm] * 5
        scratch += [VM((C, R, QC), BF16), VM((C, R, D), BF16)]
        scratch += [VM((C, R, QC), BF16), VM((C, R, D), BF16), VM((C, R, D), BF16), VM((C, R, PC), BF16)]
        scratch += [dma((4, C)), dma((4, C)), VM((width, QC), BF16), VM((width, PC), BF16)]
        for cols in (FC, QC, PC):
            scratch += [VM((3, width, cols), BF16), VM((width, cols), BF16), dma((6,)), dma((6,))]
    else:
        outs += [sds((C, R, PC), BF16)]
        specs += [hbm]
    last = pl.pallas_call(
        functools.partial(last_kernel, n, C, S, W, HD, push), name="last", out_shape=outs, in_specs=in_specs, out_specs=specs,
        scratch_shapes=scratch,
        compiler_params=pltpu.CompilerParams(collective_id=1, has_side_effects=True, vmem_limit_bytes=60 << 20),
    )(*args)
    out_high, in_own, g_attn, g_mlp, g_query, g_key = last[:6]
    if push:
        recv_up, recv_out, recv_qkv, own_out, own_qkv = last[6:]

        def by_rows(rows, cols, lead=None):
            if lead is None:
                return pl.BlockSpec((rows // grid, cols), lambda i: (i, 0))
            return pl.BlockSpec((lead, rows // grid, cols), lambda i: (0, i, 0))

        def by_cols(rows, cols, lead=None):
            if lead is None:
                return pl.BlockSpec((rows, cols // grid), lambda i: (0, i))
            return pl.BlockSpec((lead, rows, cols // grid), lambda i: (0, 0, i))

        def shard(parts):
            return pl.BlockSpec((parts, S // grid, D), lambda i: (0, i, 0))

        same = [shard(C)] + [pl.BlockSpec(v.shape, lambda i: (0,)) for v in last[2:6]]
        down, out_g, gate, up, g_q, g_k, g_v, out_own, in_own, g_attn, g_mlp, g_query, g_key = pl.pallas_call(
            finish_kernel, name="finish", grid=(grid,),
            out_shape=[sds((FC, width), F32), sds((QC, width), F32), sds((width, FC), F32), sds((width, FC), F32),
                       sds((width, QC), F32), sds((width, KC), F32), sds((width, KC), F32)]
            + [own_rows] + [sds(v.shape, v.dtype) for v in last[1:6]],
            in_specs=[by_cols(width, FC), by_cols(width, FC, 2), by_cols(width, QC), by_cols(width, QC, 2),
                      by_rows(width, FC), by_rows(width, FC, 2), by_rows(width, FC), by_rows(width, FC, 2),
                      by_rows(width, PC), by_rows(width, PC, 2), shard(1), shard(1)] + same,
            out_specs=[by_rows(FC, width), by_rows(QC, width), by_rows(width, FC), by_rows(width, FC), by_rows(width, QC),
                       by_rows(width, KC), by_rows(width, KC), shard(C)] + same,
            compiler_params=pltpu.CompilerParams(vmem_limit_bytes=62 << 20),
        )(own_down, recv_down, own_out, recv_out, own_gate, recv_gate, own_up, recv_up, own_qkv, recv_qkv, out_low, *last[:6])
        projections = (g_q, g_k, g_v)
    else:
        n2, cot, act, dg, du = [v.reshape(T, -1) for v in res[7:]]
        d_proj = last[6].reshape(T, PC)
        db, mixed, normed = db_full.reshape(T, D), mix.reshape(T, QC), normed_full.reshape(T, D)

        def scatter(a, b, dim):
            return lax.psum_scatter(dot(a, b, 0, 0).astype(BF16), "wide", scatter_dimension=dim, tiled=True).astype(F32)

        down, gate, up = scatter(act, cot, 1), scatter(n2, dg, 0), scatter(n2, du, 0)
        out_g, qkv = scatter(mixed, db, 1), scatter(normed, d_proj, 0)
        out_own = jnp.concatenate([out_low, out_high], axis=0)
        projections = (qkv[:, :QC], qkv[:, QC:QC + KC], qkv[:, QC + KC:])
    return (
        out_own[:, None], in_own[:, None], g_attn, *projections,
        g_query, g_key, out_g, g_mlp, gate, up, down,
    )


def solution(mesh):
    rows = P(None, "wide", "narrow", None)
    cols, tall = P(None, "narrow"), P("narrow", None)
    in_specs = (rows, P(None, "wide", None), P(), cols, cols, cols, P(), P(), tall, P(), cols, cols, tall, rows)
    both_ways, turned = P("wide", "narrow"), P("narrow", "wide")
    out_specs = (rows, rows, P(), both_ways, both_ways, both_ways, P(), P(), turned, P(), both_ways, both_ways, turned)
    body = functools.partial(local, mesh.shape["wide"])
    return jax.shard_map(body, mesh=mesh, in_specs=in_specs, out_specs=out_specs, check_vma=False)
```
